32 devices in a mesh: dp: 8 (over y, x, core), tp: 4 (over z).
Axes of the slice: x: 2, y: 2, z: 4, core: 2. Of those that a mesh axis runs over, the one named last changes fastest.
Arguments:
- inputs: bfloat16 [26624, 768], P(('dp', 'tp')), may hold values from -6 to 6
- segment_ids: int32 [32, 832], P('dp'), may hold values from -1 to 4, as said below
- mask_flags: int32 [32, 832], P(('dp', 'tp')), may hold values 0 or 1
- mask_token: bfloat16 [768], replicated, may hold values from -6 to 6
- norm_gain: bfloat16 [768], replicated, may hold values from 0.5 to 1.5
- norm_shift: bfloat16 [768], replicated, may hold values from -3 to 3
- heads_weight: bfloat16 [768, 12, 192], P(None, 'tp'), may hold values from -0.21875 to 0.21875
- heads_bias: bfloat16 [12, 128], P('tp'), may hold values from -1.1953125 to 1.1953125
- proj_weight: bfloat16 [768, 768], P('tp'), may hold values from -1.75 to 1.75
- proj_bias: bfloat16 [768], replicated, may hold values from -2 to 2
- attn_scale: bfloat16 [768], replicated, may hold values from 0.5 to 1.5
- mlp_gain: bfloat16 [768], replicated, may hold values from 0.5 to 1.5
- mlp_shift: bfloat16 [768], replicated, may hold values from -3 to 3
- up_weight: bfloat16 [768, 3072], P(None, 'tp'), may hold values from -0.21875 to 0.21875
- up_bias: bfloat16 [3072], P('tp'), may hold values from -2 to 2
- down_weight: bfloat16 [3072, 768], P('tp'), may hold values from -0.109375 to 0.109375
- down_bias: bfloat16 [768], replicated, may hold values from -2 to 2
- mlp_scale: bfloat16 [768], replicated, may hold values from 0.5 to 1.5
- grad_out: bfloat16 [26624, 768], P(('dp', 'tp')), may hold values from -6 to 6
Outputs:
- output: bfloat16 [26624, 768], P(('dp', 'tp'))
- grad_inputs: float32 [26624, 768], P(('dp', 'tp'))
- grad_token: float32 [768], replicated
- grad_norm_gain: float32 [768], replicated
- grad_norm_shift: float32 [768], replicated
- grad_heads_weight: float32 [768, 12, 192], P(None, 'tp')
- grad_heads_bias: float32 [12, 128], P('tp')
- grad_proj_weight: float32 [768, 768], P('tp')
- grad_proj_bias: float32 [768], replicated
- grad_attn_scale: float32 [768], replicated
- grad_mlp_gain: float32 [768], replicated
- grad_mlp_shift: float32 [768], replicated
- grad_up_weight: float32 [768, 3072], P(None, 'tp')
- grad_up_bias: float32 [3072], P('tp')
- grad_down_weight: float32 [3072, 768], P('tp')
- grad_down_bias: float32 [768], replicated
- grad_mlp_scale: float32 [768], replicated
The draws below stay inside these ranges and needn't reach their ends.
Inputs may be any that keep to these rules, and one draw needn't show every extreme that they name: `segment_ids`: every packed row holds five images numbered 0 to 4 in order from its first slot, then 1 to 32 padding slots marked -1 at its end; each of the first four images has h * w + 1 slots with h and w from 11 to 14, the fifth fills the rest.
All inputs are finite; a program needn't handle non-finite values. No bound on the sum of `mask_flags` on one device may be relied on, other than what follows from the above.
Results may differ from the reference program's by a relative error of at most 0.02.
Values may be sent and summed in bfloat16 or wider, within the bound.
A program may use at most 192 MiB of HBM per device.

```python
import jax
import jax.numpy as jnp
from jax import lax

D = 768
HEADS = 12
HEAD_DIM = 64
FF = 3072
SIDE_MIN = 11
SIDE_MAX = 14
SLOTS = 832
ROWS = 32
TOKENS = 26624
N_TP = 4


def draw_segment_ids(key, part):
    first, second, third = jax.random.split(key, 3)
    tall = jax.random.randint(first, (ROWS, 4), SIDE_MIN, SIDE_MAX + 1)
    broad = jax.random.randint(second, (ROWS, 4), SIDE_MIN, SIDE_MAX + 1)
    ends = jnp.cumsum(tall * broad + 1, axis=1)
    padding = jax.random.randint(third, (ROWS, 1), 1, 33)
    places = jnp.arange(SLOTS, dtype=jnp.int32)[None, :]
    image = jnp.sum((places[:, None, :] >= ends[:, :, None]).astype(jnp.int32), axis=1)
    return jnp.where(places >= SLOTS - padding, -1, image).astype(jnp.int32)


def set_ends(drawn, stream_key, smallest, high):
    spot = [jax.random.randint(jax.random.fold_in(stream_key, axis), (), 0, length) for axis, length in enumerate(drawn.shape)]
    longest = drawn.shape.index(max(drawn.shape))
    neighbour = spot[:longest] + [(spot[longest] + 1) % drawn.shape[longest]] + spot[longest + 1:]
    return drawn.at[tuple(spot)].set(smallest).at[tuple(neighbour)].set(high)


def level_of(key, extent, cuts, smallest, largest):
    def one(position, parts):
        steps = jax.random.uniform(jax.random.fold_in(jax.random.fold_in(key, 6), position), (parts,), jnp.float32, smallest / len(cuts), largest / len(cuts))
        return jnp.repeat(jnp.exp(steps), extent[position] // parts).reshape((-1,) + (1,) * (len(extent) - position - 1))

    factor_of = one(*cuts[0])
    for cut in cuts[1:]:
        factor_of = factor_of * one(*cut)
    return factor_of


def noise(stream_key, extent, scale, bound, shards=(), kind=jnp.bfloat16):
    level = level_of(stream_key, extent, shards, -0.22, 0.18) if shards else 1.0
    array = jax.random.normal(stream_key, extent, jnp.float32) * scale * level
    return jnp.minimum(jnp.maximum(array, -bound), bound).astype(kind)


def setup_inputs(seed: int = 0) -> dict:
    key_list = jax.random.split(jax.random.key(seed), 20)
    return {
        "inputs": noise(key_list[0], (TOKENS, D), 1.0, 6.0, ((0, 32),)),
        "segment_ids": draw_segment_ids(jax.random.fold_in(key_list[19], 71), 0),
        "mask_flags": set_ends((jax.random.randint(key_list[2], (ROWS, SLOTS), 0, 5) < 3).astype(jnp.int32), jax.random.fold_in(key_list[2], 1), 0, 1),
        "mask_token": noise(key_list[3], (D,), 1.0, 6.0),
        "norm_gain": jnp.clip(1.0 + 0.1 * jax.random.normal(key_list[4], (D,), jnp.float32), 0.5, 1.5).astype(jnp.bfloat16),
        "norm_shift": noise(key_list[5], (D,), 0.5, 3.0),
        "heads_weight": noise(key_list[6], (D, HEADS, 3 * HEAD_DIM), D ** -0.5, 0.21875, ((1, 4),)),
        "heads_bias": noise(key_list[7], (HEADS, 2 * HEAD_DIM), 0.2, 1.1953125, ((0, 4),)),
        "proj_weight": noise(key_list[8], (D, D), (D // 64) ** -0.5, 1.75, ((0, 4),)),
        "proj_bias": noise(key_list[9], (D,), 0.3, 2.0),
        "attn_scale": jnp.clip(1.0 + 0.1 * jax.random.normal(key_list[10], (D,), jnp.float32), 0.5, 1.5).astype(jnp.bfloat16),
        "mlp_gain": jnp.clip(1.0 + 0.1 * jax.random.normal(key_list[11], (D,), jnp.float32), 0.5, 1.5).astype(jnp.bfloat16),
        "mlp_shift": noise(key_list[12], (D,), 0.5, 3.0),
        "up_weight": noise(key_list[13], (D, FF), D ** -0.5, 0.21875, ((1, 4),)),
        "up_bias": noise(key_list[14], (FF,), 0.3, 2.0, ((0, 4),)),
        "down_weight": noise(key_list[15], (FF, D), FF ** -0.5, 0.109375, ((0, 4),)),
        "down_bias": noise(key_list[16], (D,), 0.3, 2.0),
        "mlp_scale": jnp.clip(1.0 + 0.1 * jax.random.normal(key_list[17], (D,), jnp.float32), 0.5, 1.5).astype(jnp.bfloat16),
        "grad_out": noise(key_list[18], (TOKENS, D), 1.0, 6.0, ((0, 32),)),
    }


@jax.custom_vjp
def low(v):
    return lax.optimization_barrier(v.astype(jnp.bfloat16)).astype(jnp.float32)

@jax.custom_vjp
def low_back(v):
    return v

def low_keep(v):
    return (low(v), None)

def low_pass(kept, grad):
    return (grad,)

def back_keep(v):
    return (v, None)

def back_low(kept, grad):
    return (low(grad),)
low.defvjp(low_keep, low_pass)
low_back.defvjp(back_keep, back_low)
EPSILON = 1e-06
FLOOR_SCORE = -1e+30
SQRT_HALF = 0.7071067811865476
HIGH = lax.Precision.HIGHEST

def both_ways(values):
    return low_back(low(values))

def layer_norm(values, gain, shift):
    centre = values - lax.optimization_barrier(jnp.mean(values, axis=-1, keepdims=True))
    return centre * lax.rsqrt(lax.optimization_barrier(jnp.mean(centre * centre, axis=-1, keepdims=True)) + EPSILON) * gain + shift

def gelu(inner):
    return inner * (0.5 * (1.0 + lax.erf(inner * SQRT_HALF)))

def attend_row(item):
    query, keys, values, groups = item
    scores = low_back(jnp.einsum('qhd,khd->hqk', query, keys, precision=HIGH) * HEAD_DIM ** (-0.5))
    same = groups[:, None] == groups[None, :]
    scores = jnp.where(same[None], scores, FLOOR_SCORE)
    shares = jax.nn.softmax(scores, axis=-1)
    mixed = jnp.einsum('hqk,khd->qhd', low(shares), values, precision=HIGH)
    return both_ways(mixed)

def block_layer(params, block, groups, flags):
    mask_token, norm_gain, norm_shift, heads_weight, heads_bias, proj_weight, proj_bias, attn_scale, mlp_gain, mlp_shift, up_weight, up_bias, down_weight, down_bias, mlp_scale = params
    size = HEAD_DIM
    valid = (groups.reshape(-1, 1) >= 0).astype(jnp.float32)
    flagged = (flags.reshape(-1, 1) == 1).astype(jnp.float32)
    start = valid * (flagged * mask_token + (1.0 - flagged) * block)
    normed1 = low(layer_norm(start, norm_gain, norm_shift))
    packed = jnp.dot(normed1, heads_weight.reshape(D, HEADS * 3 * size), precision=HIGH).reshape(-1, HEADS, 3 * size)
    query = both_ways(packed[..., :size] + heads_bias[:, :size])
    keys = both_ways(packed[..., size:2 * size])
    values = both_ways(packed[..., 2 * size:] + heads_bias[:, size:])
    shape_rows = (N_TP, SLOTS, HEADS, size)
    mixed = lax.map(jax.checkpoint(attend_row), (query.reshape(shape_rows), keys.reshape(shape_rows), values.reshape(shape_rows), groups))
    mixed = mixed.reshape(-1, HEADS * size)
    branch1 = low_back(jnp.dot(mixed, proj_weight, precision=HIGH)) + proj_bias
    middle = start + attn_scale * branch1
    normed2 = low(layer_norm(middle, mlp_gain, mlp_shift))
    unit_input = low_back(jnp.dot(normed2, up_weight, precision=HIGH) + up_bias)
    unit_value = low(gelu(unit_input))
    branch2 = low_back(jnp.dot(unit_value, down_weight, precision=HIGH)) + down_bias
    return valid * (middle + mlp_scale * branch2)

def whole_layer(params, segment_ids, mask_flags):
    inputs = params[0]
    groups = segment_ids.shape[0] // N_TP
    span = N_TP * SLOTS

    def one_group(item):
        block, ids, flags = item
        return block_layer(params[1:], block, ids, flags)
    outs = lax.map(jax.checkpoint(one_group), (inputs.reshape(groups, span, D), segment_ids.reshape(groups, N_TP, SLOTS), mask_flags.reshape(groups, N_TP, SLOTS)))
    return outs.reshape(groups * span, D)

def reference(inputs, segment_ids, mask_flags, mask_token, norm_gain, norm_shift, heads_weight, heads_bias, proj_weight, proj_bias, attn_scale, mlp_gain, mlp_shift, up_weight, up_bias, down_weight, down_bias, mlp_scale, grad_out):
    floats = tuple((item.astype(jnp.float32) for item in (inputs, mask_token, norm_gain, norm_shift, heads_weight, heads_bias, proj_weight, proj_bias, attn_scale, mlp_gain, mlp_shift, up_weight, up_bias, down_weight, down_bias, mlp_scale)))

    def forward(*params):
        return whole_layer(params, segment_ids, mask_flags)
    output, pullback = jax.vjp(forward, *floats)
    grads = pullback(grad_out.astype(jnp.float32))
    return (output.astype(jnp.bfloat16), grads[0], grads[1], grads[2], grads[3], grads[4], grads[5], grads[6], grads[7], grads[8], grads[9], grads[10], grads[11], grads[12], grads[13], grads[14], grads[15])
```

```python
import functools

import jax
import jax.numpy as jnp
from jax import lax
from jax.sharding import PartitionSpec as P

EPSILON = 1e-06
FLOOR_SCORE = -1e30
SQRT_HALF = 0.7071067811865476
INV_ROOT_TWO_PI = 0.3989422804014327


def layer_norm(values, gain, shift):
    centre = values - jnp.mean(values, axis=-1, keepdims=True)
    inverse = lax.rsqrt(jnp.mean(centre * centre, axis=-1, keepdims=True) + EPSILON)
    scaled = centre * inverse
    return (scaled * gain + shift, scaled, inverse)


def norm_back(grad_normed, scaled, inverse, gain):
    grad_scaled = grad_normed * gain
    first = jnp.mean(grad_scaled, axis=-1, keepdims=True)
    second = jnp.mean(grad_scaled * scaled, axis=-1, keepdims=True)
    return inverse * (grad_scaled - first - scaled * second)


def gelu_parts(inner):
    normal_cdf = 0.5 * (1.0 + lax.erf(inner * SQRT_HALF))
    density = jnp.exp(-0.5 * inner * inner) * INV_ROOT_TWO_PI
    return (inner * normal_cdf, normal_cdf + inner * density)


def head_bias_row(bias, head_size):
    blank = jnp.zeros((bias.shape[0], head_size), jnp.float32)
    joined = jnp.concatenate(
        [bias[:, :head_size].astype(jnp.float32), blank, bias[:, head_size:].astype(jnp.float32)],
        axis=1,
    )
    return joined.reshape(-1)


def gather_weight(block, _):
    count = lax.axis_size("dp")
    rows = block.shape[0] // 8
    own = lax.dynamic_slice_in_dim(block, (lax.axis_index("dp") % 8) * rows, rows, 0)
    if count == 8:
        return lax.all_gather(own, ("tp", "dp"), axis=0, tiled=True)
    return lax.all_gather(block, "tp", axis=0, tiled=True)


def scatter_grad(partial):
    part = lax.psum_scatter(partial, ("tp", "dp"), scatter_dimension=0, tiled=True)
    return lax.all_gather(part, "dp", axis=0, tiled=True).astype(jnp.float32)


def local(
    inputs,
    segment_ids,
    mask_flags,
    mask_token,
    norm_gain,
    norm_shift,
    heads_weight,
    heads_bias,
    proj_weight,
    proj_bias,
    attn_scale,
    mlp_gain,
    mlp_shift,
    up_weight,
    up_bias,
    down_weight,
    down_bias,
    mlp_scale,
    grad_out,
):
    own_rows, slots = mask_flags.shape
    width = inputs.shape[1]
    triple = heads_weight.shape[2]
    head_size = triple // 3
    scale = head_size ** (-0.5)
    own_ids = lax.dynamic_slice_in_dim(segment_ids, lax.axis_index("tp") * own_rows, own_rows, 0)
    valid = (own_ids.reshape(-1, 1) >= 0).astype(jnp.float32)
    flagged = (mask_flags.reshape(-1, 1) == 1).astype(jnp.float32)
    f32, bf16 = jnp.float32, jnp.bfloat16
    dot = functools.partial(lax.dot_general, preferred_element_type=f32)
    nn = (((1,), (0,)), ((), ()))
    nt = (((1,), (1,)), ((), ()))
    tn = (((0,), (0,)), ((), ()))
    heads_all = gather_weight(heads_weight.reshape(width, -1), width // 8)
    proj_all = gather_weight(proj_weight, 0)
    up_all = gather_weight(up_weight, 0)
    down_all = gather_weight(down_weight, 0)
    n_tp = lax.axis_size("tp")
    all_heads_bias = lax.all_gather(heads_bias.astype(f32), "tp", axis=0, tiled=True)
    up_bias_all = lax.all_gather(up_bias.astype(f32), "tp", axis=0, tiled=True)
    heads_now = all_heads_bias.shape[0]
    start_x = valid * (flagged * mask_token.astype(f32) + (1.0 - flagged) * inputs.astype(f32))
    first_gain = norm_gain.astype(f32)
    second_gain = mlp_gain.astype(f32)
    normed1, scaled1, inverse1 = layer_norm(start_x, first_gain, norm_shift.astype(f32))
    normed1 = normed1.astype(bf16)
    heads_cat = jnp.moveaxis(heads_all.reshape(n_tp, width, -1), 0, 1).reshape(width, -1)
    packed = (dot(normed1, heads_cat, nn) + head_bias_row(all_heads_bias, head_size)).astype(bf16)
    blocks = packed.reshape(slots, heads_now, triple)
    query = blocks[..., :head_size]
    keys = blocks[..., head_size:2 * head_size]
    values = blocks[..., 2 * head_size:]
    groups = own_ids[0]
    same = (groups[:, None] == groups[None, :])[None]
    scores = jnp.einsum("qhd,khd->hqk", query, keys, preferred_element_type=f32) * scale
    scores = jnp.where(same, scores, FLOOR_SCORE)
    largest = jnp.max(scores, axis=-1, keepdims=True)
    raised = jnp.exp(scores - largest)
    total = jnp.sum(raised, axis=-1, keepdims=True)
    shares = (raised / total).astype(bf16)
    mixed = jnp.einsum("hqk,khd->qhd", shares, values, preferred_element_type=f32).astype(bf16)
    mixed = mixed.reshape(slots, -1)
    branch1 = dot(mixed, proj_all, nn) + proj_bias.astype(f32)
    middle = start_x + attn_scale.astype(f32) * branch1
    normed2, scaled2, inverse2 = layer_norm(middle, second_gain, mlp_shift.astype(f32))
    normed2 = normed2.astype(bf16)
    up_cat = jnp.moveaxis(up_all.reshape(n_tp, width, -1), 0, 1).reshape(width, -1)
    unit_input = dot(normed2, up_cat, nn) + up_bias_all
    unit_value, derivative = gelu_parts(unit_input)
    unit_low = unit_value.astype(bf16)
    branch2 = dot(unit_low, down_all, nn) + down_bias.astype(f32)
    output = (valid * (middle + mlp_scale.astype(f32) * branch2)).astype(bf16)
    grad_final = valid * grad_out.astype(f32)
    grad_scale2 = jnp.sum(branch2 * grad_final, axis=0)
    grad_branch2 = mlp_scale.astype(f32) * grad_final
    grad_down_bias = jnp.sum(grad_branch2, axis=0)
    grad_low2 = grad_branch2.astype(bf16)
    sum_down = scatter_grad(dot(unit_low, grad_low2, tn).astype(bf16))
    grad_unit = (dot(grad_low2, down_all, nt) * derivative).astype(bf16)
    columns = lambda g: jnp.moveaxis(g.reshape(width, n_tp, -1), 1, 0).reshape(n_tp * width, -1)
    sum_up = scatter_grad(columns(dot(normed2, grad_unit, tn).astype(bf16)))
    grad_up_bias = jnp.sum(grad_unit, axis=0, dtype=f32)
    grad_normed2 = dot(grad_unit, up_cat, nt)
    grad_gain2 = jnp.sum(grad_normed2 * scaled2, axis=0)
    grad_shift2 = jnp.sum(grad_normed2, axis=0)
    grad_middle = grad_final + norm_back(grad_normed2, scaled2, inverse2, second_gain)
    grad_scale1 = jnp.sum(branch1 * grad_middle, axis=0)
    grad_branch1 = attn_scale.astype(f32) * grad_middle
    grad_proj_bias = jnp.sum(grad_branch1, axis=0)
    grad_low1 = grad_branch1.astype(bf16)
    sum_proj = scatter_grad(dot(mixed, grad_low1, tn).astype(bf16))
    grad_mixed = dot(grad_low1, proj_all, nt).astype(bf16).reshape(slots, heads_now, head_size)
    exact = raised / total
    grad_shares = jnp.einsum("qhd,khd->hqk", grad_mixed, values, preferred_element_type=f32)
    centre = jnp.sum(exact * grad_shares, axis=-1, keepdims=True)
    grad_scores = (exact * (grad_shares - centre)).astype(bf16)
    grad_query = jnp.einsum("hqk,khd->qhd", grad_scores, keys, preferred_element_type=f32) * scale
    grad_keys = jnp.einsum("hqk,qhd->khd", grad_scores, query, preferred_element_type=f32) * scale
    grad_values = jnp.einsum("hqk,qhd->khd", shares, grad_mixed, preferred_element_type=f32)
    grad_packed = jnp.concatenate([grad_query, grad_keys, grad_values], axis=-1).astype(bf16)
    grad_packed = grad_packed.reshape(slots, -1)
    sum_heads = scatter_grad(columns(dot(normed1, grad_packed, tn).astype(bf16)))
    sum_heads = sum_heads.reshape(heads_weight.shape)
    bias_sums = jnp.sum(grad_packed, axis=0, dtype=f32).reshape(heads_now, triple)
    grad_normed1 = dot(grad_packed, heads_cat, nt)
    grad_gain1 = jnp.sum(grad_normed1 * scaled1, axis=0)
    grad_shift1 = jnp.sum(grad_normed1, axis=0)
    grad_start = grad_middle + norm_back(grad_normed1, scaled1, inverse1, first_gain)
    grad_inputs = valid * (1.0 - flagged) * grad_start
    grad_token = jnp.sum(valid * flagged * grad_start, axis=0)
    small = jnp.concatenate([
        grad_token, grad_gain1, grad_shift1, grad_proj_bias, grad_scale1, grad_gain2,
        grad_shift2, grad_down_bias, grad_scale2, bias_sums.reshape(-1), grad_up_bias])
    small = lax.psum(small, ("dp", "tp"))
    (sum_token, sum_gain1, sum_shift1, sum_proj_bias, sum_scale1, sum_gain2, sum_shift2,
     sum_down_bias, sum_scale2) = [small[i * width:(i + 1) * width] for i in range(9)]
    me = lax.axis_index("tp")
    bias_sums = small[9 * width:9 * width + heads_now * triple].reshape(heads_now, triple)
    bias_sums = lax.dynamic_slice_in_dim(bias_sums, me * heads_bias.shape[0], heads_bias.shape[0], 0)
    sum_heads_bias = jnp.concatenate([bias_sums[:, :head_size], bias_sums[:, 2 * head_size:]], axis=1)
    sum_up_bias = lax.dynamic_slice_in_dim(
        small[9 * width + heads_now * triple:], me * up_bias.shape[0], up_bias.shape[0], 0)
    return (
        output,
        grad_inputs,
        sum_token,
        sum_gain1,
        sum_shift1,
        sum_heads,
        sum_heads_bias,
        sum_proj,
        sum_proj_bias,
        sum_scale1,
        sum_gain2,
        sum_shift2,
        sum_up,
        sum_up_bias,
        sum_down,
        sum_down_bias,
        sum_scale2,
    )


def solution(mesh):
    placed = (
        P(("dp", "tp"), None),
        P("dp", None),
        P(("dp", "tp"), None),
        P(),
        P(),
        P(),
        P(None, "tp", None),
        P("tp", None),
        P("tp", None),
        P(),
        P(),
        P(),
        P(),
        P(None, "tp"),
        P("tp"),
        P("tp", None),
        P(),
        P(),
        P(("dp", "tp"), None),
    )
    return jax.shard_map(
        local,
        mesh=mesh,
        in_specs=placed,
        out_specs=(
            P(("dp", "tp"), None),
            P(("dp", "tp"), None),
            P(),
            P(),
            P(),
            P(None, "tp", None),
            P("tp", None),
            P("tp", None),
            P(),
            P(),
            P(),
            P(),
            P(None, "tp"),
            P("tp"),
            P("tp", None),
            P(),
            P(),
        ),
        check_vma=False,
    )
```

```python
import functools

import jax
import jax.numpy as jnp
from jax import lax
from jax.experimental import pallas as pl
from jax.experimental.pallas import tpu as pltpu
from jax.sharding import PartitionSpec as P

EPSILON = 1e-06
FLOOR_SCORE = -1e30
SQRT_HALF = 0.7071067811865476
INV_ROOT_TWO_PI = 0.3989422804014327
LONGEST = 14 * 14 + 1
FIFTH_FROM = 4 * (11 * 11 + 1)
TILE = 128
CORE, X, Y = 1, 2, 4

f32, bf16 = jnp.float32, jnp.bfloat16
NN = (((1,), (0,)), ((), ()))
NT = (((1,), (1,)), ((), ()))
TN = (((0,), (0,)), ((), ()))


def dot(a, b, dims=NN):
    return lax.dot_general(a, b, dims, preferred_element_type=f32)


def layer_norm(values, gain, shift):
    centre = values - jnp.mean(values, axis=-1, keepdims=True)
    inverse = lax.rsqrt(jnp.mean(centre * centre, axis=-1, keepdims=True) + EPSILON)
    scaled = centre * inverse
    return (scaled * gain + shift, scaled, inverse)


def norm_back(grad_normed, scaled, inverse, gain):
    grad_scaled = grad_normed * gain
    first = jnp.mean(grad_scaled, axis=-1, keepdims=True)
    second = jnp.mean(grad_scaled * scaled, axis=-1, keepdims=True)
    return inverse * (grad_scaled - first - scaled * second)


def gelu_parts(inner):
    normal_cdf = 0.5 * (1.0 + lax.erf(inner * SQRT_HALF))
    density = jnp.exp(-0.5 * inner * inner) * INV_ROOT_TWO_PI
    return (inner * normal_cdf, normal_cdf + inner * density)


def head_bias_row(bias, head_size):
    blank = jnp.zeros((bias.shape[0], head_size), f32)
    joined = jnp.concatenate(
        [bias[:, :head_size].astype(f32), blank, bias[:, head_size:].astype(f32)], axis=1
    )
    return joined.reshape(1, -1)


def exchange(value, dp_bits=0, tp_bits=0):
    n_dp, n_tp = lax.axis_size("dp"), lax.axis_size("tp")
    pairs = [
        (d * n_tp + t, (d ^ dp_bits) * n_tp + (t ^ tp_bits)) for d in range(n_dp) for t in range(n_tp)
    ]
    return lax.ppermute(value, ("dp", "tp"), pairs)


def spread(value, first, second):
    held = {0: value}
    for bits in (first, second, CORE):
        held.update({at ^ bits: exchange(item, bits) for at, item in list(held.items())})
    return held


def windows(slots):
    out = []
    for low in range(0, slots, TILE):
        high = min(low + TILE, slots)
        begin = low - LONGEST + 1
        if low >= FIFTH_FROM:
            begin = min(begin, FIFTH_FROM)
        end = high + LONGEST - 1
        if high > FIFTH_FROM:
            end = slots
        begin = max(begin, 0) // 128 * 128
        end = min((end + 127) // 128 * 128, slots)
        out.append((low, high, begin, end))
    return out


def as_row(column):
    rows = column.shape[0]
    shape = (rows, rows)
    here = lax.broadcasted_iota(jnp.int32, shape, 0) == lax.broadcasted_iota(jnp.int32, shape, 1)
    return jnp.sum(jnp.where(here, column, 0.0), axis=0, keepdims=True)


def attend_kernel(normed_ref, weight_ref, bias_ref, column_ref, row_ref, packed_ref, mixed_ref, lse_ref):
    slots = normed_ref.shape[0]
    triple = weight_ref.shape[2] // 3
    size = triple // 3
    scale = size ** (-0.5)
    for low in range(0, slots, 208):
        high = min(low + 208, slots)
        packed_ref[0, low:high, :] = (dot(normed_ref[low:high, :], weight_ref[0]) + bias_ref[0]).astype(bf16)
    lse_ref[...] = jnp.zeros_like(lse_ref)
    for head in range(3):
        base = head * triple
        for low, high, begin, end in windows(slots):
            query = packed_ref[0, low:high, base:base + size] * jnp.bfloat16(scale)
            keys = packed_ref[0, begin:end, base + size:base + 2 * size]
            values = packed_ref[0, begin:end, base + 2 * size:base + 3 * size]
            scores = dot(query, keys, NT)
            same = column_ref[low:high, :] == row_ref[:, begin:end]
            scores = jnp.where(same, scores, FLOOR_SCORE)
            largest = jnp.max(scores, axis=1, keepdims=True)
            raised = jnp.exp(scores - largest)
            total = jnp.sum(raised, axis=1, keepdims=True)
            mixed = dot(raised.astype(bf16), values) * (1.0 / total)
            mixed_ref[0, low:high, head * size:(head + 1) * size] = mixed.astype(bf16)
            lse_ref[0, head:head + 1, low:high] = as_row(largest + jnp.log(total))


def attend(normed, weight, bias, column, row, offset, count):
    _, width, columns = weight.shape
    slots = normed.shape[0]
    whole = lambda shape: pl.BlockSpec(shape, lambda k: (0,) * len(shape))
    each = lambda *shape: pl.BlockSpec((1,) + shape, lambda k: (k, 0, 0))
    return pl.pallas_call(
        attend_kernel,
        grid=(count,),
        in_specs=[
            whole((slots, width)),
            pl.BlockSpec((1, width, columns), lambda k: (k + offset, 0, 0)),
            pl.BlockSpec((1, 1, columns), lambda k: (k + offset, 0, 0)),
            whole((slots, 1)),
            whole((1, slots)),
        ],
        out_specs=[each(slots, columns), each(slots, columns // 3), each(8, slots)],
        out_shape=[
            jax.ShapeDtypeStruct((count, slots, columns), bf16),
            jax.ShapeDtypeStruct((count, slots, columns // 3), bf16),
            jax.ShapeDtypeStruct((count, 8, slots), f32),
        ],
        compiler_params=pltpu.CompilerParams(vmem_limit_bytes=50 << 20),
        cost_estimate=pl.CostEstimate(flops=count * 4 * 10**9, transcendentals=count * 3 * 480000, bytes_accessed=count * 4 * 10**6),
        name="attend",
    )(normed, weight, bias, column, row)


def whole(*shape):
    return pl.BlockSpec(shape, lambda k: (0,) * len(shape))


def each(*shape, at=lambda k: k):
    return pl.BlockSpec((1,) + shape, lambda k: (at(k),) + (0,) * len(shape))


def params(megabytes):
    return pltpu.CompilerParams(vmem_limit_bytes=megabytes << 20)


def cost(flops, moved, exps=0):
    return pl.CostEstimate(flops=int(flops), transcendentals=int(exps), bytes_accessed=int(moved))


def axis_bit(bit):
    return lax.rem(lax.div(lax.axis_index("dp"), bit), 2)


def split_store(bit, value, give_ref, keep_ref):
    rows = value.shape[0] // 2
    mine = axis_bit(bit)
    low, high = value[:rows].astype(bf16), value[rows:].astype(bf16)

    @pl.when(mine == 0)
    def _():
        keep_ref[0] = low
        give_ref[0] = high

    @pl.when(mine == 1)
    def _():
        keep_ref[0] = high
        give_ref[0] = low


def attend_back_kernel(
    grad_ref, proj_ref, packed_ref, mixed_ref, lse_ref, normed_ref, weight_ref, column_ref, row_ref,
    give_ref, keep_ref, give_proj_ref, keep_proj_ref, grad_bias_ref, grad_normed_ref,
    grad_mixed, grad_packed, delta, grad_query,
):
    slots = normed_ref.shape[0]
    triple = weight_ref.shape[2] // 3
    size = triple // 3
    scale = size ** (-0.5)
    tiles = windows(slots)
    for low in range(0, slots, 208):
        grad_mixed[low:low + 208, :] = dot(grad_ref[low:low + 208, :], proj_ref[...], NT).astype(bf16)
    split_store(CORE, dot(mixed_ref[0], grad_ref[...], TN), give_proj_ref, keep_proj_ref)
    for head in range(3):
        base = head * triple
        own = slice(head * size, (head + 1) * size)
        for low, high, _, _ in tiles:
            product = grad_mixed[low:high, own].astype(f32) * mixed_ref[0, low:high, own].astype(f32)
            delta[0:1, low:high] = as_row(jnp.sum(product, axis=1, keepdims=True))
        grad_query[...] = jnp.zeros_like(grad_query)
        for low, high, begin, end in tiles:
            keys = packed_ref[0, low:high, base + size:base + 2 * size]
            values = packed_ref[0, low:high, base + 2 * size:base + 3 * size]
            query = packed_ref[0, begin:end, base:base + size] * jnp.bfloat16(scale)
            grads = grad_mixed[begin:end, own]
            scores = dot(keys, query, NT)
            same = column_ref[low:high, :] == row_ref[:, begin:end]
            shares = jnp.exp(jnp.where(same, scores - lse_ref[0, head:head + 1, begin:end], FLOOR_SCORE))
            grad_shares = dot(values, grads, NT)
            grad_scores = (shares * (grad_shares - delta[0:1, begin:end])).astype(bf16)
            grad_packed[low:high, base + 2 * size:base + 3 * size] = dot(shares.astype(bf16), grads).astype(bf16)
            grad_packed[low:high, base + size:base + 2 * size] = dot(grad_scores, query).astype(bf16)
            grad_query[begin:end, :] += dot(grad_scores, keys, TN)
        grad_packed[:, base:base + size] = (grad_query[...] * scale).astype(bf16)
    split_store(CORE, dot(normed_ref[...], grad_packed[...], TN), give_ref, keep_ref)
    grad_bias_ref[0] = jnp.sum(grad_packed[...].astype(f32), axis=0, keepdims=True)

    first = pl.program_id(0) == 0
    for low in range(0, slots, 208):
        part = dot(grad_packed[low:low + 208, :], weight_ref[0], NT)

        @pl.when(first)
        def _():
            grad_normed_ref[low:low + 208, :] = part

        @pl.when(jnp.logical_not(first))
        def _():
            grad_normed_ref[low:low + 208, :] += part


def attend_back(shards, grad, proj, packed, mixed, lse, normed, weight, column, row):
    _, width, columns = weight.shape
    slots = normed.shape[0]
    mixed_columns = columns // 3
    at = lambda k: jnp.where(k == 0, shards[0], shards[1])
    half, half_proj = width // 2, mixed_columns // 2
    return pl.pallas_call(
        attend_back_kernel,
        grid=(2,),
        in_specs=[
            whole(slots, width), pl.BlockSpec((mixed_columns, width), lambda k: (at(k), 0)),
            each(slots, columns, at=at), each(slots, mixed_columns, at=at),
            each(8, slots, at=at), whole(slots, width), each(width, columns, at=at), whole(slots, 1), whole(1, slots),
        ],
        out_specs=[
            each(half, columns), each(half, columns), each(half_proj, width), each(half_proj, width),
            each(1, columns), whole(slots, width),
        ],
        out_shape=[
            jax.ShapeDtypeStruct((2, half, columns), bf16),
            jax.ShapeDtypeStruct((2, half, columns), bf16),
            jax.ShapeDtypeStruct((2, half_proj, width), bf16),
            jax.ShapeDtypeStruct((2, half_proj, width), bf16),
            jax.ShapeDtypeStruct((2, 1, columns), f32),
            jax.ShapeDtypeStruct((slots, width), f32),
        ],
        scratch_shapes=[
            pltpu.VMEM((slots, mixed_columns), bf16),
            pltpu.VMEM((slots, columns), bf16),
            pltpu.VMEM((8, slots), f32),
            pltpu.VMEM((slots, columns // 9), f32),
        ],
        compiler_params=params(40),
        cost_estimate=cost(2 * 8e9, 2 * 5e6, 2 * 3 * 480000),
        name="attend_back",
    )(grad, proj, packed, mixed, lse, normed, weight, column, row)


def start_of(inputs_ref, column_ref, flag_ref, token_ref, low, high):
    valid = (column_ref[low:high, :] >= 0).astype(f32)
    flagged = (flag_ref[low:high, :] == 1).astype(f32)
    start = valid * (flagged * token_ref[...].astype(f32) + (1.0 - flagged) * inputs_ref[low:high, :].astype(f32))
    return valid, flagged, start


def rows_of(slots, step=104):
    return [(low, min(low + step, slots)) for low in range(0, slots, step)]


def first_norm_kernel(inputs_ref, column_ref, flag_ref, token_ref, gain_ref, shift_ref, normed_ref):
    gain, shift = gain_ref[...].astype(f32), shift_ref[...].astype(f32)
    for low, high in rows_of(inputs_ref.shape[0]):
        _, _, start = start_of(inputs_ref, column_ref, flag_ref, token_ref, low, high)
        normed_ref[low:high, :] = layer_norm(start, gain, shift)[0].astype(bf16)


def first_norm(inputs, column, flag, token, gain, shift):
    return pl.pallas_call(
        first_norm_kernel,
        out_shape=jax.ShapeDtypeStruct(inputs.shape, bf16),
        compiler_params=params(16),
        cost_estimate=cost(1e7, 4e6),
        name="first_norm",
    )(inputs, column, flag, token, gain, shift)


def mlp_kernel(
    inputs_ref, column_ref, flag_ref, token_ref, mixed0_ref, mixed1_ref, proj_ref, proj_bias_ref, attn_scale_ref,
    gain_ref, shift_ref, up_ref, unit_bias_ref, down_ref, down_bias_ref, mlp_scale_ref, grad_out_ref,
    branch1_ref, middle_ref, normed_ref, hidden_ref, slope_ref, output_ref, grad_low_ref, sums_ref,
    mixed, total,
):
    slots = inputs_ref.shape[0]
    part = mixed0_ref.shape[2]
    k = pl.program_id(0)

    @pl.when(k == 0)
    def _():
        mixed[:, :part] = mixed0_ref[0]
        for n in range(3):
            mixed[:, (n + 1) * part:(n + 2) * part] = mixed1_ref[n]
        proj_bias, attn_scale = proj_bias_ref[...].astype(f32), attn_scale_ref[...].astype(f32)
        gain, shift = gain_ref[...].astype(f32), shift_ref[...].astype(f32)
        for low, high in rows_of(slots, 208):
            _, _, start = start_of(inputs_ref, column_ref, flag_ref, token_ref, low, high)
            branch1 = dot(mixed[low:high, :], proj_ref[...]) + proj_bias
            middle = start + attn_scale * branch1
            branch1_ref[low:high, :] = branch1.astype(bf16)
            middle_ref[low:high, :] = middle
            normed_ref[low:high, :] = layer_norm(middle, gain, shift)[0].astype(bf16)
        total[...] = jnp.zeros_like(total)

    units = up_ref.shape[2]
    for low, high in rows_of(slots, 208):
        for left in range(0, units, 256):
            columns = slice(left, left + 256)
            inner = dot(normed_ref[low:high, :], up_ref[0, :, columns]) + unit_bias_ref[0, :, columns]
            value, slope = gelu_parts(inner)
            hidden_ref[0, low:high, columns] = value.astype(bf16)
            slope_ref[0, low:high, columns] = slope.astype(bf16)
        total[low:high, :] += dot(hidden_ref[0, low:high, :], down_ref[0])

    @pl.when(k == pl.num_programs(0) - 1)
    def _():
        down_bias, mlp_scale = down_bias_ref[...].astype(f32), mlp_scale_ref[...].astype(f32)
        sums_ref[...] = jnp.zeros_like(sums_ref)
        for low, high in rows_of(slots):
            valid = (column_ref[low:high, :] >= 0).astype(f32)
            branch2 = total[low:high, :] + down_bias
            output_ref[low:high, :] = (valid * (middle_ref[low:high, :] + mlp_scale * branch2)).astype(bf16)
            grad_final = valid * grad_out_ref[low:high, :].astype(f32)
            grad_branch2 = mlp_scale * grad_final
            grad_low_ref[low:high, :] = grad_branch2.astype(bf16)
            sums_ref[0:1, :] += jnp.sum(branch2 * grad_final, axis=0, keepdims=True)
            sums_ref[1:2, :] += jnp.sum(grad_branch2, axis=0, keepdims=True)


def mlp(inputs, column, flag, token, mixed0, mixed1, proj, proj_bias, attn_scale, gain, shift, up, unit_bias,
        down, down_bias, mlp_scale, grad_out):
    slots, width = inputs.shape
    count, _, units = up.shape
    vector = whole(1, width)
    tokens = whole(slots, width)
    return pl.pallas_call(
        mlp_kernel,
        grid=(count,),
        in_specs=[
            tokens, whole(slots, 1), whole(slots, 1), vector, whole(*mixed0.shape), whole(*mixed1.shape),
            whole(width, width), vector, vector, vector, vector, each(width, units), each(1, units),
            each(units, width), vector, vector, tokens,
        ],
        out_specs=[
            tokens, tokens, tokens, each(slots, units), each(slots, units), tokens, tokens, whole(8, width),
        ],
        out_shape=[
            jax.ShapeDtypeStruct((slots, width), bf16),
            jax.ShapeDtypeStruct((slots, width), f32),
            jax.ShapeDtypeStruct((slots, width), bf16),
            jax.ShapeDtypeStruct((count, slots, units), bf16),
            jax.ShapeDtypeStruct((count, slots, units), bf16),
            jax.ShapeDtypeStruct((slots, width), bf16),
            jax.ShapeDtypeStruct((slots, width), bf16),
            jax.ShapeDtypeStruct((8, width), f32),
        ],
        scratch_shapes=[pltpu.VMEM((slots, width), bf16), pltpu.VMEM((slots, width), f32)],
        compiler_params=params(48),
        cost_estimate=cost(9e9, 30e6, 5e6),
        name="mlp",
    )(inputs, column, flag, token, mixed0, mixed1, proj, proj_bias, attn_scale, gain, shift, up, unit_bias,
      down, down_bias, mlp_scale, grad_out)


def down_back_kernel(hidden_ref, grad_low_ref, give_ref, keep_ref):
    split_store(CORE, dot(hidden_ref[0], grad_low_ref[...], TN), give_ref, keep_ref)


def down_back(hidden, grad_low):
    count, slots, units = hidden.shape
    width = grad_low.shape[1]
    out = jax.ShapeDtypeStruct((count, units // 2, width), bf16)
    return pl.pallas_call(
        down_back_kernel,
        grid=(count,),
        in_specs=[each(slots, units), whole(slots, width)],
        out_specs=[each(units // 2, width), each(units // 2, width)],
        out_shape=[out, out],
        compiler_params=params(24),
        cost_estimate=cost(4e9, 12e6),
        name="down_back",
    )(hidden, grad_low)


def mlp_back_kernel(
    grad_low_ref, slope_ref, down_ref, up_ref, normed_ref, middle_ref, branch1_ref, grad_out_ref, column_ref,
    gain_ref, shift_ref, attn_scale_ref, mlp_scale_ref,
    give_ref, keep_ref, unit_bias_ref, grad_middle_ref, grad_low1_ref, sums_ref,
    grad_unit, total, flipped,
):
    slots, width = normed_ref.shape
    k = pl.program_id(0)

    @pl.when(k == 0)
    def _():
        total[...] = jnp.zeros_like(total)
        flipped[...] = normed_ref[...].T

    unit_sum = jnp.zeros((1, slope_ref.shape[2]), f32)
    for low, high in rows_of(slots, 208):
        unit = (dot(grad_low_ref[low:high, :], down_ref[0], NT) * slope_ref[0, low:high, :].astype(f32)).astype(bf16)
        grad_unit[low:high, :] = unit
        unit_sum += jnp.sum(unit.astype(f32), axis=0, keepdims=True)
        total[low:high, :] += dot(unit, up_ref[0], NT)
    unit_bias_ref[0] = unit_sum
    split_store(CORE, dot(flipped[...], grad_unit[...]), give_ref, keep_ref)

    @pl.when(k == pl.num_programs(0) - 1)
    def _():
        gain, attn_scale = gain_ref[...].astype(f32), attn_scale_ref[...].astype(f32)
        sums_ref[...] = jnp.zeros_like(sums_ref)
        for low, high in rows_of(slots):
            valid = (column_ref[low:high, :] >= 0).astype(f32)
            grad_final = valid * grad_out_ref[low:high, :].astype(f32)
            grad_normed = total[low:high, :]
            _, scaled, inverse = layer_norm(middle_ref[low:high, :], gain, gain)
            grad_middle = grad_final + norm_back(grad_normed, scaled, inverse, gain)
            grad_branch1 = attn_scale * grad_middle
            grad_middle_ref[low:high, :] = grad_middle
            grad_low1_ref[low:high, :] = grad_branch1.astype(bf16)
            sums_ref[0:1, :] += jnp.sum(grad_normed * scaled, axis=0, keepdims=True)
            sums_ref[1:2, :] += jnp.sum(grad_normed, axis=0, keepdims=True)
            sums_ref[2:3, :] += jnp.sum(branch1_ref[low:high, :].astype(f32) * grad_middle, axis=0, keepdims=True)
            sums_ref[3:4, :] += jnp.sum(grad_branch1, axis=0, keepdims=True)


def mlp_back(grad_low, slope, down, up, normed, middle, branch1, grad_out, column, gain, shift, attn_scale, mlp_scale):
    slots, width = normed.shape
    count, _, units = up.shape
    vector, tokens = whole(1, width), whole(slots, width)
    out = jax.ShapeDtypeStruct((count, width // 2, units), bf16)
    return pl.pallas_call(
        mlp_back_kernel,
        grid=(count,),
        in_specs=[
            tokens, each(slots, units), each(units, width), each(width, units), tokens, tokens, tokens, tokens,
            whole(slots, 1), vector, vector, vector, vector,
        ],
        out_specs=[
            each(width // 2, units), each(width // 2, units), each(1, units), tokens, tokens, whole(8, width),
        ],
        out_shape=[
            out, out,
            jax.ShapeDtypeStruct((count, 1, units), f32),
            jax.ShapeDtypeStruct((slots, width), f32),
            jax.ShapeDtypeStruct((slots, width), bf16),
            jax.ShapeDtypeStruct((8, width), f32),
        ],
        scratch_shapes=[pltpu.VMEM((slots, units), bf16), pltpu.VMEM((slots, width), f32), pltpu.VMEM((width, slots), bf16)],
        compiler_params=params(48),
        cost_estimate=cost(12e9, 30e6),
        name="mlp_back",
    )(grad_low, slope, down, up, normed, middle, branch1, grad_out, column, gain, shift, attn_scale, mlp_scale)


def last_kernel(
    inputs_ref, column_ref, flag_ref, token_ref, gain_ref, grad_a_ref, grad_b_ref, grad_middle_ref, out_ref, sums_ref
):
    gain = gain_ref[...].astype(f32)
    sums_ref[...] = jnp.zeros_like(sums_ref)
    for low, high in rows_of(inputs_ref.shape[0]):
        valid, flagged, start = start_of(inputs_ref, column_ref, flag_ref, token_ref, low, high)
        _, scaled, inverse = layer_norm(start, gain, gain)
        grad_normed = grad_a_ref[low:high, :] + grad_b_ref[low:high, :]
        grad_start = grad_middle_ref[low:high, :] + norm_back(grad_normed, scaled, inverse, gain)
        out_ref[low:high, :] = valid * (1.0 - flagged) * grad_start
        sums_ref[0:1, :] += jnp.sum(valid * flagged * grad_start, axis=0, keepdims=True)
        sums_ref[1:2, :] += jnp.sum(grad_normed * scaled, axis=0, keepdims=True)
        sums_ref[2:3, :] += jnp.sum(grad_normed, axis=0, keepdims=True)


def last(inputs, column, flag, token, gain, grad_a, grad_b, grad_middle):
    slots, width = inputs.shape
    return pl.pallas_call(
        last_kernel,
        out_shape=[jax.ShapeDtypeStruct((slots, width), f32), jax.ShapeDtypeStruct((8, width), f32)],
        compiler_params=params(24),
        cost_estimate=cost(2e7, 12e6),
        name="last",
    )(inputs, column, flag, token, gain, grad_a, grad_b, grad_middle)


def place_kernel(rows, mine_ref, *refs):
    n = len(rows)
    pieces, owns, outs = refs[:8], refs[8:8 + n], refs[8 + n:]
    step = pl.program_id(0)
    for i in range(n):
        outs[i][0] = owns[i][...]
    for at in range(8):

        @pl.when(step == at)
        def _():
            begin = 0
            for i, height in enumerate(rows):
                outs[i][1:4] = pieces[at][:, begin:begin + height, :]
                begin += height


def place(held, owns):
    rows = [own.shape[0] // 8 for own in owns]
    columns = owns[0].shape[1]
    mine = lax.rem(lax.axis_index("dp"), 8).reshape(1)
    spot = lambda at, mine: jnp.bitwise_xor(at, mine[0])
    return pl.pallas_call(
        functools.partial(place_kernel, rows),
        grid_spec=pltpu.PrefetchScalarGridSpec(
            num_scalar_prefetch=1,
            grid=(8,),
            in_specs=[pl.BlockSpec(held[0].shape, lambda at, mine: (0, 0, 0))] * 8
            + [pl.BlockSpec((height, columns), lambda at, mine: (spot(at, mine), 0)) for height in rows],
            out_specs=[pl.BlockSpec((4, height, columns), lambda at, mine: (0, spot(at, mine), 0)) for height in rows],
        ),
        out_shape=[jax.ShapeDtypeStruct((4,) + own.shape, bf16) for own in owns],
        compiler_params=params(20),
        cost_estimate=cost(0, 2 * 4 * sum(own.size for own in owns) * 2),
        name="place",
    )(mine, *[held[at] for at in range(8)], *owns)


def own_eighth(block):
    rows = block.shape[0] // 8
    return lax.dynamic_slice_in_dim(block, lax.rem(lax.axis_index("dp"), 8) * rows, rows, 0)


def others(value):
    return [exchange(value, 0, k) for k in (1, 2, 3)]


def join_kernel(order, *refs):
    pieces, out = refs[:8], refs[8]
    mine = lax.axis_index("dp")
    rows = pieces[0].shape[0]
    for at in range(8):
        owner = jnp.bitwise_xor(mine, at)
        spot = 0
        for bit in order:
            spot = spot * 2 + lax.rem(lax.div(owner, bit), 2)
        out[pl.ds(pl.multiple_of(spot * rows, 8), rows), :] = pieces[at][...].astype(f32)


def join(held, order):
    rows, columns = held[0].shape
    return pl.pallas_call(
        functools.partial(join_kernel, order),
        out_shape=jax.ShapeDtypeStruct((8 * rows, columns), f32),
        in_specs=[pl.BlockSpec(memory_space=pltpu.VMEM)] * 8,
        out_specs=pl.BlockSpec(memory_space=pltpu.VMEM),
        compiler_params=params(12),
        cost_estimate=cost(0, 8 * rows * columns * 6),
        name="join",
    )(*[held[at] for at in range(8)])


def stage_kernel(bit, count, *refs):
    mine = axis_bit(bit)
    for n in range(count):
        kept, got, give, keep = (refs[part * count + n] for part in range(4))
        rows = kept.shape[1] // 2
        for own in (0, 1):

            @pl.when(mine == own)
            def _():
                for out, index in ((keep, own), (give, 1 - own)):
                    part = slice(index * rows, (index + 1) * rows)
                    out[...] = (kept[:, part, :].astype(f32) + got[:, part, :].astype(f32)).astype(bf16)


def stage(bit, kept, got):
    out = [jax.ShapeDtypeStruct((item.shape[0], item.shape[1] // 2, item.shape[2]), bf16) for item in kept]
    result = pl.pallas_call(
        functools.partial(stage_kernel, bit, len(kept)),
        out_shape=out + out,
        compiler_params=params(20),
        cost_estimate=cost(0, 6 * sum(item.size for item in kept)),
        name="stage",
    )(*kept, *got)
    return result[:len(kept)], result[len(kept):]


def add(a, b):
    return (a.astype(f32) + b.astype(f32)).astype(bf16)


def swap(items, bit):
    return [exchange(item, bit) for item in items]


def upper(total):
    bit = 8
    while bit < lax.axis_size("dp"):
        total = add(total, exchange(total, bit))
        bit *= 2
    return total


def after(items, *needs):
    return lax.optimization_barrier((items, needs))[0]


def local(
    inputs,
    segment_ids,
    mask_flags,
    mask_token,
    norm_gain,
    norm_shift,
    heads_weight,
    heads_bias,
    proj_weight,
    proj_bias,
    attn_scale,
    mlp_gain,
    mlp_shift,
    up_weight,
    up_bias,
    down_weight,
    down_bias,
    mlp_scale,
    grad_out,
):
    slots = mask_flags.shape[1]
    own_rows = mask_flags.shape[0]
    width = inputs.shape[1]
    triple = heads_weight.shape[2]
    head_size = triple // 3
    heads_here = heads_weight.shape[1]
    own_ids = lax.dynamic_slice_in_dim(segment_ids, lax.axis_index("tp") * own_rows, own_rows, 0)
    column, row = own_ids.reshape(-1, 1), own_ids.reshape(1, -1)
    flag = mask_flags.reshape(-1, 1)
    vector = lambda v: v.reshape(1, -1)
    token, gain1, gain2 = vector(mask_token), vector(norm_gain), vector(mlp_gain)
    own_heads = heads_weight.reshape(width, -1)
    heads_cols = own_heads.shape[1]

    heads_piece = own_eighth(own_heads)
    heads_others = jnp.stack(others(heads_piece))
    mix_piece = jnp.concatenate([own_eighth(up_weight), own_eighth(proj_weight)], axis=0)
    down_piece = own_eighth(down_weight)
    mix_others = jnp.stack(others(after(mix_piece, heads_others)))
    down_others = jnp.stack(others(after(down_piece, mix_others)))
    heads_held = spread(heads_others, X, Y)
    mix_held = spread(mix_others, Y, X)
    down_held = spread(down_others, X, Y)
    own_bias = jnp.concatenate([head_bias_row(heads_bias, head_size), up_bias.astype(f32).reshape(1, -1)], axis=1)
    bias = jnp.stack([own_bias] + others(own_bias))
    head_bias, unit_bias = bias[:, :, :heads_cols], bias[:, :, heads_cols:]

    normed1 = first_norm(inputs, column, flag, token, gain1, vector(norm_shift))
    packed0, mixed0, lse0 = attend(normed1, own_heads[None], head_bias[:1], column, row, 0, 1)
    (heads_all,) = place(heads_held, [own_heads])
    packed1, mixed1, lse1 = attend(normed1, heads_all, head_bias, column, row, 1, 3)
    up_all, proj_all = place(mix_held, [up_weight, proj_weight])
    (down_all,) = place(down_held, [down_weight])
    proj_flat = proj_all.reshape(-1, width)
    branch1, middle, normed2, hidden, slope, output, grad_low2, sums_a = mlp(
        inputs, column, flag, token, mixed0, mixed1, proj_flat, vector(proj_bias), vector(attn_scale), gain2,
        vector(mlp_shift), up_all, unit_bias, down_all, vector(down_bias), vector(mlp_scale), grad_out,
    )
    packed = jnp.concatenate([packed0, packed1], axis=0)
    mixed = jnp.concatenate([mixed0, mixed1], axis=0)
    lse = jnp.concatenate([lse0, lse1], axis=0)

    d_give, d_keep = down_back(hidden, grad_low2)
    d_got = exchange(d_give, CORE)
    u_give, u_keep, unit_sums, grad_middle, grad_low1, sums_b = mlp_back(
        grad_low2, slope, down_all, up_all, normed2, middle, branch1, grad_out, column, gain2, vector(mlp_shift),
        vector(attn_scale), vector(mlp_scale),
    )
    u_got = exchange(u_give, CORE)
    (d_give,), (d_keep,) = stage(X, [d_keep], [d_got])
    d_got = exchange(d_give, X)
    (u_give,), (u_keep,) = stage(Y, [u_keep], [u_got])
    u_got = exchange(u_give, Y)
    grad_low1 = after(grad_low1, d_give, u_give)
    h_give, h_keep, p_give, p_keep, head_sums_a, grad_normed_a = attend_back(
        (1, 2), grad_low1, proj_flat, packed, mixed, lse, normed1, heads_all, column, row
    )
    (d_give,), (d_keep,) = stage(Y, [d_keep], [d_got])
    d_got = exchange(d_give, Y)
    (u_give,), (u_keep,) = stage(X, [u_keep], [u_got])
    u_got = exchange(u_give, X)
    h_got, p_got = swap([h_give, p_give], CORE)
    grad_low1 = after(grad_low1, d_give, u_give, h_give)
    g_give, g_keep, q_give, q_keep, head_sums_b, grad_normed_b = attend_back(
        (3, 0), grad_low1, proj_flat, packed, mixed, lse, normed1, heads_all, column, row
    )
    g_got, q_got = swap([g_give, q_give], CORE)
    (h_give, p_give), (h_keep, p_keep) = stage(X, [h_keep, p_keep], [h_got, p_got])
    h_got, p_got = swap([h_give, p_give], X)
    d_total, u_total = upper(add(d_keep, d_got)), upper(add(u_keep, u_got))
    d_parts = [d_total[0]] + [exchange(d_total[k], 0, k) for k in (1, 2, 3)]
    u_parts = [u_total[0]] + [exchange(u_total[k], 0, k) for k in (1, 2, 3)]
    (g_give, q_give), (g_keep, q_keep) = stage(X, [g_keep, q_keep], [g_got, q_got])
    g_got, q_got = swap([g_give, q_give], X)
    grad_inputs, sums_c = last(inputs, column, flag, token, gain1, grad_normed_a, grad_normed_b, grad_middle)
    (h_give, p_give), (h_keep, p_keep) = stage(Y, [h_keep, p_keep], [h_got, p_got])
    h_got, p_got = swap([h_give, p_give], Y)
    (g_give, q_give), (g_keep, q_keep) = stage(Y, [g_keep, q_keep], [g_got, q_got])
    g_got, q_got = swap([g_give, q_give], Y)
    h_total, p_total = upper(add(h_keep, h_got)), upper(add(p_keep, p_got))
    g_total, q_total = upper(add(g_keep, g_got)), upper(add(q_keep, q_got))
    h_parts = [g_total[1], exchange(h_total[0], 0, 1), exchange(h_total[1], 0, 2), exchange(g_total[0], 0, 3)]
    p_parts = [q_total[1], exchange(p_total[0], 0, 1), exchange(p_total[1], 0, 2), exchange(q_total[0], 0, 3)]

    def finish(parts, first, second):
        mine = sum(part.astype(f32) for part in parts).astype(bf16)
        return join(spread(mine, second, first), (CORE, first, second))

    sum_down = finish(d_parts, X, Y)
    sum_up = finish(u_parts, Y, X)
    sum_heads, sum_proj = finish(h_parts, X, Y), finish(p_parts, X, Y)
    sum_heads = sum_heads.reshape(heads_weight.shape)

    head_sums = jnp.concatenate([head_sums_b[1], head_sums_a[0], head_sums_a[1], head_sums_b[0]], axis=0)
    bias_parts = jnp.concatenate([head_sums, unit_sums[:, 0, :]], axis=1)
    bias_size = bias_parts.size
    small = jnp.concatenate([
        bias_parts.reshape(-1), sums_c[:3].reshape(-1), sums_b[3], sums_b[2], sums_b[0], sums_b[1], sums_a[1], sums_a[0]])
    bit = 1
    while bit < lax.axis_size("dp"):
        small = small + exchange(small, bit)
        bit *= 2
    bias_parts, small = small[:bias_size].reshape(4, -1), small[bias_size:]
    own_sums = bias_parts[0] + sum(exchange(bias_parts[k], 0, k) for k in (1, 2, 3))
    for k in (1, 2):
        small = small + exchange(small, 0, k)
    bias_sums = own_sums[:heads_cols].reshape(heads_here, triple)
    sum_heads_bias = jnp.concatenate([bias_sums[:, :head_size], bias_sums[:, 2 * head_size:]], axis=1)
    sum_up_bias = own_sums[heads_cols:]
    (sum_token, sum_gain1, sum_shift1, sum_proj_bias, sum_scale1, sum_gain2, sum_shift2,
     sum_down_bias, sum_scale2) = [small[i * width:(i + 1) * width] for i in range(9)]
    return (
        output,
        grad_inputs,
        sum_token,
        sum_gain1,
        sum_shift1,
        sum_heads,
        sum_heads_bias,
        sum_proj,
        sum_proj_bias,
        sum_scale1,
        sum_gain2,
        sum_shift2,
        sum_up,
        sum_up_bias,
        sum_down,
        sum_down_bias,
        sum_scale2,
    )


def solution(mesh):
    placed = (
        P(("dp", "tp"), None),
        P("dp", None),
        P(("dp", "tp"), None),
        P(),
        P(),
        P(),
        P(None, "tp", None),
        P("tp", None),
        P("tp", None),
        P(),
        P(),
        P(),
        P(),
        P(None, "tp"),
        P("tp"),
        P("tp", None),
        P(),
        P(),
        P(("dp", "tp"), None),
    )
    return jax.shard_map(
        local,
        mesh=mesh,
        in_specs=placed,
        out_specs=(
            P(("dp", "tp"), None),
            P(("dp", "tp"), None),
            P(),
            P(),
            P(),
            P(None, "tp", None),
            P("tp", None),
            P("tp", None),
            P(),
            P(),
            P(),
            P(),
            P(None, "tp"),
            P("tp"),
            P("tp", None),
            P(),
            P(),
        ),
        check_vma=False,
    )
```

```python
import functools

import jax
import jax.numpy as jnp
from jax import lax
from jax.experimental import pallas as pl
from jax.experimental.pallas import tpu as pltpu
from jax.sharding import PartitionSpec as P

EPSILON = 1e-06
FLOOR_SCORE = -1e30
SQRT_HALF = 0.7071067811865476
INV_ROOT_TWO_PI = 0.3989422804014327
LONGEST = 14 * 14 + 1
FIFTH_FROM = 4 * (11 * 11 + 1)
TILE = 128
CORE, X, Y = 1, 2, 4

f32, bf16 = jnp.float32, jnp.bfloat16
NN = (((1,), (0,)), ((), ()))
NT = (((1,), (1,)), ((), ()))
TN = (((0,), (0,)), ((), ()))


def dot(a, b, dims=NN):
    return lax.dot_general(a, b, dims, preferred_element_type=f32)


def layer_norm(values, gain, shift):
    centre = values - jnp.mean(values, axis=-1, keepdims=True)
    inverse = lax.rsqrt(jnp.mean(centre * centre, axis=-1, keepdims=True) + EPSILON)
    scaled = centre * inverse
    return (scaled * gain + shift, scaled, inverse)


def norm_back(grad_normed, scaled, inverse, gain):
    grad_scaled = grad_normed * gain
    first = jnp.mean(grad_scaled, axis=-1, keepdims=True)
    second = jnp.mean(grad_scaled * scaled, axis=-1, keepdims=True)
    return inverse * (grad_scaled - first - scaled * second)


def gelu_parts(inner):
    normal_cdf = 0.5 * (1.0 + lax.erf(inner * SQRT_HALF))
    density = jnp.exp(-0.5 * inner * inner) * INV_ROOT_TWO_PI
    return (inner * normal_cdf, normal_cdf + inner * density)


def head_bias_row(bias, head_size):
    blank = jnp.zeros((bias.shape[0], head_size), f32)
    joined = jnp.concatenate(
        [bias[:, :head_size].astype(f32), blank, bias[:, head_size:].astype(f32)], axis=1
    )
    return joined.reshape(1, -1)


def exchange(value, dp_bits=0, tp_bits=0):
    n_dp, n_tp = lax.axis_size("dp"), lax.axis_size("tp")
    pairs = [
        (d * n_tp + t, (d ^ dp_bits) * n_tp + (t ^ tp_bits)) for d in range(n_dp) for t in range(n_tp)
    ]
    return lax.ppermute(value, ("dp", "tp"), pairs)


def spread(value, first, second):
    held = {0: value}
    for bits in (first, second, CORE):
        held.update({at ^ bits: exchange(item, bits) for at, item in list(held.items())})
    return held


def windows(slots):
    out = []
    for low in range(0, slots, TILE):
        high = min(low + TILE, slots)
        begin = low - LONGEST + 1
        if low >= FIFTH_FROM:
            begin = min(begin, FIFTH_FROM)
        end = high + LONGEST - 1
        if high > FIFTH_FROM:
            end = slots
        begin = max(begin, 0) // 128 * 128
        end = min((end + 127) // 128 * 128, slots)
        out.append((low, high, begin, end))
    return out


def as_row(column):
    rows = column.shape[0]
    shape = (rows, rows)
    here = lax.broadcasted_iota(jnp.int32, shape, 0) == lax.broadcasted_iota(jnp.int32, shape, 1)
    return jnp.sum(jnp.where(here, column, 0.0), axis=0, keepdims=True)


def whole(*shape):
    return pl.BlockSpec(shape, lambda k: (0,) * len(shape))


def each(*shape, at=lambda k: k):
    return pl.BlockSpec((1,) + shape, lambda k: (at(k),) + (0,) * len(shape))


def params(megabytes):
    return pltpu.CompilerParams(vmem_limit_bytes=megabytes << 20)


def cost(flops, moved, exps=0):
    return pl.CostEstimate(flops=int(flops), transcendentals=int(exps), bytes_accessed=int(moved))


def axis_bit(bit):
    return lax.rem(lax.div(lax.axis_index("dp"), bit), 2)


def split_store(bit, value, give_ref, keep_ref):
    rows = value.shape[0] // 2
    mine = axis_bit(bit)
    low, high = value[:rows].astype(bf16), value[rows:].astype(bf16)

    @pl.when(mine == 0)
    def _():
        keep_ref[0] = low
        give_ref[0] = high

    @pl.when(mine == 1)
    def _():
        keep_ref[0] = high
        give_ref[0] = low


def attend_back_kernel(
    grad_ref, proj_ref, packed_ref, mixed_ref, lse_ref, normed_ref, weight_ref, column_ref, row_ref,
    give_ref, keep_ref, give_proj_ref, keep_proj_ref, grad_bias_ref, grad_normed_ref,
    grad_mixed, grad_packed, delta, grad_query,
):
    slots = normed_ref.shape[0]
    triple = weight_ref.shape[2] // 3
    size = triple // 3
    scale = size ** (-0.5)
    tiles = windows(slots)
    for low in range(0, slots, 208):
        grad_mixed[low:low + 208, :] = dot(grad_ref[low:low + 208, :], proj_ref[...], NT).astype(bf16)
    split_store(CORE, dot(mixed_ref[0], grad_ref[...], TN), give_proj_ref, keep_proj_ref)
    for head in range(3):
        base = head * triple
        own = slice(head * size, (head + 1) * size)
        for low, high, _, _ in tiles:
            product = grad_mixed[low:high, own].astype(f32) * mixed_ref[0, low:high, own].astype(f32)
            delta[0:1, low:high] = as_row(jnp.sum(product, axis=1, keepdims=True))
        grad_query[...] = jnp.zeros_like(grad_query)
        for low, high, begin, end in tiles:
            keys = packed_ref[0, low:high, base + size:base + 2 * size]
            values = packed_ref[0, low:high, base + 2 * size:base + 3 * size]
            query = packed_ref[0, begin:end, base:base + size] * jnp.bfloat16(scale)
            grads = grad_mixed[begin:end, own]
            scores = dot(keys, query, NT)
            same = column_ref[low:high, :] == row_ref[:, begin:end]
            shares = jnp.exp(jnp.where(same, scores - lse_ref[0, head:head + 1, begin:end], FLOOR_SCORE))
            grad_shares = dot(values, grads, NT)
            grad_scores = (shares * (grad_shares - delta[0:1, begin:end])).astype(bf16)
            grad_packed[low:high, base + 2 * size:base + 3 * size] = dot(shares.astype(bf16), grads).astype(bf16)
            grad_packed[low:high, base + size:base + 2 * size] = dot(grad_scores, query).astype(bf16)
            grad_query[begin:end, :] += dot(grad_scores, keys, TN)
        grad_packed[:, base:base + size] = (grad_query[...] * scale).astype(bf16)
    split_store(CORE, dot(normed_ref[...], grad_packed[...], TN), give_ref, keep_ref)
    grad_bias_ref[0] = jnp.sum(grad_packed[...].astype(f32), axis=0, keepdims=True)

    first = pl.program_id(0) == 0
    for low in range(0, slots, 208):
        part = dot(grad_packed[low:low + 208, :], weight_ref[0], NT)

        @pl.when(first)
        def _():
            grad_normed_ref[low:low + 208, :] = part

        @pl.when(jnp.logical_not(first))
        def _():
            grad_normed_ref[low:low + 208, :] += part


def attend_back(shards, grad, proj, packed, mixed, lse, normed, weight, column, row):
    _, width, columns = weight.shape
    slots = normed.shape[0]
    mixed_columns = columns // 3
    at = lambda k: jnp.where(k == 0, shards[0], shards[1])
    half, half_proj = width // 2, mixed_columns // 2
    return pl.pallas_call(
        attend_back_kernel,
        grid=(2,),
        in_specs=[
            whole(slots, width), pl.BlockSpec((mixed_columns, width), lambda k: (at(k), 0)),
            each(slots, columns, at=at), each(slots, mixed_columns, at=at),
            each(8, slots, at=at), whole(slots, width), each(width, columns, at=at), whole(slots, 1), whole(1, slots),
        ],
        out_specs=[
            each(half, columns), each(half, columns), each(half_proj, width), each(half_proj, width),
            each(1, columns), whole(slots, width),
        ],
        out_shape=[
            jax.ShapeDtypeStruct((2, half, columns), bf16),
            jax.ShapeDtypeStruct((2, half, columns), bf16),
            jax.ShapeDtypeStruct((2, half_proj, width), bf16),
            jax.ShapeDtypeStruct((2, half_proj, width), bf16),
            jax.ShapeDtypeStruct((2, 1, columns), f32),
            jax.ShapeDtypeStruct((slots, width), f32),
        ],
        scratch_shapes=[
            pltpu.VMEM((slots, mixed_columns), bf16),
            pltpu.VMEM((slots, columns), bf16),
            pltpu.VMEM((8, slots), f32),
            pltpu.VMEM((slots, columns // 9), f32),
        ],
        compiler_params=params(40),
        cost_estimate=cost(2 * 8e9, 2 * 5e6, 2 * 3 * 480000),
        name="attend_back",
    )(grad, proj, packed, mixed, lse, normed, weight, column, row)


def start_of(inputs_ref, column_ref, flag_ref, token_ref, low, high):
    valid = (column_ref[low:high, :] >= 0).astype(f32)
    flagged = (flag_ref[low:high, :] == 1).astype(f32)
    start = valid * (flagged * token_ref[...].astype(f32) + (1.0 - flagged) * inputs_ref[low:high, :].astype(f32))
    return valid, flagged, start


def rows_of(slots, step=104):
    return [(low, min(low + step, slots)) for low in range(0, slots, step)]


def flip(index, bits):
    bit = 1
    while bit <= bits:
        if bits & bit:
            index = index + bit * (1 - 2 * lax.rem(lax.div(index, bit), 2))
        bit *= 2
    return index


class Gather:
    ROUTES = ("z", "x", "y", "fx", "fy", "c0", "c2", "c4", "c6")
    COPIES = 3 * len(ROUTES)

    def __init__(self, shard_ref, full_ref, send_sems, recv_sems):
        self.dp, self.tp = lax.axis_index("dp"), lax.axis_index("tp")
        self.own = lax.rem(self.dp, 8)
        self.shard, self.full = shard_ref, full_ref
        self.sends, self.recvs = send_sems, recv_sems
        self.rows = shard_ref.shape[0] // 8
        self.half = self.rows // 16 * 8

    def piece(self, k, bits, half=None):
        begin, height = flip(self.own, bits) * self.rows, self.rows
        if half == 0:
            height = self.half
        elif half == 1:
            begin, height = begin + self.half, self.rows - self.half
        return self.full.at[k, pl.ds(pl.multiple_of(begin, 8), height), :]

    def copy(self, k, route):
        if route == "z":
            source = self.shard.at[pl.ds(pl.multiple_of(self.own * self.rows, 8), self.rows), :]
            target, to = self.piece(k, 0), (self.dp, flip(self.tp, k))
        else:
            bits, half, link = {
                "x": (0, None, X), "y": (0, None, Y), "fx": (Y, 1, X), "fy": (X, 0, Y),
                "c0": (0, None, CORE), "c2": (X, None, CORE), "c4": (Y, None, CORE), "c6": (X | Y, None, CORE),
            }[route]
            source = target = self.piece(k, bits, half)
            to = (flip(self.dp, link), self.tp)
        n = (k - 1) * len(self.ROUTES) + self.ROUTES.index(route)
        return pltpu.make_async_remote_copy(
            src_ref=source, dst_ref=target, send_sem=self.sends.at[n], recv_sem=self.recvs.at[n],
            device_id=to, device_id_type=pl.DeviceIdType.MESH,
        )

    def start(self, k, *routes):
        for route in routes:
            self.copy(k, route).start()

    def arrived(self, k, *routes):
        for route in routes:
            self.copy(k, route).wait_recv()

    def begin(self, k):
        self.start(k, "z")

    def step1(self, k):
        self.arrived(k, "z")
        self.start(k, "x", "y", "c0")

    def step2(self, k):
        self.arrived(k, "x")
        self.start(k, "fy", "c2")
        self.arrived(k, "y")
        self.start(k, "fx", "c4")

    def step3(self, k):
        self.arrived(k, "fx", "fy")
        self.start(k, "c6")

    def step4(self, k):
        self.arrived(k, "c0", "c2", "c4", "c6")

    def sent(self):
        for k in (1, 2, 3):
            for route in self.ROUTES:
                self.copy(k, route).wait_send()


def meet(peers):
    barrier = pltpu.get_barrier_semaphore()
    for peer in peers:
        pl.semaphore_signal(barrier, inc=1, device_id=peer, device_id_type=pl.DeviceIdType.MESH)
    pl.semaphore_wait(barrier, len(peers))


def gather_attend_kernel(
    inputs_ref, column_ref, row_ref, flag_ref, token_ref, gain_ref, shift_ref, bias_ref,
    heads_ref, up_ref, proj_ref, down_ref,
    normed_ref, packed_ref, mixed_ref, lse_ref, heads_all, up_all, proj_all, down_all,
    weight, bounce_up, bounce_proj, bounce_down, load_sem, own_sems,
    *sems,
):
    slots = inputs_ref.shape[0]
    triple = weight.shape[1] // 3
    size = triple // 3
    scale = size ** (-0.5)
    step = pl.program_id(0)
    shards, fulls = (heads_ref, up_ref, proj_ref, down_ref), (heads_all, up_all, proj_all, down_all)
    heads, up, proj, down = gathers = [Gather(shards[n], fulls[n], sems[2 * n], sems[2 * n + 1]) for n in range(4)]
    bounces = (weight, bounce_up, bounce_proj, bounce_down)
    loads = [pltpu.make_async_copy(shards[n], bounces[n], own_sems.at[n]) for n in range(4)]
    stores = [pltpu.make_async_copy(bounces[n], fulls[n].at[0], own_sems.at[4 + n]) for n in range(4)]

    events = {}

    def on(at, unit, *actions):
        events.setdefault((at, unit), []).extend(actions)

    for k, (a, b, c) in {1: (3, 9, 14), 2: (14, 20, 23), 3: (16, 22, 25)}.items():
        for unit, action in ((a, heads.step1), (b, heads.step2), (c, heads.step3)):
            on(unit // 21, unit % 21, functools.partial(action, k))
    for n, item in enumerate((proj, up, down)):
        on(0, 6 if n < 2 else 16, *[functools.partial(item.begin, k) for k in (1, 2, 3)])
    for item, base in ((proj, 28), (up, 30), (down, 52)):
        for k in (1, 2, 3):
            for n, action in enumerate((item.step1, item.step2, item.step3)):
                unit = min(base + 3 * k + n * 14, 83)
                on(unit // 21, unit % 21, functools.partial(action, k))

    def pump(unit):
        for at in range(4):
            if (at, unit) in events:

                @pl.when(step == at)
                def _():
                    for action in events[(at, unit)]:
                        action()

    @pl.when(step == 0)
    def _():
        dp, tp = heads.dp, heads.tp
        loads[0].start()
        meet([(dp, flip(tp, k)) for k in (1, 2, 3)] + [(flip(dp, bit), tp) for bit in (X, Y, CORE)])
        for k in (1, 2, 3):
            heads.begin(k)
        for load in loads[1:]:
            load.start()
        gain, shift = gain_ref[...].astype(f32), shift_ref[...].astype(f32)
        for low, high in rows_of(slots):
            _, _, start = start_of(inputs_ref, column_ref, flag_ref, token_ref, low, high)
            normed_ref[low:high, :] = layer_norm(start, gain, shift)[0].astype(bf16)
        loads[0].wait()
        stores[0].start()

    for k in (1, 2, 3):

        @pl.when(step == k)
        def _():
            if k == 1:
                stores[0].wait()
            heads.step4(k)
            load = pltpu.make_async_copy(heads_all.at[k], weight, load_sem)
            load.start()
            load.wait()

    for low in range(0, slots, 208):
        packed_ref[0, low:low + 208, :] = (dot(normed_ref[low:low + 208, :], weight[...]) + bias_ref[0]).astype(bf16)
    lse_ref[...] = jnp.zeros_like(lse_ref)
    unit = 0
    for head in range(3):
        base = head * triple
        for low, high, begin, end in windows(slots):
            query = packed_ref[0, low:high, base:base + size] * jnp.bfloat16(scale)
            keys = packed_ref[0, begin:end, base + size:base + 2 * size]
            values = packed_ref[0, begin:end, base + 2 * size:base + 3 * size]
            scores = dot(query, keys, NT)
            same = column_ref[low:high, :] == row_ref[:, begin:end]
            scores = jnp.where(same, scores, FLOOR_SCORE)
            largest = jnp.max(scores, axis=1, keepdims=True)
            raised = jnp.exp(scores - largest)
            total = jnp.sum(raised, axis=1, keepdims=True)
            mixed = dot(raised.astype(bf16), values) * (1.0 / total)
            mixed_ref[0, low:high, head * size:(head + 1) * size] = mixed.astype(bf16)
            lse_ref[0, head:head + 1, low:high] = as_row(largest + jnp.log(total))
            pump(unit)
            unit += 1

    @pl.when(step == 0)
    def _():
        for load, store in zip(loads[1:], stores[1:]):
            load.wait()
            store.start()

    @pl.when(step == 3)
    def _():
        for store in stores[1:]:
            store.wait()
        for item in (proj, up, down):
            for k in (1, 2, 3):
                item.step4(k)
        for item in gathers:
            item.sent()


def gather_attend(inputs, column, row, flag, token, gain, shift, bias, heads, up, proj, down):
    slots, width = inputs.shape
    columns = heads.shape[1]
    vector, anywhere = whole(1, width), pl.BlockSpec(memory_space=pl.ANY)
    sems = [pltpu.SemaphoreType.DMA((Gather.COPIES,))] * 8
    return pl.pallas_call(
        gather_attend_kernel,
        grid=(4,),
        in_specs=[
            whole(slots, width), whole(slots, 1), whole(1, slots), whole(slots, 1), vector, vector, vector,
            each(1, columns), anywhere, anywhere, anywhere, anywhere,
        ],
        out_specs=[
            whole(slots, width), each(slots, columns), each(slots, columns // 3), each(8, slots),
            anywhere, anywhere, anywhere, anywhere,
        ],
        out_shape=[
            jax.ShapeDtypeStruct((slots, width), bf16),
            jax.ShapeDtypeStruct((4, slots, columns), bf16),
            jax.ShapeDtypeStruct((4, slots, columns // 3), bf16),
            jax.ShapeDtypeStruct((4, 8, slots), f32),
        ] + [jax.ShapeDtypeStruct((4,) + item.shape, bf16) for item in (heads, up, proj, down)],
        scratch_shapes=[
            pltpu.VMEM(heads.shape, bf16), pltpu.VMEM(up.shape, bf16), pltpu.VMEM(proj.shape, bf16),
            pltpu.VMEM(down.shape, bf16), pltpu.SemaphoreType.DMA, pltpu.SemaphoreType.DMA((8,)),
        ] + sems,
        compiler_params=pltpu.CompilerParams(vmem_limit_bytes=40 << 20, collective_id=0, has_side_effects=True),
        cost_estimate=cost(16e9, 40e6, 12 * 480000),
        name="gather_attend",
    )(inputs, column, row, flag, token, gain, shift, bias, heads, up, proj, down)


def mlp_kernel(
    inputs_ref, column_ref, flag_ref, token_ref, mixed_ref, proj_ref, proj_bias_ref, attn_scale_ref,
    gain_ref, shift_ref, up_ref, unit_bias_ref, down_ref, down_bias_ref, mlp_scale_ref, grad_out_ref,
    branch1_ref, middle_ref, normed_ref, hidden_ref, slope_ref, output_ref, grad_low_ref, sums_ref,
    mixed, total,
):
    slots = inputs_ref.shape[0]
    part = mixed_ref.shape[2]
    k = pl.program_id(0)

    @pl.when(k == 0)
    def _():
        for n in range(4):
            mixed[:, n * part:(n + 1) * part] = mixed_ref[n]
        proj_bias, attn_scale = proj_bias_ref[...].astype(f32), attn_scale_ref[...].astype(f32)
        gain, shift = gain_ref[...].astype(f32), shift_ref[...].astype(f32)
        for low, high in rows_of(slots, 208):
            _, _, start = start_of(inputs_ref, column_ref, flag_ref, token_ref, low, high)
            branch1 = dot(mixed[low:high, :], proj_ref[...]) + proj_bias
            middle = start + attn_scale * branch1
            branch1_ref[low:high, :] = branch1.astype(bf16)
            middle_ref[low:high, :] = middle
            normed_ref[low:high, :] = layer_norm(middle, gain, shift)[0].astype(bf16)
        total[...] = jnp.zeros_like(total)

    units = up_ref.shape[2]
    for low, high in rows_of(slots, 208):
        for left in range(0, units, 256):
            columns = slice(left, left + 256)
            inner = dot(normed_ref[low:high, :], up_ref[0, :, columns]) + unit_bias_ref[0, :, columns]
            value, slope = gelu_parts(inner)
            hidden_ref[0, low:high, columns] = value.astype(bf16)
            slope_ref[0, low:high, columns] = slope.astype(bf16)
        total[low:high, :] += dot(hidden_ref[0, low:high, :], down_ref[0])

    @pl.when(k == pl.num_programs(0) - 1)
    def _():
        down_bias, mlp_scale = down_bias_ref[...].astype(f32), mlp_scale_ref[...].astype(f32)
        sums_ref[...] = jnp.zeros_like(sums_ref)
        for low, high in rows_of(slots):
            valid = (column_ref[low:high, :] >= 0).astype(f32)
            branch2 = total[low:high, :] + down_bias
            output_ref[low:high, :] = (valid * (middle_ref[low:high, :] + mlp_scale * branch2)).astype(bf16)
            grad_final = valid * grad_out_ref[low:high, :].astype(f32)
            grad_branch2 = mlp_scale * grad_final
            grad_low_ref[low:high, :] = grad_branch2.astype(bf16)
            sums_ref[0:1, :] += jnp.sum(branch2 * grad_final, axis=0, keepdims=True)
            sums_ref[1:2, :] += jnp.sum(grad_branch2, axis=0, keepdims=True)


def mlp(inputs, column, flag, token, mixed, proj, proj_bias, attn_scale, gain, shift, up, unit_bias,
        down, down_bias, mlp_scale, grad_out):
    slots, width = inputs.shape
    count, _, units = up.shape
    vector = whole(1, width)
    tokens = whole(slots, width)
    return pl.pallas_call(
        mlp_kernel,
        grid=(count,),
        in_specs=[
            tokens, whole(slots, 1), whole(slots, 1), vector, whole(*mixed.shape),
            whole(width, width), vector, vector, vector, vector, each(width, units), each(1, units),
            each(units, width), vector, vector, tokens,
        ],
        out_specs=[
            tokens, tokens, tokens, each(slots, units), each(slots, units), tokens, tokens, whole(8, width),
        ],
        out_shape=[
            jax.ShapeDtypeStruct((slots, width), bf16),
            jax.ShapeDtypeStruct((slots, width), f32),
            jax.ShapeDtypeStruct((slots, width), bf16),
            jax.ShapeDtypeStruct((count, slots, units), bf16),
            jax.ShapeDtypeStruct((count, slots, units), bf16),
            jax.ShapeDtypeStruct((slots, width), bf16),
            jax.ShapeDtypeStruct((slots, width), bf16),
            jax.ShapeDtypeStruct((8, width), f32),
        ],
        scratch_shapes=[pltpu.VMEM((slots, width), bf16), pltpu.VMEM((slots, width), f32)],
        compiler_params=params(48),
        cost_estimate=cost(9e9, 30e6, 5e6),
        name="mlp",
    )(inputs, column, flag, token, mixed, proj, proj_bias, attn_scale, gain, shift, up, unit_bias,
      down, down_bias, mlp_scale, grad_out)


def down_back_kernel(hidden_ref, grad_low_ref, give_ref, keep_ref):
    split_store(CORE, dot(hidden_ref[0], grad_low_ref[...], TN), give_ref, keep_ref)


def down_back(hidden, grad_low):
    count, slots, units = hidden.shape
    width = grad_low.shape[1]
    out = jax.ShapeDtypeStruct((count, units // 2, width), bf16)
    return pl.pallas_call(
        down_back_kernel,
        grid=(count,),
        in_specs=[each(slots, units), whole(slots, width)],
        out_specs=[each(units // 2, width), each(units // 2, width)],
        out_shape=[out, out],
        compiler_params=params(24),
        cost_estimate=cost(4e9, 12e6),
        name="down_back",
    )(hidden, grad_low)


def mlp_back_kernel(
    grad_low_ref, slope_ref, down_ref, up_ref, normed_ref, middle_ref, branch1_ref, grad_out_ref, column_ref,
    gain_ref, shift_ref, attn_scale_ref, mlp_scale_ref,
    give_ref, keep_ref, unit_bias_ref, grad_middle_ref, grad_low1_ref, sums_ref,
    grad_unit, total, flipped,
):
    slots, width = normed_ref.shape
    k = pl.program_id(0)

    @pl.when(k == 0)
    def _():
        total[...] = jnp.zeros_like(total)
        flipped[...] = normed_ref[...].T

    unit_sum = jnp.zeros((1, slope_ref.shape[2]), f32)
    for low, high in rows_of(slots, 208):
        unit = (dot(grad_low_ref[low:high, :], down_ref[0], NT) * slope_ref[0, low:high, :].astype(f32)).astype(bf16)
        grad_unit[low:high, :] = unit
        unit_sum += jnp.sum(unit.astype(f32), axis=0, keepdims=True)
        total[low:high, :] += dot(unit, up_ref[0], NT)
    unit_bias_ref[0] = unit_sum
    split_store(CORE, dot(flipped[...], grad_unit[...]), give_ref, keep_ref)

    @pl.when(k == pl.num_programs(0) - 1)
    def _():
        gain, attn_scale = gain_ref[...].astype(f32), attn_scale_ref[...].astype(f32)
        sums_ref[...] = jnp.zeros_like(sums_ref)
        for low, high in rows_of(slots):
            valid = (column_ref[low:high, :] >= 0).astype(f32)
            grad_final = valid * grad_out_ref[low:high, :].astype(f32)
            grad_normed = total[low:high, :]
            _, scaled, inverse = layer_norm(middle_ref[low:high, :], gain, gain)
            grad_middle = grad_final + norm_back(grad_normed, scaled, inverse, gain)
            grad_branch1 = attn_scale * grad_middle
            grad_middle_ref[low:high, :] = grad_middle
            grad_low1_ref[low:high, :] = grad_branch1.astype(bf16)
            sums_ref[0:1, :] += jnp.sum(grad_normed * scaled, axis=0, keepdims=True)
            sums_ref[1:2, :] += jnp.sum(grad_normed, axis=0, keepdims=True)
            sums_ref[2:3, :] += jnp.sum(branch1_ref[low:high, :].astype(f32) * grad_middle, axis=0, keepdims=True)
            sums_ref[3:4, :] += jnp.sum(grad_branch1, axis=0, keepdims=True)


def mlp_back(grad_low, slope, down, up, normed, middle, branch1, grad_out, column, gain, shift, attn_scale, mlp_scale):
    slots, width = normed.shape
    count, _, units = up.shape
    vector, tokens = whole(1, width), whole(slots, width)
    out = jax.ShapeDtypeStruct((count, width // 2, units), bf16)
    return pl.pallas_call(
        mlp_back_kernel,
        grid=(count,),
        in_specs=[
            tokens, each(slots, units), each(units, width), each(width, units), tokens, tokens, tokens, tokens,
            whole(slots, 1), vector, vector, vector, vector,
        ],
        out_specs=[
            each(width // 2, units), each(width // 2, units), each(1, units), tokens, tokens, whole(8, width),
        ],
        out_shape=[
            out, out,
            jax.ShapeDtypeStruct((count, 1, units), f32),
            jax.ShapeDtypeStruct((slots, width), f32),
            jax.ShapeDtypeStruct((slots, width), bf16),
            jax.ShapeDtypeStruct((8, width), f32),
        ],
        scratch_shapes=[pltpu.VMEM((slots, units), bf16), pltpu.VMEM((slots, width), f32), pltpu.VMEM((width, slots), bf16)],
        compiler_params=params(48),
        cost_estimate=cost(12e9, 30e6),
        name="mlp_back",
    )(grad_low, slope, down, up, normed, middle, branch1, grad_out, column, gain, shift, attn_scale, mlp_scale)


def last_kernel(
    inputs_ref, column_ref, flag_ref, token_ref, gain_ref, grad_a_ref, grad_b_ref, grad_middle_ref, out_ref, sums_ref
):
    gain = gain_ref[...].astype(f32)
    sums_ref[...] = jnp.zeros_like(sums_ref)
    for low, high in rows_of(inputs_ref.shape[0]):
        valid, flagged, start = start_of(inputs_ref, column_ref, flag_ref, token_ref, low, high)
        _, scaled, inverse = layer_norm(start, gain, gain)
        grad_normed = grad_a_ref[low:high, :] + grad_b_ref[low:high, :]
        grad_start = grad_middle_ref[low:high, :] + norm_back(grad_normed, scaled, inverse, gain)
        out_ref[low:high, :] = valid * (1.0 - flagged) * grad_start
        sums_ref[0:1, :] += jnp.sum(valid * flagged * grad_start, axis=0, keepdims=True)
        sums_ref[1:2, :] += jnp.sum(grad_normed * scaled, axis=0, keepdims=True)
        sums_ref[2:3, :] += jnp.sum(grad_normed, axis=0, keepdims=True)


def last(inputs, column, flag, token, gain, grad_a, grad_b, grad_middle):
    slots, width = inputs.shape
    return pl.pallas_call(
        last_kernel,
        out_shape=[jax.ShapeDtypeStruct((slots, width), f32), jax.ShapeDtypeStruct((8, width), f32)],
        compiler_params=params(24),
        cost_estimate=cost(2e7, 12e6),
        name="last",
    )(inputs, column, flag, token, gain, grad_a, grad_b, grad_middle)


def others(value):
    return [exchange(value, 0, k) for k in (1, 2, 3)]


def join_kernel(order, *refs):
    pieces, out = refs[:8], refs[8]
    mine = lax.axis_index("dp")
    rows = pieces[0].shape[0]
    for at in range(8):
        owner = jnp.bitwise_xor(mine, at)
        spot = 0
        for bit in order:
            spot = spot * 2 + lax.rem(lax.div(owner, bit), 2)
        out[pl.ds(pl.multiple_of(spot * rows, 8), rows), :] = pieces[at][...].astype(f32)


def join(held, order):
    rows, columns = held[0].shape
    return pl.pallas_call(
        functools.partial(join_kernel, order),
        out_shape=jax.ShapeDtypeStruct((8 * rows, columns), f32),
        in_specs=[pl.BlockSpec(memory_space=pltpu.VMEM)] * 8,
        out_specs=pl.BlockSpec(memory_space=pltpu.VMEM),
        compiler_params=params(12),
        cost_estimate=cost(0, 8 * rows * columns * 6),
        name="join",
    )(*[held[at] for at in range(8)])


def stage_kernel(bit, count, *refs):
    mine = axis_bit(bit)
    for n in range(count):
        kept, got, give, keep = (refs[part * count + n] for part in range(4))
        rows = kept.shape[1] // 2
        for own in (0, 1):

            @pl.when(mine == own)
            def _():
                for out, index in ((keep, own), (give, 1 - own)):
                    part = slice(index * rows, (index + 1) * rows)
                    out[...] = (kept[:, part, :].astype(f32) + got[:, part, :].astype(f32)).astype(bf16)


def stage(bit, kept, got):
    out = [jax.ShapeDtypeStruct((item.shape[0], item.shape[1] // 2, item.shape[2]), bf16) for item in kept]
    result = pl.pallas_call(
        functools.partial(stage_kernel, bit, len(kept)),
        out_shape=out + out,
        compiler_params=params(20),
        cost_estimate=cost(0, 6 * sum(item.size for item in kept)),
        name="stage",
    )(*kept, *got)
    return result[:len(kept)], result[len(kept):]


def add(a, b):
    return (a.astype(f32) + b.astype(f32)).astype(bf16)


def swap(items, bit):
    return [exchange(item, bit) for item in items]


def upper(total):
    bit = 8
    while bit < lax.axis_size("dp"):
        total = add(total, exchange(total, bit))
        bit *= 2
    return total


def after(items, *needs):
    return lax.optimization_barrier((items, needs))[0]


def local(
    inputs,
    segment_ids,
    mask_flags,
    mask_token,
    norm_gain,
    norm_shift,
    heads_weight,
    heads_bias,
    proj_weight,
    proj_bias,
    attn_scale,
    mlp_gain,
    mlp_shift,
    up_weight,
    up_bias,
    down_weight,
    down_bias,
    mlp_scale,
    grad_out,
):
    slots = mask_flags.shape[1]
    own_rows = mask_flags.shape[0]
    width = inputs.shape[1]
    triple = heads_weight.shape[2]
    head_size = triple // 3
    heads_here = heads_weight.shape[1]
    own_ids = lax.dynamic_slice_in_dim(segment_ids, lax.axis_index("tp") * own_rows, own_rows, 0)
    column, row = own_ids.reshape(-1, 1), own_ids.reshape(1, -1)
    flag = mask_flags.reshape(-1, 1)
    vector = lambda v: v.reshape(1, -1)
    token, gain1, gain2 = vector(mask_token), vector(norm_gain), vector(mlp_gain)
    own_heads = heads_weight.reshape(width, -1)
    heads_cols = own_heads.shape[1]

    own_bias = jnp.concatenate([head_bias_row(heads_bias, head_size), up_bias.astype(f32).reshape(1, -1)], axis=1)
    bias = jnp.stack([own_bias] + others(own_bias))
    head_bias, unit_bias = bias[:, :, :heads_cols], bias[:, :, heads_cols:]

    normed1, packed, mixed, lse, heads_all, up_all, proj_all, down_all = gather_attend(
        inputs, column, row, flag, token, gain1, vector(norm_shift), head_bias, own_heads, up_weight, proj_weight,
        down_weight,
    )
    proj_flat = proj_all.reshape(-1, width)
    branch1, middle, normed2, hidden, slope, output, grad_low2, sums_a = mlp(
        inputs, column, flag, token, mixed, proj_flat, vector(proj_bias), vector(attn_scale), gain2,
        vector(mlp_shift), up_all, unit_bias, down_all, vector(down_bias), vector(mlp_scale), grad_out,
    )
    d_give, d_keep = down_back(hidden, grad_low2)
    d_got = exchange(d_give, CORE)
    u_give, u_keep, unit_sums, grad_middle, grad_low1, sums_b = mlp_back(
        grad_low2, slope, down_all, up_all, normed2, middle, branch1, grad_out, column, gain2, vector(mlp_shift),
        vector(attn_scale), vector(mlp_scale),
    )
    u_got = exchange(u_give, CORE)
    (d_give,), (d_keep,) = stage(X, [d_keep], [d_got])
    d_got = exchange(d_give, X)
    (u_give,), (u_keep,) = stage(Y, [u_keep], [u_got])
    u_got = exchange(u_give, Y)
    grad_low1 = after(grad_low1, d_give, u_give)
    h_give, h_keep, p_give, p_keep, head_sums_a, grad_normed_a = attend_back(
        (1, 2), grad_low1, proj_flat, packed, mixed, lse, normed1, heads_all, column, row
    )
    (d_give,), (d_keep,) = stage(Y, [d_keep], [d_got])
    d_got = exchange(d_give, Y)
    (u_give,), (u_keep,) = stage(X, [u_keep], [u_got])
    u_got = exchange(u_give, X)
    h_got, p_got = swap([h_give, p_give], CORE)
    grad_low1 = after(grad_low1, d_give, u_give, h_give)
    g_give, g_keep, q_give, q_keep, head_sums_b, grad_normed_b = attend_back(
        (3, 0), grad_low1, proj_flat, packed, mixed, lse, normed1, heads_all, column, row
    )
    g_got, q_got = swap([g_give, q_give], CORE)
    (h_give, p_give), (h_keep, p_keep) = stage(X, [h_keep, p_keep], [h_got, p_got])
    h_got, p_got = swap([h_give, p_give], X)
    d_total, u_total = upper(add(d_keep, d_got)), upper(add(u_keep, u_got))
    d_parts = [d_total[0]] + [exchange(d_total[k], 0, k) for k in (1, 2, 3)]
    u_parts = [u_total[0]] + [exchange(u_total[k], 0, k) for k in (1, 2, 3)]
    (g_give, q_give), (g_keep, q_keep) = stage(X, [g_keep, q_keep], [g_got, q_got])
    g_got, q_got = swap([g_give, q_give], X)
    grad_inputs, sums_c = last(inputs, column, flag, token, gain1, grad_normed_a, grad_normed_b, grad_middle)
    (h_give, p_give), (h_keep, p_keep) = stage(Y, [h_keep, p_keep], [h_got, p_got])
    h_got, p_got = swap([h_give, p_give], Y)
    (g_give, q_give), (g_keep, q_keep) = stage(Y, [g_keep, q_keep], [g_got, q_got])
    g_got, q_got = swap([g_give, q_give], Y)
    h_total, p_total = upper(add(h_keep, h_got)), upper(add(p_keep, p_got))
    g_total, q_total = upper(add(g_keep, g_got)), upper(add(q_keep, q_got))
    h_parts = [g_total[1], exchange(h_total[0], 0, 1), exchange(h_total[1], 0, 2), exchange(g_total[0], 0, 3)]
    p_parts = [q_total[1], exchange(p_total[0], 0, 1), exchange(p_total[1], 0, 2), exchange(q_total[0], 0, 3)]

    def finish(parts, first, second):
        mine = sum(part.astype(f32) for part in parts).astype(bf16)
        return join(spread(mine, second, first), (CORE, first, second))

    sum_down = finish(d_parts, X, Y)
    sum_up = finish(u_parts, Y, X)
    sum_heads, sum_proj = finish(h_parts, X, Y), finish(p_parts, X, Y)
    sum_heads = sum_heads.reshape(heads_weight.shape)

    head_sums = jnp.concatenate([head_sums_b[1], head_sums_a[0], head_sums_a[1], head_sums_b[0]], axis=0)
    bias_parts = jnp.concatenate([head_sums, unit_sums[:, 0, :]], axis=1)
    bias_size = bias_parts.size
    small = jnp.concatenate([
        bias_parts.reshape(-1), sums_c[:3].reshape(-1), sums_b[3], sums_b[2], sums_b[0], sums_b[1], sums_a[1], sums_a[0]])
    bit = 1
    while bit < lax.axis_size("dp"):
        small = small + exchange(small, bit)
        bit *= 2
    bias_parts, small = small[:bias_size].reshape(4, -1), small[bias_size:]
    own_sums = bias_parts[0] + sum(exchange(bias_parts[k], 0, k) for k in (1, 2, 3))
    for k in (1, 2):
        small = small + exchange(small, 0, k)
    bias_sums = own_sums[:heads_cols].reshape(heads_here, triple)
    sum_heads_bias = jnp.concatenate([bias_sums[:, :head_size], bias_sums[:, 2 * head_size:]], axis=1)
    sum_up_bias = own_sums[heads_cols:]
    (sum_token, sum_gain1, sum_shift1, sum_proj_bias, sum_scale1, sum_gain2, sum_shift2,
     sum_down_bias, sum_scale2) = [small[i * width:(i + 1) * width] for i in range(9)]
    return (
        output,
        grad_inputs,
        sum_token,
        sum_gain1,
        sum_shift1,
        sum_heads,
        sum_heads_bias,
        sum_proj,
        sum_proj_bias,
        sum_scale1,
        sum_gain2,
        sum_shift2,
        sum_up,
        sum_up_bias,
        sum_down,
        sum_down_bias,
        sum_scale2,
    )


def solution(mesh):
    placed = (
        P(("dp", "tp"), None),
        P("dp", None),
        P(("dp", "tp"), None),
        P(),
        P(),
        P(),
        P(None, "tp", None),
        P("tp", None),
        P("tp", None),
        P(),
        P(),
        P(),
        P(),
        P(None, "tp"),
        P("tp"),
        P("tp", None),
        P(),
        P(),
        P(("dp", "tp"), None),
    )
    return jax.shard_map(
        local,
        mesh=mesh,
        in_specs=placed,
        out_specs=(
            P(("dp", "tp"), None),
            P(("dp", "tp"), None),
            P(),
            P(),
            P(),
            P(None, "tp", None),
            P("tp", None),
            P("tp", None),
            P(),
            P(),
            P(),
            P(),
            P(None, "tp"),
            P("tp"),
            P("tp", None),
            P(),
            P(),
        ),
        check_vma=False,
    )
```

```python
import functools

import jax
import jax.numpy as jnp
from jax import lax
from jax.experimental import pallas as pl
from jax.experimental.pallas import tpu as pltpu
from jax.sharding import PartitionSpec as P

EPSILON = 1e-06
FLOOR_SCORE = -1e30
SQRT_HALF = 0.7071067811865476
INV_ROOT_TWO_PI = 0.3989422804014327
LONGEST = 14 * 14 + 1
FIFTH_FROM = 4 * (11 * 11 + 1)
TILE = 128
CORE, X, Y = 1, 2, 4

f32, bf16 = jnp.float32, jnp.bfloat16
NN = (((1,), (0,)), ((), ()))
NT = (((1,), (1,)), ((), ()))
TN = (((0,), (0,)), ((), ()))


def dot(a, b, dims=NN):
    return lax.dot_general(a, b, dims, preferred_element_type=f32)


def layer_norm(values, gain, shift):
    centre = values - jnp.mean(values, axis=-1, keepdims=True)
    inverse = lax.rsqrt(jnp.mean(centre * centre, axis=-1, keepdims=True) + EPSILON)
    scaled = centre * inverse
    return (scaled * gain + shift, scaled, inverse)


def norm_back(grad_normed, scaled, inverse, gain):
    grad_scaled = grad_normed * gain
    first = jnp.mean(grad_scaled, axis=-1, keepdims=True)
    second = jnp.mean(grad_scaled * scaled, axis=-1, keepdims=True)
    return inverse * (grad_scaled - first - scaled * second)


def gelu_parts(inner):
    normal_cdf = 0.5 * (1.0 + lax.erf(inner * SQRT_HALF))
    density = jnp.exp(-0.5 * inner * inner) * INV_ROOT_TWO_PI
    return (inner * normal_cdf, normal_cdf + inner * density)


def head_bias_row(bias, head_size):
    blank = jnp.zeros((bias.shape[0], head_size), f32)
    joined = jnp.concatenate(
        [bias[:, :head_size].astype(f32), blank, bias[:, head_size:].astype(f32)], axis=1
    )
    return joined.reshape(1, -1)


def exchange(value, dp_bits=0, tp_bits=0):
    n_dp, n_tp = lax.axis_size("dp"), lax.axis_size("tp")
    pairs = [
        (d * n_tp + t, (d ^ dp_bits) * n_tp + (t ^ tp_bits)) for d in range(n_dp) for t in range(n_tp)
    ]
    return lax.ppermute(value, ("dp", "tp"), pairs)


def windows(slots):
    out = []
    for low in range(0, slots, TILE):
        high = min(low + TILE, slots)
        begin = low - LONGEST + 1
        if low >= FIFTH_FROM:
            begin = min(begin, FIFTH_FROM)
        end = high + LONGEST - 1
        if high > FIFTH_FROM:
            end = slots
        begin = max(begin, 0) // 128 * 128
        end = min((end + 127) // 128 * 128, slots)
        out.append((low, high, begin, end))
    return out


def as_row(column):
    rows = column.shape[0]
    shape = (rows, rows)
    here = lax.broadcasted_iota(jnp.int32, shape, 0) == lax.broadcasted_iota(jnp.int32, shape, 1)
    return jnp.sum(jnp.where(here, column, 0.0), axis=0, keepdims=True)


def whole(*shape):
    return pl.BlockSpec(shape, lambda k: (0,) * len(shape))


def each(*shape, at=lambda k: k):
    return pl.BlockSpec((1,) + shape, lambda k: (at(k),) + (0,) * len(shape))


def params(megabytes):
    return pltpu.CompilerParams(vmem_limit_bytes=megabytes << 20)


def cost(flops, moved, exps=0):
    return pl.CostEstimate(flops=int(flops), transcendentals=int(exps), bytes_accessed=int(moved))


def start_of(inputs_ref, column_ref, flag_ref, token_ref, here):
    valid = (column_ref[here, :] >= 0).astype(f32)
    flagged = (flag_ref[here, :] == 1).astype(f32)
    start = valid * (flagged * token_ref[...].astype(f32) + (1.0 - flagged) * inputs_ref[here, :].astype(f32))
    return valid, flagged, start


def rows_of(slots, step=104):
    return [(low, min(low + step, slots)) for low in range(0, slots, step)]


def flip(index, bits):
    bit = 1
    while bit <= bits:
        if bits & bit:
            index = index + bit * (1 - 2 * lax.rem(lax.div(index, bit), 2))
        bit *= 2
    return index


class Gather:
    ROUTES = ("z", "x", "y", "fx", "fy", "c0", "c2", "c4", "c6")
    COPIES = 3 * len(ROUTES)

    def __init__(self, shard_ref, full_ref, send_sems, recv_sems):
        self.dp, self.tp = lax.axis_index("dp"), lax.axis_index("tp")
        self.own = lax.rem(self.dp, 8)
        self.shard, self.full = shard_ref, full_ref
        self.sends, self.recvs = send_sems, recv_sems
        self.rows = shard_ref.shape[0] // 8
        self.half = self.rows // 16 * 8

    def piece(self, k, bits, half=None):
        begin, height = flip(self.own, bits) * self.rows, self.rows
        if half == 0:
            height = self.half
        elif half == 1:
            begin, height = begin + self.half, self.rows - self.half
        return self.full.at[k, pl.ds(pl.multiple_of(begin, 8), height), :]

    def copy(self, k, route):
        if route == "z":
            source = self.shard.at[pl.ds(pl.multiple_of(self.own * self.rows, 8), self.rows), :]
            target, to = self.piece(k, 0), (self.dp, flip(self.tp, k))
        else:
            bits, half, link = {
                "x": (0, None, X), "y": (0, None, Y), "fx": (Y, 1, X), "fy": (X, 0, Y),
                "c0": (0, None, CORE), "c2": (X, None, CORE), "c4": (Y, None, CORE), "c6": (X | Y, None, CORE),
            }[route]
            source = target = self.piece(k, bits, half)
            to = (flip(self.dp, link), self.tp)
        n = (k - 1) * len(self.ROUTES) + self.ROUTES.index(route)
        return pltpu.make_async_remote_copy(
            src_ref=source, dst_ref=target, send_sem=self.sends.at[n], recv_sem=self.recvs.at[n],
            device_id=to, device_id_type=pl.DeviceIdType.MESH,
        )

    def start(self, k, *routes):
        for route in routes:
            self.copy(k, route).start()

    def arrived(self, k, *routes):
        for route in routes:
            self.copy(k, route).wait_recv()

    def begin(self, k):
        self.start(k, "z")

    def step1(self, k):
        self.arrived(k, "z")
        self.start(k, "x", "y", "c0")

    def step2(self, k):
        self.arrived(k, "x")
        self.start(k, "fy", "c2")
        self.arrived(k, "y")
        self.start(k, "fx", "c4")

    def step3(self, k):
        self.arrived(k, "fx", "fy")
        self.start(k, "c6")

    def step4(self, k):
        self.arrived(k, "c0", "c2", "c4", "c6")

    def sent(self):
        for k in (1, 2, 3):
            for route in self.ROUTES:
                self.copy(k, route).wait_send()


def meet(peers):
    barrier = pltpu.get_barrier_semaphore()
    for peer in peers:
        pl.semaphore_signal(barrier, inc=1, device_id=peer, device_id_type=pl.DeviceIdType.MESH)
    pl.semaphore_wait(barrier, len(peers))


def gather_attend_kernel(
    inputs_ref, column_ref, row_ref, flag_ref, token_ref, gain_ref, shift_ref, bias_ref,
    heads_ref, up_ref, proj_ref, down_ref,
    normed_ref, packed_ref, mixed_ref, lse_ref, heads_all, up_all, proj_all, down_all,
    weight, bounce_up, bounce_proj, bounce_down, load_sem, own_sems,
    *sems,
):
    slots = inputs_ref.shape[0]
    triple = weight.shape[1] // 3
    size = triple // 3
    scale = size ** (-0.5)
    step = pl.program_id(0)
    shards, fulls = (heads_ref, up_ref, proj_ref, down_ref), (heads_all, up_all, proj_all, down_all)
    heads, up, proj, down = gathers = [Gather(shards[n], fulls[n], sems[2 * n], sems[2 * n + 1]) for n in range(4)]
    bounces = (weight, bounce_up, bounce_proj, bounce_down)
    loads = [pltpu.make_async_copy(shards[n], bounces[n], own_sems.at[n]) for n in range(4)]
    stores = [pltpu.make_async_copy(bounces[n], fulls[n].at[0], own_sems.at[4 + n]) for n in range(4)]

    events = {}

    def on(at, unit, *actions):
        events.setdefault((at, unit), []).extend(actions)

    for k, (a, b, c) in {1: (3, 9, 14), 2: (14, 20, 23), 3: (16, 22, 25)}.items():
        for unit, action in ((a, heads.step1), (b, heads.step2), (c, heads.step3)):
            on(unit // 21, unit % 21, functools.partial(action, k))
    for n, item in enumerate((proj, up, down)):
        on(0, 6 if n < 2 else 16, *[functools.partial(item.begin, k) for k in (1, 2, 3)])
    for item, base in ((proj, 28), (up, 30), (down, 52)):
        for k in (1, 2, 3):
            for n, action in enumerate((item.step1, item.step2, item.step3)):
                unit = min(base + 3 * k + n * 14, 83)
                on(unit // 21, unit % 21, functools.partial(action, k))

    def pump(unit):
        for at in range(4):
            if (at, unit) in events:

                @pl.when(step == at)
                def _():
                    for action in events[(at, unit)]:
                        action()

    @pl.when(step == 0)
    def _():
        dp, tp = heads.dp, heads.tp
        loads[0].start()
        meet([(dp, flip(tp, k)) for k in (1, 2, 3)] + [(flip(dp, bit), tp) for bit in (X, Y, CORE)])
        for k in (1, 2, 3):
            heads.begin(k)
        for load in loads[1:]:
            load.start()
        gain, shift = gain_ref[...].astype(f32), shift_ref[...].astype(f32)
        for low, high in rows_of(slots):
            _, _, start = start_of(inputs_ref, column_ref, flag_ref, token_ref, slice(low, high))
            normed_ref[low:high, :] = layer_norm(start, gain, shift)[0].astype(bf16)
        loads[0].wait()
        stores[0].start()

    for k in (1, 2, 3):

        @pl.when(step == k)
        def _():
            if k == 1:
                stores[0].wait()
            heads.step4(k)
            load = pltpu.make_async_copy(heads_all.at[k], weight, load_sem)
            load.start()
            load.wait()

    for low in range(0, slots, 208):
        packed_ref[0, low:low + 208, :] = (dot(normed_ref[low:low + 208, :], weight[...]) + bias_ref[0]).astype(bf16)
    lse_ref[...] = jnp.zeros_like(lse_ref)
    unit = 0
    for head in range(3):
        base = head * triple
        for low, high, begin, end in windows(slots):
            query = packed_ref[0, low:high, base:base + size] * jnp.bfloat16(scale)
            keys = packed_ref[0, begin:end, base + size:base + 2 * size]
            values = packed_ref[0, begin:end, base + 2 * size:base + 3 * size]
            scores = dot(query, keys, NT)
            same = column_ref[low:high, :] == row_ref[:, begin:end]
            scores = jnp.where(same, scores, FLOOR_SCORE)
            largest = jnp.max(scores, axis=1, keepdims=True)
            raised = jnp.exp(scores - largest)
            total = jnp.sum(raised, axis=1, keepdims=True)
            mixed = dot(raised.astype(bf16), values) * (1.0 / total)
            mixed_ref[0, low:high, head * size:(head + 1) * size] = mixed.astype(bf16)
            lse_ref[0, head:head + 1, low:high] = as_row(largest + jnp.log(total))
            pump(unit)
            unit += 1

    @pl.when(step == 0)
    def _():
        for load, store in zip(loads[1:], stores[1:]):
            load.wait()
            store.start()

    @pl.when(step == 3)
    def _():
        for store in stores[1:]:
            store.wait()
        for item in (proj, up, down):
            for k in (1, 2, 3):
                item.step4(k)
        for item in gathers:
            item.sent()


def gather_attend(inputs, column, row, flag, token, gain, shift, bias, heads, up, proj, down):
    slots, width = inputs.shape
    columns = heads.shape[1]
    vector, anywhere = whole(1, width), pl.BlockSpec(memory_space=pl.ANY)
    sems = [pltpu.SemaphoreType.DMA((Gather.COPIES,))] * 8
    return pl.pallas_call(
        gather_attend_kernel,
        grid=(4,),
        in_specs=[
            whole(slots, width), whole(slots, 1), whole(1, slots), whole(slots, 1), vector, vector, vector,
            each(1, columns), anywhere, anywhere, anywhere, anywhere,
        ],
        out_specs=[
            whole(slots, width), each(slots, columns), each(slots, columns // 3), each(8, slots),
            anywhere, anywhere, anywhere, anywhere,
        ],
        out_shape=[
            jax.ShapeDtypeStruct((slots, width), bf16),
            jax.ShapeDtypeStruct((4, slots, columns), bf16),
            jax.ShapeDtypeStruct((4, slots, columns // 3), bf16),
            jax.ShapeDtypeStruct((4, 8, slots), f32),
        ] + [jax.ShapeDtypeStruct((4,) + item.shape, bf16) for item in (heads, up, proj, down)],
        scratch_shapes=[
            pltpu.VMEM(heads.shape, bf16), pltpu.VMEM(up.shape, bf16), pltpu.VMEM(proj.shape, bf16),
            pltpu.VMEM(down.shape, bf16), pltpu.SemaphoreType.DMA, pltpu.SemaphoreType.DMA((8,)),
        ] + sems,
        compiler_params=pltpu.CompilerParams(vmem_limit_bytes=40 << 20, collective_id=0, has_side_effects=True),
        cost_estimate=cost(16e9, 40e6, 12 * 480000),
        name="gather_attend",
    )(inputs, column, row, flag, token, gain, shift, bias, heads, up, proj, down)


def mlp_kernel(
    inputs_ref, column_ref, flag_ref, token_ref, mixed_ref, proj_ref, proj_bias_ref, attn_scale_ref,
    gain_ref, shift_ref, up_ref, unit_bias_ref, down_ref, down_bias_ref, mlp_scale_ref, grad_out_ref,
    middle_ref, normed_ref, hidden_ref, slope_ref, output_ref, grad_low_ref, sums_ref,
    mixed, total,
):
    slots = inputs_ref.shape[0]
    part = mixed_ref.shape[2]
    k = pl.program_id(0)

    @pl.when(k == 0)
    def _():
        for n in range(4):
            mixed[:, n * part:(n + 1) * part] = mixed_ref[n]
        proj_bias, attn_scale = proj_bias_ref[...].astype(f32), attn_scale_ref[...].astype(f32)
        gain, shift = gain_ref[...].astype(f32), shift_ref[...].astype(f32)
        for low, high in rows_of(slots, 208):
            _, _, start = start_of(inputs_ref, column_ref, flag_ref, token_ref, slice(low, high))
            branch1 = dot(mixed[low:high, :], proj_ref[...]) + proj_bias
            middle = start + attn_scale * branch1
            middle_ref[low:high, :] = middle
            normed_ref[low:high, :] = layer_norm(middle, gain, shift)[0].astype(bf16)
        total[...] = jnp.zeros_like(total)

    units = up_ref.shape[2]
    for low, high in rows_of(slots, 208):
        for left in range(0, units, 256):
            columns = slice(left, left + 256)
            inner = dot(normed_ref[low:high, :], up_ref[0, :, columns]) + unit_bias_ref[0, :, columns]
            value, slope = gelu_parts(inner)
            hidden_ref[0, low:high, columns] = value.astype(bf16)
            slope_ref[0, low:high, columns] = slope.astype(bf16)
        total[low:high, :] += dot(hidden_ref[0, low:high, :], down_ref[0])

    @pl.when(k == pl.num_programs(0) - 1)
    def _():
        down_bias, mlp_scale = down_bias_ref[...].astype(f32), mlp_scale_ref[...].astype(f32)
        sums_ref[...] = jnp.zeros_like(sums_ref)
        for low, high in rows_of(slots):
            valid = (column_ref[low:high, :] >= 0).astype(f32)
            branch2 = total[low:high, :] + down_bias
            output_ref[low:high, :] = (valid * (middle_ref[low:high, :] + mlp_scale * branch2)).astype(bf16)
            grad_final = valid * grad_out_ref[low:high, :].astype(f32)
            grad_branch2 = mlp_scale * grad_final
            grad_low_ref[low:high, :] = grad_branch2.astype(bf16)
            sums_ref[0:1, :] += jnp.sum(branch2 * grad_final, axis=0, keepdims=True)
            sums_ref[1:2, :] += jnp.sum(grad_branch2, axis=0, keepdims=True)


def mlp(inputs, column, flag, token, mixed, proj, proj_bias, attn_scale, gain, shift, up, unit_bias,
        down, down_bias, mlp_scale, grad_out):
    slots, width = inputs.shape
    count, _, units = up.shape
    vector = whole(1, width)
    tokens = whole(slots, width)
    return pl.pallas_call(
        mlp_kernel,
        grid=(count,),
        in_specs=[
            tokens, whole(slots, 1), whole(slots, 1), vector, whole(*mixed.shape),
            whole(width, width), vector, vector, vector, vector, each(width, units), each(1, units),
            each(units, width), vector, vector, tokens,
        ],
        out_specs=[
            tokens, tokens, each(slots, units), each(slots, units), tokens, tokens, whole(8, width),
        ],
        out_shape=[
            jax.ShapeDtypeStruct((slots, width), f32),
            jax.ShapeDtypeStruct((slots, width), bf16),
            jax.ShapeDtypeStruct((count, slots, units), bf16),
            jax.ShapeDtypeStruct((count, slots, units), bf16),
            jax.ShapeDtypeStruct((slots, width), bf16),
            jax.ShapeDtypeStruct((slots, width), bf16),
            jax.ShapeDtypeStruct((8, width), f32),
        ],
        scratch_shapes=[pltpu.VMEM((slots, width), bf16), pltpu.VMEM((slots, width), f32)],
        compiler_params=params(48),
        cost_estimate=cost(9e9, 30e6, 5e6),
        name="mlp",
    )(inputs, column, flag, token, mixed, proj, proj_bias, attn_scale, gain, shift, up, unit_bias,
      down, down_bias, mlp_scale, grad_out)


class Reduce:
    COPIES = 4 * 4 + 7

    def __init__(self, first, second, by_columns, keep, give, got, out, send_sems, recv_sems, own_sem):
        self.dp, self.tp = lax.axis_index("dp"), lax.axis_index("tp")
        self.first, self.second, self.by_columns = first, second, by_columns
        self.keep, self.give, self.out = keep, give, out
        self.got0, self.got1, self.got2, self.got_tp, self.total = got
        self.sends, self.recvs, self.own_sem = send_sems, recv_sems, own_sem
        self.rows, self.columns = keep.shape[1] * 2, keep.shape[2]
        self.bits = tuple(lax.rem(lax.div(self.dp, bit), 2) for bit in (CORE, first, second))

    def quarter(self, first):
        rows = self.rows // 4
        return pl.multiple_of(first * rows, 16), rows

    def eighth(self, first, second):
        begin, rows = self.quarter(first)
        if self.by_columns:
            width = self.columns // 2
            return begin, rows, pl.ds(pl.multiple_of(second * width, 128), width)
        return pl.multiple_of(begin + second * (rows // 2), 16), rows // 2, slice(None)

    def part(self, ref, spot):
        begin, rows, columns = spot
        return ref.at[pl.ds(begin, rows), columns]

    def place(self, flips):
        core, first, second = (1 - bit if turned else bit for bit, turned in zip(self.bits, flips))
        begin, rows, columns = self.eighth(first, second)
        return self.out.at[pl.ds(pl.multiple_of(core * (self.rows // 2) + begin, 16), rows), columns]

    def remote(self, n, source, target, bits=0, k=0):
        return pltpu.make_async_remote_copy(
            src_ref=source, dst_ref=target, send_sem=self.sends.at[n], recv_sem=self.recvs.at[n],
            device_id=(flip(self.dp, bits), flip(self.tp, k)), device_id_type=pl.DeviceIdType.MESH,
        )

    def copy(self, k, level):
        core, first, second = self.bits
        n = 4 * k + level
        if level == 0:
            return self.remote(n, self.give.at[k], self.got0.at[k], CORE)
        if level == 1:
            begin, rows = self.quarter(1 - first)
            return self.remote(n, self.keep.at[k, pl.ds(begin, rows), :], self.got1.at[k], self.first)
        if level == 2:
            return self.remote(n, self.part(self.keep.at[k], self.eighth(first, 1 - second)), self.got2.at[k], self.second)
        return self.remote(n, self.part(self.keep.at[k], self.eighth(first, second)), self.got_tp.at[k - 1], 0, k)

    def share(self, n):
        first, second = self.first, self.second
        bits, source = (
            (first, (0, 0, 0)), (second, (0, 0, 0)), (first | second, (0, 0, 0)), (CORE, (0, 0, 0)),
            (CORE, (0, 1, 0)), (CORE, (0, 0, 1)), (CORE, (0, 1, 1)),
        )[n]
        place = self.place(source)
        return self.remote(16 + n, self.total if n < 4 else place, place, bits)

    def add(self, target, begin, rows, columns, *items):
        step = 48

        def body(i, carry):
            here = pl.ds(pl.multiple_of(begin + i * step, 16), step)
            there = pl.ds(pl.multiple_of(i * step, 16), step)
            total = target[here, columns].astype(f32)
            for item in items:
                total += item[there, :].astype(f32)
            target[here, columns] = total.astype(bf16)
            return carry

        lax.fori_loop(0, rows // step, body, 0)

    def step0(self, k):
        self.copy(k, 0).start()

    def given(self, k):
        self.copy(k, 0).wait_send()

    def step1(self, k):
        self.copy(k, 0).wait_recv()
        self.add(self.keep.at[k], 0, self.rows // 2, slice(None), self.got0.at[k])
        self.copy(k, 1).start()

    def step2(self, k):
        self.copy(k, 1).wait_recv()
        begin, rows = self.quarter(self.bits[1])
        self.add(self.keep.at[k], begin, rows, slice(None), self.got1.at[k])
        self.copy(k, 2).start()

    def step3(self, k):
        self.copy(k, 2).wait_recv()
        self.add(self.keep.at[k], *self.eighth(*self.bits[1:]), self.got2.at[k])
        if k:
            self.copy(k, 3).start()

    def step4(self):
        for k in (1, 2, 3):
            self.copy(k, 3).wait_recv()
        begin, rows, columns = self.eighth(*self.bits[1:])
        self.add(self.keep.at[0], begin, rows, columns, *[self.got_tp.at[k] for k in range(3)])
        self.total[...] = self.keep[0, pl.ds(begin, rows), columns]
        for n in range(4):
            self.share(n).start()
        self.own_copy().start()

    def own_copy(self):
        return pltpu.make_async_copy(self.total, self.place((0, 0, 0)), self.own_sem)

    def step5(self):
        for n in range(3):
            self.share(n).wait_recv()
            self.share(4 + n).start()

    def step6(self, lowest=0):
        for n in range(3, 7):
            self.share(n).wait_recv()
        for n in range(7):
            self.share(n).wait_send()
        for k in range(4):
            for level in range(lowest, 4 if k else 3):
                self.copy(k, level).wait_send()
        self.own_copy().wait()


def schedule(points, events):
    table, rest = {}, []
    for when, action in sorted(events, key=lambda event: event[0]):
        key = next((key for key, time in points if time >= when), None)
        if key is None:
            rest.append(action)
        else:
            table.setdefault(key, []).append(action)
    return table, rest


VECTORS = 24
UNIT_ROW, HEAD_ROW = 9, 13


def back_kernel(
    grad_low_ref, hidden_ref, slope_ref, down_ref, up_ref, normed2_ref, middle_ref, grad_out_ref,
    inputs_ref, normed1_ref, packed_ref, mixed_ref, lse_ref, heads_ref, proj_ref, column_ref, row_ref, flag_ref,
    token_ref, gain1_ref, gain2_ref, attn_scale_ref, sums_ref,
    grad_inputs_ref, vector_ref, out_down, out_up, out_heads, out_proj,
    grad_unit, total, flipped, grad_mixed, grad_packed, delta, grad_query,
    keep_down, keep_up, keep_heads, keep_proj, give_down, give_heads, give_proj,
    vectors, vector_got, vector_tp, vector_sends, vector_recvs, own_sems,
    *rest,
):
    slots, width = normed2_ref.shape
    triple = heads_ref.shape[2] // 3
    size = triple // 3
    scale = size ** (-0.5)
    step = pl.program_id(0)
    got, sems = [rest[5 * n:5 * n + 5] for n in range(4)], rest[20:]
    give_up = give_down
    make = lambda n, first, second, by_columns, keep, give, out: Reduce(
        first, second, by_columns, keep, give, got[n], out, sems[2 * n], sems[2 * n + 1], own_sems.at[n])
    down = make(0, X, Y, False, keep_down, give_down, out_down)
    up = make(1, Y, X, False, keep_up, give_up, out_up)
    heads = make(2, X, Y, False, keep_heads, give_heads, out_heads)
    proj = make(3, Y, X, True, keep_proj, give_proj, out_proj)
    dp, tp, core = down.dp, down.tp, down.bits[0]
    n_dp = lax.axis_size("dp")
    levels = [bit for bit in (1, 2, 4, 8, 16, 32, 64, 128) if bit < n_dp]

    points = [((k, 0), 4.5 + 1.6 * k) for k in range(4)]
    points += [((4 + k, n), 10.5 + 6.4 * k + 1.2 * n) for k in range(4) for n in range(5)]
    points += [((8 + k, n), 40.0 + 13 * k + 0.5 * n) for k in range(4) for n in range(22)]
    points += [((12, n), 92.0 + n) for n in range(4)]
    events = []
    for k in range(4):
        events += [(8.5 + 1.6 * k, functools.partial(down.step1, k)), (17.0 + 6.5 * k, functools.partial(down.step2, k)),
                   (25.0 + 6.5 * k, functools.partial(down.step3, k))]
        events += [(19.5 + 6.4 * k, functools.partial(up.step1, k)), (30.0 + 7.0 * k, functools.partial(up.step2, k)),
                   (37.0 + 7.0 * k, functools.partial(up.step3, k))]
    events += [(53.0, down.step4), (63.0, down.step5), (68.0, up.step4), (79.0, up.step5)]
    for n, k in enumerate((1, 2, 3, 0)):
        done = 53.0 + 13 * n
        for item in (heads, proj):
            events += [(done + 3, functools.partial(item.step1, k)), (done + 10.5, functools.partial(item.step2, k)),
                       (done + 17, functools.partial(item.step3, k))]
    events += [(110.0, proj.step4), (110.1, heads.step4), (116.0, proj.step5), (116.1, heads.step5)]

    def vector_copy(n):
        if n < len(levels):
            return heads_like(vectors.at[n], vector_got.at[n], n, levels[n], 0)
        k = n - len(levels) + 1
        return heads_like(vectors.at[len(levels)], vector_tp.at[k - 1], n, 0, k)

    def heads_like(source, target, n, bits, k):
        return pltpu.make_async_remote_copy(
            src_ref=source, dst_ref=target, send_sem=vector_sends.at[n], recv_sem=vector_recvs.at[n],
            device_id=(flip(dp, bits), flip(tp, k)), device_id_type=pl.DeviceIdType.MESH,
        )

    def vector_step(n):
        vector_copy(n).wait_recv()
        vectors[n + 1] = vectors[n] + vector_got[n]
        if n + 1 < len(levels):
            vector_copy(n + 1).start()
        else:
            for k in (1, 2, 3):
                vector_copy(len(levels) + k - 1).start()

    events += [(99.0 + 3 * n, functools.partial(vector_step, n)) for n in range(len(levels))]
    table, tail = schedule(points, events)

    def pump(steps, unit):
        for at in steps:
            if (at, unit) in table:

                @pl.when(step == at)
                def _():
                    for action in table[(at, unit)]:
                        action()

    def each_send(item, place, steps):
        for k, at in steps:

            @pl.when(step == at)
            def _():
                item.step0(k)

    halves_of = (pl.ds(pl.multiple_of(core * (width // 2), 128), width // 2),
                 pl.ds(pl.multiple_of((1 - core) * (width // 2), 128), width // 2))

    @pl.when(step == 0)
    def _():
        vectors[0] = jnp.zeros_like(vectors[0])
        vectors[0, 7:8, :] = sums_ref[1:2, :]
        vectors[0, 8:9, :] = sums_ref[0:1, :]
        peers = [(dp, flip(tp, k)) for k in (1, 2, 3)]
        peers += [(flip(dp, bits), tp) for bits in (X, Y, X | Y, CORE)]
        peers += [(flip(dp, bit), tp) for bit in levels if bit >= 8]
        meet(peers)

    @pl.when(step < 4)
    def _():
        keep_down[step] = dot(hidden_ref[0, :, halves_of[0]], grad_low_ref[...], TN).astype(bf16)
        give_down[step] = dot(hidden_ref[0, :, halves_of[1]], grad_low_ref[...], TN).astype(bf16)
        each_send(down, 0, [(k, k) for k in range(4)])
        pump(range(4), 0)

    @pl.when(step == 4)
    def _():
        total[...] = jnp.zeros_like(total)
        flipped[...] = normed2_ref[...].T

    @pl.when(jnp.logical_and(step >= 4, step < 8))
    def _():
        unit_sum = jnp.zeros((1, slope_ref.shape[2]), f32)
        for n, (low, high) in enumerate(rows_of(slots, 208)):
            unit = dot(grad_low_ref[low:high, :], down_ref[0], NT) * slope_ref[0, low:high, :].astype(f32)
            unit = unit.astype(bf16)
            grad_unit[low:high, :] = unit
            unit_sum += jnp.sum(unit.astype(f32), axis=0, keepdims=True)
            total[low:high, :] += dot(unit, up_ref[0], NT)
            pump(range(4, 8), n)
        k = step - 4
        for at in range(4):

            @pl.when(k == at)
            def _():
                vectors[0, UNIT_ROW + at:UNIT_ROW + at + 1, :] = unit_sum
        keep_up[k] = dot(flipped[halves_of[0], :], grad_unit[...]).astype(bf16)
        for at in range(4):

            @pl.when(k == at)
            def _():
                down.given(at)
        give_up[k] = dot(flipped[halves_of[1], :], grad_unit[...]).astype(bf16)
        each_send(up, 0, [(k, 4 + k) for k in range(4)])
        pump(range(4, 8), 4)

    @pl.when(step == 7)
    def _():
        gain, attn_scale = gain2_ref[...].astype(f32), attn_scale_ref[...].astype(f32)

        def body(i, sums):
            here = pl.ds(pl.multiple_of(i * 64, 64), 64)
            valid, _, start = start_of(inputs_ref, column_ref, flag_ref, token_ref, here)
            grad_final = valid * grad_out_ref[here, :].astype(f32)
            grad_normed = total[here, :]
            _, scaled, inverse = layer_norm(middle_ref[here, :], gain, gain)
            grad_middle = grad_final + norm_back(grad_normed, scaled, inverse, gain)
            grad_branch1 = attn_scale * grad_middle
            grad_inputs_ref[here, :] = grad_middle
            grad_unit[here, :] = grad_branch1.astype(bf16)
            new = (grad_branch1, (middle_ref[here, :] - start) / attn_scale * grad_middle, grad_normed * scaled, grad_normed)
            return tuple(a + jnp.sum(b, axis=0, keepdims=True) for a, b in zip(sums, new))

        zero = jnp.zeros((1, width), f32)
        sums = lax.fori_loop(0, slots // 64, body, (zero,) * 4)
        for n in range(4):
            vectors[0, 3 + n:4 + n, :] = sums[n]
        total[...] = jnp.zeros_like(total)
        flipped[...] = normed1_ref[...].T

    attending = range(8, 12)
    shard_of = {8: 1, 9: 2, 10: 3, 11: 0}

    @pl.when(jnp.logical_and(step >= 8, step < 12))
    def _():
        k = lax.rem(step - 7, 4)
        grad_low1 = grad_unit
        for low in range(0, slots, 208):
            grad_mixed[low:low + 208, :] = dot(grad_low1[low:low + 208, :], proj_ref[0], NT).astype(bf16)
        value = dot(mixed_ref[0], grad_low1[...], TN).astype(bf16)
        rows = value.shape[0] // 2
        for own in (0, 1):

            @pl.when(core == own)
            def _():
                keep_proj[k] = value[own * rows:(own + 1) * rows]
                give_proj[k] = value[(1 - own) * rows:(2 - own) * rows]
        each_send(proj, 0, [(shard_of[at], at) for at in attending])
        unit = 0
        tiles = windows(slots)
        for head in range(3):
            base = head * triple
            own = slice(head * size, (head + 1) * size)
            for low, high, _, _ in tiles:
                product = grad_mixed[low:high, own].astype(f32) * mixed_ref[0, low:high, own].astype(f32)
                delta[0:1, low:high] = as_row(jnp.sum(product, axis=1, keepdims=True))
            grad_query[...] = jnp.zeros_like(grad_query)
            for low, high, begin, end in tiles:
                keys = packed_ref[0, low:high, base + size:base + 2 * size]
                values = packed_ref[0, low:high, base + 2 * size:base + 3 * size]
                query = packed_ref[0, begin:end, base:base + size] * jnp.bfloat16(scale)
                grads = grad_mixed[begin:end, own]
                scores = dot(keys, query, NT)
                same = column_ref[low:high, :] == row_ref[:, begin:end]
                shares = jnp.exp(jnp.where(same, scores - lse_ref[0, head:head + 1, begin:end], FLOOR_SCORE))
                grad_shares = dot(values, grads, NT)
                grad_scores = (shares * (grad_shares - delta[0:1, begin:end])).astype(bf16)
                grad_packed[low:high, base + 2 * size:base + 3 * size] = dot(shares.astype(bf16), grads).astype(bf16)
                grad_packed[low:high, base + size:base + 2 * size] = dot(grad_scores, query).astype(bf16)
                grad_query[begin:end, :] += dot(grad_scores, keys, TN)
                pump(attending, unit)
                unit += 1
            grad_packed[:, base:base + size] = (grad_query[...] * scale).astype(bf16)
        keep_heads[k] = dot(flipped[halves_of[0], :], grad_packed[...]).astype(bf16)
        give_heads[k] = dot(flipped[halves_of[1], :], grad_packed[...]).astype(bf16)
        each_send(heads, 0, [(shard_of[at], at) for at in attending])
        sums = jnp.sum(grad_packed[...].astype(f32), axis=0, keepdims=True)
        for at in range(4):

            @pl.when(k == at)
            def _():
                vectors[0, HEAD_ROW + at:HEAD_ROW + at + 1, :sums.shape[1]] = sums
        for low in range(0, slots, 208):
            total[low:low + 208, :] += dot(grad_packed[low:low + 208, :], heads_ref[0], NT)
        pump(attending, 21)

    @pl.when(step == 12)
    def _():
        gain = gain1_ref[...].astype(f32)

        def body(i, sums):
            here = pl.ds(pl.multiple_of(i * 64, 64), 64)
            valid, flagged, start = start_of(inputs_ref, column_ref, flag_ref, token_ref, here)
            _, scaled, inverse = layer_norm(start, gain, gain)
            grad_normed = total[here, :]
            grad_start = grad_inputs_ref[here, :] + norm_back(grad_normed, scaled, inverse, gain)
            grad_inputs_ref[here, :] = valid * (1.0 - flagged) * grad_start
            new = (valid * flagged * grad_start, grad_normed * scaled, grad_normed)
            return tuple(a + jnp.sum(b, axis=0, keepdims=True) for a, b in zip(sums, new))

        zero = jnp.zeros((1, width), f32)
        sums = (zero,) * 3
        for n, (low, high) in enumerate(((0, 4), (4, 8), (8, slots // 64))):
            sums = lax.fori_loop(low, high, body, sums)
            pump((12,), n)
        for n in range(3):
            vectors[0, n:n + 1, :] = sums[n]
        vector_copy(0).start()
        pump((12,), 3)
        for action in tail:
            action()
        last_level = len(levels)
        for k in (1, 2, 3):
            vector_copy(last_level + k - 1).wait_recv()
        mine = vectors[last_level]
        vector_ref[...] = mine + vector_tp[0] + vector_tp[1] + vector_tp[2]
        for row_at in (UNIT_ROW, HEAD_ROW):
            value = mine[row_at:row_at + 1]
            for k in (1, 2, 3):
                value += vector_tp[k - 1, row_at + k:row_at + k + 1, :]
            vector_ref[row_at:row_at + 1, :] = value
        for n in range(last_level + 3):
            vector_copy(n).wait_send()
        down.step6(1)
        for item in (up, heads, proj):
            item.step6()


def back(grad_low, hidden, slope, down, up, normed2, middle, grad_out, inputs, normed1, packed, mixed, lse,
         heads, proj, column, row, flag, token, gain1, gain2, attn_scale, sums):
    slots, width = normed2.shape
    units, columns, part = hidden.shape[2], heads.shape[2], mixed.shape[2]
    levels = lax.axis_size("dp").bit_length() - 1
    clip = lambda low, high: lambda at: jnp.minimum(jnp.maximum(at, low), high)
    in_down, in_up = clip(0, 3), lambda at: clip(4, 7)(at) - 4
    in_heads = lambda at: lax.rem(clip(8, 11)(at) - 7, 4)
    once = lambda *shape: pl.BlockSpec(shape, lambda at: (0,) * len(shape), pipeline_mode=pl.Buffered(1))
    tokens, vector, anywhere = once(slots, width), once(1, width), pl.BlockSpec(memory_space=pl.ANY)
    shapes = [(units, width), (width, units), (width, columns), (part, width)]
    got = []
    for n, (rows, cols) in enumerate(shapes):
        eighth = (rows // 4, cols // 2) if n == 3 else (rows // 8, cols)
        got += [pltpu.VMEM((4, rows // 2, cols), bf16), pltpu.VMEM((4, rows // 4, cols), bf16),
                pltpu.VMEM((4,) + eighth, bf16), pltpu.VMEM((3,) + eighth, bf16), pltpu.VMEM(eighth, bf16)]
    half = [pltpu.VMEM((4, rows // 2, cols), bf16) for rows, cols in shapes]
    return pl.pallas_call(
        back_kernel,
        grid=(13,),
        in_specs=[
            tokens, each(slots, units, at=in_down), each(slots, units, at=in_up), each(units, width, at=in_up),
            each(width, units, at=in_up), tokens, tokens, tokens, tokens, tokens,
            each(slots, columns, at=in_heads), each(slots, part, at=in_heads), each(8, slots, at=in_heads),
            each(width, columns, at=in_heads), each(part, width, at=in_heads), once(slots, 1), once(1, slots),
            once(slots, 1), vector, vector, vector, vector, once(8, width),
        ],
        out_specs=[once(slots, width), once(VECTORS, width), anywhere, anywhere, anywhere, anywhere],
        out_shape=[jax.ShapeDtypeStruct((slots, width), f32), jax.ShapeDtypeStruct((VECTORS, width), f32)]
        + [jax.ShapeDtypeStruct(shape, bf16) for shape in shapes],
        scratch_shapes=[
            pltpu.VMEM((slots, units), bf16), pltpu.VMEM((slots, width), f32), pltpu.VMEM((width, slots), bf16),
            pltpu.VMEM((slots, part), bf16), pltpu.VMEM((slots, columns), bf16), pltpu.VMEM((8, slots), f32),
            pltpu.VMEM((slots, columns // 9), f32),
        ] + half + [half[0]] + half[2:] + [
            pltpu.VMEM((levels + 1, VECTORS, width), f32), pltpu.VMEM((levels, VECTORS, width), f32),
            pltpu.VMEM((3, VECTORS, width), f32), pltpu.SemaphoreType.DMA((levels + 3,)),
            pltpu.SemaphoreType.DMA((levels + 3,)), pltpu.SemaphoreType.DMA((4,)),
        ] + got + [pltpu.SemaphoreType.DMA((Reduce.COPIES,))] * 8,
        compiler_params=pltpu.CompilerParams(vmem_limit_bytes=65400 << 10, collective_id=1, has_side_effects=True),
        cost_estimate=cost(36e9, 60e6, 12 * 480000),
        name="back",
    )(grad_low, hidden, slope, down, up, normed2, middle, grad_out, inputs, normed1, packed, mixed, lse,
      heads, proj, column, row, flag, token, gain1, gain2, attn_scale, sums)


def others(value):
    return [exchange(value, 0, k) for k in (1, 2, 3)]


def local(
    inputs,
    segment_ids,
    mask_flags,
    mask_token,
    norm_gain,
    norm_shift,
    heads_weight,
    heads_bias,
    proj_weight,
    proj_bias,
    attn_scale,
    mlp_gain,
    mlp_shift,
    up_weight,
    up_bias,
    down_weight,
    down_bias,
    mlp_scale,
    grad_out,
):
    slots = mask_flags.shape[1]
    own_rows = mask_flags.shape[0]
    width = inputs.shape[1]
    triple = heads_weight.shape[2]
    head_size = triple // 3
    heads_here = heads_weight.shape[1]
    own_ids = lax.dynamic_slice_in_dim(segment_ids, lax.axis_index("tp") * own_rows, own_rows, 0)
    column, row = own_ids.reshape(-1, 1), own_ids.reshape(1, -1)
    flag = mask_flags.reshape(-1, 1)
    vector = lambda v: v.reshape(1, -1)
    token, gain1, gain2 = vector(mask_token), vector(norm_gain), vector(mlp_gain)
    own_heads = heads_weight.reshape(width, -1)
    heads_cols = own_heads.shape[1]

    own_bias = jnp.concatenate([head_bias_row(heads_bias, head_size), up_bias.astype(f32).reshape(1, -1)], axis=1)
    bias = jnp.stack([own_bias] + others(own_bias))
    head_bias, unit_bias = bias[:, :, :heads_cols], bias[:, :, heads_cols:]

    normed1, packed, mixed, lse, heads_all, up_all, proj_all, down_all = gather_attend(
        inputs, column, row, flag, token, gain1, vector(norm_shift), head_bias, own_heads, up_weight, proj_weight,
        down_weight,
    )
    proj_flat = proj_all.reshape(-1, width)
    middle, normed2, hidden, slope, output, grad_low2, sums_a = mlp(
        inputs, column, flag, token, mixed, proj_flat, vector(proj_bias), vector(attn_scale), gain2,
        vector(mlp_shift), up_all, unit_bias, down_all, vector(down_bias), vector(mlp_scale), grad_out,
    )
    grad_inputs, small, sum_down, sum_up, sum_heads, sum_proj = back(
        grad_low2, hidden, slope, down_all, up_all, normed2, middle, grad_out, inputs, normed1, packed, mixed,
        lse, heads_all, proj_all, column, row, flag, token, gain1, gain2, vector(attn_scale), sums_a,
    )
    sum_down, sum_up, sum_proj = (item.astype(f32) for item in (sum_down, sum_up, sum_proj))
    sum_heads = sum_heads.astype(f32).reshape(heads_weight.shape)
    bias_sums = small[HEAD_ROW, :heads_cols].reshape(heads_here, triple)
    sum_heads_bias = jnp.concatenate([bias_sums[:, :head_size], bias_sums[:, 2 * head_size:]], axis=1)
    sum_up_bias = small[UNIT_ROW, :up_bias.shape[0]]
    (sum_token, sum_gain1, sum_shift1, sum_proj_bias, sum_scale1, sum_gain2, sum_shift2,
     sum_down_bias, sum_scale2) = [small[i] for i in range(9)]
    return (
        output,
        grad_inputs,
        sum_token,
        sum_gain1,
        sum_shift1,
        sum_heads,
        sum_heads_bias,
        sum_proj,
        sum_proj_bias,
        sum_scale1,
        sum_gain2,
        sum_shift2,
        sum_up,
        sum_up_bias,
        sum_down,
        sum_down_bias,
        sum_scale2,
    )


def solution(mesh):
    placed = (
        P(("dp", "tp"), None),
        P("dp", None),
        P(("dp", "tp"), None),
        P(),
        P(),
        P(),
        P(None, "tp", None),
        P("tp", None),
        P("tp", None),
        P(),
        P(),
        P(),
        P(),
        P(None, "tp"),
        P("tp"),
        P("tp", None),
        P(),
        P(),
        P(("dp", "tp"), None),
    )
    return jax.shard_map(
        local,
        mesh=mesh,
        in_specs=placed,
        out_specs=(
            P(("dp", "tp"), None),
            P(("dp", "tp"), None),
            P(),
            P(),
            P(),
            P(None, "tp", None),
            P("tp", None),
            P("tp", None),
            P(),
            P(),
            P(),
            P(),
            P(None, "tp"),
            P("tp"),
            P("tp", None),
            P(),
            P(),
        ),
        check_vma=False,
    )
```

```python
import functools

import jax
import jax.numpy as jnp
from jax import lax
from jax.experimental import pallas as pl
from jax.experimental.pallas import tpu as pltpu
from jax.sharding import PartitionSpec as P

EPSILON = 1e-06
FLOOR_SCORE = -1e30
SQRT_HALF = 0.7071067811865476
INV_ROOT_TWO_PI = 0.3989422804014327
LONGEST = 14 * 14 + 1
FIFTH_FROM = 4 * (11 * 11 + 1)
TILE = 128
CORE, X, Y = 1, 2, 4

f32, bf16 = jnp.float32, jnp.bfloat16
NN = (((1,), (0,)), ((), ()))
NT = (((1,), (1,)), ((), ()))
TN = (((0,), (0,)), ((), ()))


def dot(a, b, dims=NN):
    return lax.dot_general(a, b, dims, preferred_element_type=f32)


def layer_norm(values, gain, shift):
    centre = values - jnp.mean(values, axis=-1, keepdims=True)
    inverse = lax.rsqrt(jnp.mean(centre * centre, axis=-1, keepdims=True) + EPSILON)
    scaled = centre * inverse
    return (scaled * gain + shift, scaled, inverse)


def norm_back(grad_normed, scaled, inverse, gain):
    grad_scaled = grad_normed * gain
    first = jnp.mean(grad_scaled, axis=-1, keepdims=True)
    second = jnp.mean(grad_scaled * scaled, axis=-1, keepdims=True)
    return inverse * (grad_scaled - first - scaled * second)


def gelu_parts(inner):
    normal_cdf = 0.5 * (1.0 + lax.erf(inner * SQRT_HALF))
    density = jnp.exp(-0.5 * inner * inner) * INV_ROOT_TWO_PI
    return (inner * normal_cdf, normal_cdf + inner * density)


def windows(slots):
    out = []
    for low in range(0, slots, TILE):
        high = min(low + TILE, slots)
        begin = low - LONGEST + 1
        if low >= FIFTH_FROM:
            begin = min(begin, FIFTH_FROM)
        end = high + LONGEST - 1
        if high > FIFTH_FROM:
            end = slots
        begin = max(begin, 0) // 128 * 128
        end = min((end + 127) // 128 * 128, slots)
        out.append((low, high, begin, end))
    return out


def as_row(column):
    rows = column.shape[0]
    shape = (rows, rows)
    here = lax.broadcasted_iota(jnp.int32, shape, 0) == lax.broadcasted_iota(jnp.int32, shape, 1)
    return jnp.sum(jnp.where(here, column, 0.0), axis=0, keepdims=True)


def whole(*shape):
    return pl.BlockSpec(shape, lambda k: (0,) * len(shape))


def each(*shape, at=lambda k: k):
    return pl.BlockSpec((1,) + shape, lambda k: (at(k),) + (0,) * len(shape))


def params(megabytes):
    return pltpu.CompilerParams(vmem_limit_bytes=megabytes << 20)


def cost(flops, moved, exps=0):
    return pl.CostEstimate(flops=int(flops), transcendentals=int(exps), bytes_accessed=int(moved))


def start_of(inputs_ref, column_ref, flag_ref, token, here):
    valid = (column_ref[here, :] >= 0).astype(f32)
    flagged = (flag_ref[here, :] == 1).astype(f32)
    start = valid * (flagged * token + (1.0 - flagged) * inputs_ref[here, :].astype(f32))
    return valid, flagged, start


def blocks(columns, step=256):
    return [slice(low, min(low + step, columns)) for low in range(0, columns, step)]


def rows_of(slots, step=104):
    return [(low, min(low + step, slots)) for low in range(0, slots, step)]


def flip(index, bits):
    bit = 1
    while bit <= bits:
        if bits & bit:
            index = index + bit * (1 - 2 * lax.rem(lax.div(index, bit), 2))
        bit *= 2
    return index


class Gather:
    ROUTES = ("z", "x", "y", "fx", "fy", "c0", "c2", "c4", "c6")
    COPIES = 3 * len(ROUTES)

    def __init__(self, full_ref, by_columns, send_sems, recv_sems):
        self.dp, self.tp = lax.axis_index("dp"), lax.axis_index("tp")
        self.own = lax.rem(self.dp, 8)
        self.full, self.by_columns = full_ref, by_columns
        self.sends, self.recvs = send_sems, recv_sems
        _, rows, columns = full_ref.shape
        self.rows, self.columns = (rows // 4, columns // 2) if by_columns else (rows // 8, columns)
        self.half = self.rows // 32 * 16

    def piece(self, k, bits, half=None):
        place, columns = flip(self.own, bits), slice(None)
        if self.by_columns:
            columns = pl.ds(pl.multiple_of(lax.rem(place, 2) * self.columns, 128), self.columns)
            place = lax.div(place, 2)
        begin, height = place * self.rows, self.rows
        if half == 0:
            height = self.half
        elif half == 1:
            begin, height = begin + self.half, self.rows - self.half
        return self.full.at[k, pl.ds(pl.multiple_of(begin, 16), height), columns]

    def copy(self, k, route):
        if route == "z":
            source, target, to = self.piece(0, 0), self.piece(k, 0), (self.dp, flip(self.tp, k))
        else:
            bits, half, link = {
                "x": (0, None, X), "y": (0, None, Y), "fx": (Y, 1, X), "fy": (X, 0, Y),
                "c0": (0, None, CORE), "c2": (X, None, CORE), "c4": (Y, None, CORE), "c6": (X | Y, None, CORE),
            }[route]
            source = target = self.piece(k, bits, half)
            to = (flip(self.dp, link), self.tp)
        n = (k - 1) * len(self.ROUTES) + self.ROUTES.index(route)
        return pltpu.make_async_remote_copy(
            src_ref=source, dst_ref=target, send_sem=self.sends.at[n], recv_sem=self.recvs.at[n],
            device_id=to, device_id_type=pl.DeviceIdType.MESH,
        )

    def start(self, k, *routes):
        for route in routes:
            self.copy(k, route).start()

    def arrived(self, k, *routes):
        for route in routes:
            self.copy(k, route).wait_recv()

    def begin(self, k):
        self.start(k, "z")

    def step1(self, k):
        self.arrived(k, "z")
        self.start(k, "x", "y", "c0")

    def step2(self, k):
        self.arrived(k, "x")
        self.start(k, "fy", "c2")
        self.arrived(k, "y")
        self.start(k, "fx", "c4")

    def step3(self, k):
        self.arrived(k, "fx", "fy")
        self.start(k, "c6")

    def step4(self, k):
        self.arrived(k, "c0", "c2", "c4", "c6")

    def sent(self):
        for k in (1, 2, 3):
            for route in self.ROUTES:
                self.copy(k, route).wait_send()


def meet(peers):
    barrier = pltpu.get_barrier_semaphore()
    for peer in peers:
        pl.semaphore_signal(barrier, inc=1, device_id=peer, device_id_type=pl.DeviceIdType.MESH)
    pl.semaphore_wait(barrier, len(peers))


def as_column(row):
    size = row.shape[1]
    shape = (size, size)
    here = lax.broadcasted_iota(jnp.int32, shape, 0) == lax.broadcasted_iota(jnp.int32, shape, 1)
    return jnp.sum(jnp.where(here, row, 0), axis=1, keepdims=True)


def dispatch(table, step, steps, unit):
    for at in steps:
        if table.get((at, unit)):

            @pl.when(step == at)
            def _():
                for action in table[(at, unit)]:
                    action()


TOKEN, GAIN1, SHIFT1, PROJ_BIAS, ATTN_SCALE, GAIN2, SHIFT2, DOWN_BIAS, MLP_SCALE = range(9)

HEADS, UP, PROJ, DOWN = range(4)
FORWARD_PLAN = {
    (0, 1): ((HEADS, (1, 2), 1),),
    (0, 6): ((HEADS, (3,), 1), (HEADS, (1,), 2),),
    (1, -1): ((PROJ, (1, 2, 3), 0), (UP, (1, 2, 3), 0), (HEADS, (2, 3), 2), (PROJ, (1,), 1), (HEADS, (1, 2), 3), (PROJ, (2, 3), 1), (HEADS, (3,), 3), (HEADS, (1,), 4),),
    (1, 1): ((HEADS, (2,), 4), (PROJ, (1, 2), 2), (UP, (1,), 1),),
    (1, 3): ((HEADS, (3,), 4), (PROJ, (3,), 2),),
    (1, 6): ((DOWN, (1, 2, 3), 0), (UP, (2,), 1), (PROJ, (1, 2), 3),),
    (2, 1): ((UP, (1,), 2), (PROJ, (3,), 3), (UP, (3,), 1), (PROJ, (1, 2), 4),),
    (2, 3): ((DOWN, (1,), 1),),
    (2, 6): ((UP, (2,), 2), (PROJ, (3,), 4), (UP, (1,), 3),),
    (3, 1): ((DOWN, (2,), 1), (UP, (3,), 2),),
    (3, 3): ((UP, (1,), 4),),
    (3, 6): ((DOWN, (1,), 2), (DOWN, (3,), 1), (UP, (2,), 3),),
    (4, 1): ((UP, (2,), 4), (UP, (3,), 3), (DOWN, (2,), 2),),
    (4, 3): ((DOWN, (1,), 3),),
    (5, -1): ((DOWN, (3,), 2), (UP, (3,), 4), (DOWN, (2,), 3), (DOWN, (1,), 4),),
    (5, 3): ((DOWN, (3,), 3), (DOWN, (2,), 4),),
    (6, 3): ((DOWN, (3,), 4),),
}


def forward_kernel(
    inputs_ref, segment_ref, mask_ref, vectors_ref, heads_bias_ref, unit_bias_ref, grad_out_ref,
    heads_ref, up_ref, proj_ref, down_ref,
    normed1_ref, column_ref, flag_ref, row_ref, packed_ref, mixed_ref, lse_ref, middle_ref, normed2_ref, hidden_ref,
    slope_ref, output_ref, grad_low_ref, sums_ref, heads_all, up_all, proj_all, down_all,
    heads_now, up_now, proj_now, down_now, head_bias, unit_bias, mixed_all, total,
    own_sems, store_sems, bias_sends, bias_recvs,
    *sems,
):
    slots = inputs_ref.shape[0]
    triple = heads_now.shape[2] // 3
    size = triple // 3
    scale = size ** (-0.5)
    part = mixed_ref.shape[2]
    step = pl.program_id(0)
    vector = lambda n: vectors_ref[n:n + 1, :]
    shards, fulls = (heads_ref, up_ref, proj_ref, down_ref), (heads_all, up_all, proj_all, down_all)
    nows = (heads_now, up_now, proj_now, down_now)
    gathers = [Gather(nows[n], n == PROJ, sems[2 * n], sems[2 * n + 1]) for n in range(4)]
    dp, tp = gathers[0].dp, gathers[0].tp
    loads = [pltpu.make_async_copy(shards[n], nows[n].at[0], own_sems.at[n]) for n in range(4)]
    store = lambda n, k: pltpu.make_async_copy(nows[n].at[k], fulls[n].at[k], store_sems.at[n, k])

    def bias_copy(n, k):
        item = (head_bias, unit_bias)[n]
        return pltpu.make_async_remote_copy(
            src_ref=item.at[0], dst_ref=item.at[k], send_sem=bias_sends.at[n, k], recv_sem=bias_recvs.at[n, k],
            device_id=(dp, flip(tp, k)), device_id_type=pl.DeviceIdType.MESH,
        )

    table = {}
    for key, entries in FORWARD_PLAN.items():
        table[key] = []
        for n, ks, action in entries:
            item = gathers[n]
            for k in ks:
                table[key].append(functools.partial(
                    (item.begin, item.step1, item.step2, item.step3, item.step4)[action], k))
                if action == 4:
                    table[key].append(store(n, k).start)

    @pl.when(step == 0)
    def _():
        for load in loads:
            load.start()
        meet([(dp, flip(tp, k)) for k in (1, 2, 3)] + [(flip(dp, bit), tp) for bit in (X, Y, CORE)])
        loads[HEADS].wait()
        for k in (1, 2, 3):
            gathers[HEADS].begin(k)
        blank = jnp.zeros((1, size), f32)
        pieces = []
        for head in range(3):
            here = heads_bias_ref[head:head + 1, :].astype(f32)
            pieces += [here[:, :size], blank, here[:, size:]]
        head_bias[0] = jnp.broadcast_to(jnp.concatenate(pieces, axis=1), head_bias.shape[1:])
        unit_bias[0] = jnp.broadcast_to(unit_bias_ref[...].astype(f32), unit_bias.shape[1:])
        for n in range(2):
            for k in (1, 2, 3):
                bias_copy(n, k).start()
        row_ref[...] = segment_ref[pl.ds(tp, 1), :]
        for low in range(0, slots, 128):
            high = min(low + 128, slots)
            column_ref[low:high, :] = as_column(row_ref[:, low:high])
            flag_ref[low:high, :] = as_column(mask_ref[:, low:high])

        def body(i, carry):
            here = pl.ds(pl.multiple_of(i * 64, 64), 64)
            _, _, start = start_of(inputs_ref, column_ref, flag_ref, vector(TOKEN), here)
            normed1_ref[here, :] = layer_norm(start, vector(GAIN1), vector(SHIFT1))[0].astype(bf16)
            return carry

        lax.fori_loop(0, slots // 64, body, 0)
        for load in loads[1:]:
            load.wait()
        for n in range(4):
            store(n, 0).start()

    @pl.when(step == 1)
    def _():
        for k in (1, 2, 3):
            bias_copy(0, k).wait_recv()

    dispatch(table, step, range(1, 8), -1)

    @pl.when(step < 4)
    def _():
        for low in range(0, slots, 208):
            product = dot(normed1_ref[low:low + 208, :], heads_now[step])
            packed_ref[0, low:low + 208, :] = (product + head_bias[step, 0:1, :]).astype(bf16)
        lse_ref[...] = jnp.zeros_like(lse_ref)
        bases = [head * triple for head in range(3)]
        for unit, (low, high, begin, end) in enumerate(windows(slots)):
            same = column_ref[low:high, :] == row_ref[:, begin:end]
            scores = [
                dot(packed_ref[0, low:high, base:base + size] * jnp.bfloat16(scale),
                    packed_ref[0, begin:end, base + size:base + 2 * size], NT)
                for base in bases
            ]
            scores = [jnp.where(same, item, FLOOR_SCORE) for item in scores]
            largest = [jnp.max(item, axis=1, keepdims=True) for item in scores]
            raised = [jnp.exp(item - top) for item, top in zip(scores, largest)]
            totals = [jnp.sum(item, axis=1, keepdims=True) for item in raised]
            mixed = [
                dot(item.astype(bf16), packed_ref[0, begin:end, base + 2 * size:base + 3 * size])
                for item, base in zip(raised, bases)
            ]
            mixed = [(item * (1.0 / total)).astype(bf16) for item, total in zip(mixed, totals)]
            mixed_ref[0, low:high, :] = jnp.concatenate(mixed, axis=1)
            for head in range(3):
                lse_ref[0, head:head + 1, low:high] = as_row(largest[head] + jnp.log(totals[head]))
            dispatch(table, step, range(4), unit)

    for k in range(4):

        @pl.when(step == k)
        def _():
            mixed_all[:, k * part:(k + 1) * part] = mixed_ref[0]

    @pl.when(step == 4)
    def _():
        for k in (1, 2, 3):
            bias_copy(1, k).wait_recv()
        total[...] = jnp.zeros_like(total)
        proj = proj_now[...].reshape(-1, proj_now.shape[2])
        for low, high in rows_of(slots, 208):
            middle_ref[low:high, :] = dot(mixed_all[low:high, :], proj) + vector(PROJ_BIAS)

        def body(i, carry):
            here = pl.ds(pl.multiple_of(i * 64, 64), 64)
            _, _, start = start_of(inputs_ref, column_ref, flag_ref, vector(TOKEN), here)
            middle = start + vector(ATTN_SCALE) * middle_ref[here, :]
            middle_ref[here, :] = middle
            normed2_ref[here, :] = layer_norm(middle, vector(GAIN2), vector(SHIFT2))[0].astype(bf16)
            return carry

        lax.fori_loop(0, slots // 64, body, 0)

    @pl.when(step >= 4)
    def _():
        k = step - 4
        for unit, (low, high) in enumerate(rows_of(slots, 208)):
            for columns in blocks(hidden_ref.shape[2]):
                inner = dot(normed2_ref[low:high, :], up_now[k, :, columns]) + unit_bias[k, 0:1, columns]
                value, slope = gelu_parts(inner)
                hidden_ref[0, low:high, columns] = value.astype(bf16)
                slope_ref[0, low:high, columns] = slope.astype(bf16)
            total[low:high, :] += dot(hidden_ref[0, low:high, :], down_now[k])
            dispatch(table, step, range(4, 8), unit)

    @pl.when(step == 7)
    def _():
        def body(i, sums):
            here = pl.ds(pl.multiple_of(i * 64, 64), 64)
            valid = (column_ref[here, :] >= 0).astype(f32)
            branch2 = total[here, :] + vector(DOWN_BIAS)
            output_ref[here, :] = (valid * (middle_ref[here, :] + vector(MLP_SCALE) * branch2)).astype(bf16)
            grad_final = valid * grad_out_ref[here, :].astype(f32)
            grad_branch2 = vector(MLP_SCALE) * grad_final
            grad_low_ref[here, :] = grad_branch2.astype(bf16)
            return tuple(a + jnp.sum(b, axis=0, keepdims=True) for a, b in zip(sums, (branch2 * grad_final, grad_branch2)))

        zero = jnp.zeros((1, inputs_ref.shape[1]), f32)
        sums = lax.fori_loop(0, slots // 64, body, (zero, zero))
        sums_ref[...] = jnp.zeros_like(sums_ref)
        sums_ref[0:1, :], sums_ref[1:2, :] = sums
        for n, item in enumerate(gathers):
            item.sent()
            for k in range(4):
                store(n, k).wait()
        for n in range(2):
            for k in (1, 2, 3):
                bias_copy(n, k).wait_send()


def once(*shape):
    return pl.BlockSpec(shape, lambda at: (0,) * len(shape), pipeline_mode=pl.Buffered(1))


def forward(inputs, segments, mask, vectors, heads_bias, unit_bias, grad_out, heads, up, proj, down):
    slots, width = inputs.shape
    columns, units = heads.shape[1], up.shape[1]
    part = columns // 3
    anywhere = pl.BlockSpec(memory_space=pl.ANY)
    early = lambda at: jnp.minimum(at, 3)
    late = lambda at: jnp.maximum(at - 4, 0)
    tokens = once(slots, width)
    shape = jax.ShapeDtypeStruct
    return pl.pallas_call(
        forward_kernel,
        grid=(8,),
        in_specs=[
            tokens, once(*segments.shape), once(1, slots), once(*vectors.shape), once(*heads_bias.shape),
            once(*unit_bias.shape), tokens, anywhere, anywhere, anywhere, anywhere,
        ],
        out_specs=[
            tokens, once(slots, 1), once(slots, 1), once(1, slots), each(slots, columns, at=early),
            each(slots, part, at=early), each(8, slots, at=early), tokens, tokens, each(slots, units, at=late),
            each(slots, units, at=late), tokens, tokens, once(8, width), anywhere, anywhere, anywhere, anywhere,
        ],
        out_shape=[
            shape((slots, width), bf16), shape((slots, 1), jnp.int32), shape((slots, 1), jnp.int32),
            shape((1, slots), jnp.int32), shape((4, slots, columns), bf16), shape((4, slots, part), bf16),
            shape((4, 8, slots), f32), shape((slots, width), f32), shape((slots, width), bf16),
            shape((4, slots, units), bf16), shape((4, slots, units), bf16), shape((slots, width), bf16),
            shape((slots, width), bf16), shape((8, width), f32),
        ] + [shape((4,) + item.shape, bf16) for item in (heads, up, proj, down)],
        scratch_shapes=[
            pltpu.VMEM((4,) + heads.shape, bf16), pltpu.VMEM((4,) + up.shape, bf16), pltpu.VMEM((4,) + proj.shape, bf16),
            pltpu.VMEM((4,) + down.shape, bf16), pltpu.VMEM((4, 8, columns), f32), pltpu.VMEM((4, 8, units), f32),
            pltpu.VMEM((slots, width), bf16), pltpu.VMEM((slots, width), f32),
            pltpu.SemaphoreType.DMA((4,)), pltpu.SemaphoreType.DMA((4, 4)), pltpu.SemaphoreType.DMA((2, 4)), pltpu.SemaphoreType.DMA((2, 4)),
        ] + [pltpu.SemaphoreType.DMA((Gather.COPIES,))] * 8,
        compiler_params=pltpu.CompilerParams(vmem_limit_bytes=60 << 20, collective_id=0, has_side_effects=True),
        cost_estimate=cost(26e9, 60e6, 6e6),
        name="forward",
    )(inputs, segments, mask, vectors, heads_bias, unit_bias, grad_out, heads, up, proj, down)


class Reduce:
    COPIES = 4 * 4 + 7

    def __init__(self, first, second, by_columns, keep, give, got, out, send_sems, recv_sems, own_sem):
        self.dp, self.tp = lax.axis_index("dp"), lax.axis_index("tp")
        self.first, self.second, self.by_columns = first, second, by_columns
        self.keep, self.give, self.out = keep, give, out
        self.got0, self.got1, self.got2, self.got_tp, self.total = got
        self.sends, self.recvs, self.own_sem = send_sems, recv_sems, own_sem
        self.rows, self.columns = keep.shape[1] * 2, keep.shape[2]
        self.bits = tuple(lax.rem(lax.div(self.dp, bit), 2) for bit in (CORE, first, second))

    def quarter(self, first):
        rows = self.rows // 4
        return pl.multiple_of(first * rows, 16), rows

    def eighth(self, first, second):
        begin, rows = self.quarter(first)
        if self.by_columns:
            width = self.columns // 2
            return begin, rows, pl.ds(pl.multiple_of(second * width, 128), width)
        return pl.multiple_of(begin + second * (rows // 2), 16), rows // 2, slice(None)

    def part(self, ref, spot):
        begin, rows, columns = spot
        return ref.at[pl.ds(begin, rows), columns]

    def place(self, flips):
        core, first, second = (1 - bit if turned else bit for bit, turned in zip(self.bits, flips))
        begin, rows, columns = self.eighth(first, second)
        return self.out.at[pl.ds(pl.multiple_of(core * (self.rows // 2) + begin, 16), rows), columns]

    def remote(self, n, source, target, bits=0, k=0):
        return pltpu.make_async_remote_copy(
            src_ref=source, dst_ref=target, send_sem=self.sends.at[n], recv_sem=self.recvs.at[n],
            device_id=(flip(self.dp, bits), flip(self.tp, k)), device_id_type=pl.DeviceIdType.MESH,
        )

    def copy(self, k, level):
        core, first, second = self.bits
        n = 4 * k + level
        if level == 0:
            return self.remote(n, self.give.at[k], self.got0.at[k], CORE)
        if level == 1:
            begin, rows = self.quarter(1 - first)
            return self.remote(n, self.keep.at[k, pl.ds(begin, rows), :], self.got1.at[k], self.first)
        if level == 2:
            return self.remote(n, self.part(self.keep.at[k], self.eighth(first, 1 - second)), self.got2.at[k], self.second)
        return self.remote(n, self.part(self.keep.at[k], self.eighth(first, second)), self.got_tp.at[k - 1], 0, k)

    def share(self, n):
        first, second = self.first, self.second
        bits, source = (
            (first, (0, 0, 0)), (second, (0, 0, 0)), (first | second, (0, 0, 0)), (CORE, (0, 0, 0)),
            (CORE, (0, 1, 0)), (CORE, (0, 0, 1)), (CORE, (0, 1, 1)),
        )[n]
        place = self.place(source)
        return self.remote(16 + n, self.total if n < 4 else place, place, bits)

    def add(self, target, begin, rows, columns, *items):
        step = 48

        def body(i, carry):
            here = pl.ds(pl.multiple_of(begin + i * step, 16), step)
            there = pl.ds(pl.multiple_of(i * step, 16), step)
            if len(items) == 1:
                target[here, columns] = target[here, columns] + items[0][there, :]
            else:
                total = target[here, columns].astype(f32)
                for item in items:
                    total += item[there, :].astype(f32)
                target[here, columns] = total.astype(bf16)
            return carry

        lax.fori_loop(0, rows // step, body, 0)

    def step0(self, k):
        self.copy(k, 0).start()

    def given(self, k):
        self.copy(k, 0).wait_send()

    def step1(self, k):
        self.copy(k, 0).wait_recv()
        self.add(self.keep.at[k], 0, self.rows // 2, slice(None), self.got0.at[k])
        self.copy(k, 1).start()

    def step2(self, k):
        self.copy(k, 1).wait_recv()
        begin, rows = self.quarter(self.bits[1])
        self.add(self.keep.at[k], begin, rows, slice(None), self.got1.at[k])
        self.copy(k, 2).start()

    def step3(self, k):
        self.copy(k, 2).wait_recv()
        self.add(self.keep.at[k], *self.eighth(*self.bits[1:]), self.got2.at[k])
        if k:
            self.copy(k, 3).start()

    def step4(self):
        for k in (1, 2, 3):
            self.copy(k, 3).wait_recv()
        begin, rows, columns = self.eighth(*self.bits[1:])
        self.add(self.keep.at[0], begin, rows, columns, *[self.got_tp.at[k] for k in range(3)])
        self.total[...] = self.keep[0, pl.ds(begin, rows), columns]
        for n in range(4):
            self.share(n).start()
        self.own_copy().start()

    def own_copy(self):
        return pltpu.make_async_copy(self.total, self.place((0, 0, 0)), self.own_sem)

    def step5(self):
        for n in range(3):
            self.share(n).wait_recv()
            self.share(4 + n).start()

    def step6(self, lowest=0):
        for n in range(3, 7):
            self.share(n).wait_recv()
        for n in range(7):
            self.share(n).wait_send()
        for k in range(4):
            for level in range(lowest, 4 if k else 3):
                self.copy(k, level).wait_send()
        self.own_copy().wait()


VECTORS = 24
UNIT_ROW, HEAD_ROW = 9, 13


VECTOR = 4
BACK_PLAN = {
    (3, 0): ((DOWN, 0, 1),),
    (4, 1): ((DOWN, 1, 1), (DOWN, 2, 1),),
    (4, 3): ((DOWN, 3, 1),),
    (5, 3): ((DOWN, 0, 2), (UP, 0, 1),),
    (6, 1): ((DOWN, 1, 2),),
    (6, 3): ((UP, 1, 1), (DOWN, 0, 3),),
    (7, 1): ((DOWN, 2, 2),),
    (7, 3): ((UP, 2, 1), (UP, 0, 2),),
    (8, 1): ((DOWN, 1, 3), (DOWN, 3, 2), (UP, 3, 1), (UP, 0, 3), (UP, 1, 2),),
    (8, 3): ((DOWN, 2, 3), (PROJ, 1, 1),),
    (8, 7): ((UP, 2, 2), (UP, 1, 3),),
    (9, 1): ((DOWN, 3, 3), (HEADS, 1, 1),),
    (9, 3): ((PROJ, 2, 1), (UP, 2, 3),),
    (9, 6): ((UP, 3, 2), (PROJ, 1, 2),),
    (9, 7): ((PROJ, 2, 2),),
    (10, 1): ((HEADS, 1, 2), (DOWN, 0, 4), (HEADS, 2, 1), (UP, 3, 3),),
    (10, 3): ((PROJ, 1, 3), (PROJ, 3, 1), (PROJ, 2, 3),),
    (10, 6): ((HEADS, 1, 3),),
    (11, 1): ((UP, 0, 4), (HEADS, 3, 1), (DOWN, 0, 5),),
    (11, 3): ((PROJ, 3, 2), (PROJ, 0, 1), (HEADS, 2, 2),),
    (12, 1): ((UP, 0, 5), (PROJ, 0, 2),),
    (12, 2): ((HEADS, 0, 1),),
}
BACK_TAIL = (
    (HEADS, 2, 3),
    (HEADS, 3, 2),
    (PROJ, 3, 3),
    (PROJ, 0, 3),
    (VECTOR, 0, 0),
    (HEADS, 3, 3),
    (HEADS, 0, 2),
    (VECTOR, 1, 0),
    (PROJ, 0, 4),
    (HEADS, 0, 3),
    (HEADS, 0, 4),
    (VECTOR, 2, 0),
    (PROJ, 0, 5),
    (HEADS, 0, 5),
)


def back_kernel(
    grad_low_ref, hidden_ref, slope_ref, down_ref, up_ref, normed2_ref, middle_ref, grad_out_ref,
    inputs_ref, normed1_ref, packed_ref, mixed_ref, lse_ref, heads_ref, proj_ref, column_ref, row_ref, flag_ref,
    constants_ref, sums_ref,
    grad_inputs_ref, vector_ref, out_down, out_up, out_heads, out_proj,
    grad_unit, total, flipped, grad_mixed, grad_packed, delta, grad_query,
    keep_down, keep_up, keep_heads, keep_proj, give_down, give_heads, give_proj,
    vectors, vector_got, vector_tp, vector_sends, vector_recvs, own_sems,
    *rest,
):
    slots, width = normed2_ref.shape
    triple = heads_ref.shape[2] // 3
    size = triple // 3
    scale = size ** (-0.5)
    step = pl.program_id(0)
    got, sems = [rest[5 * n:5 * n + 5] for n in range(4)], rest[20:]
    give_up = give_down
    constant = lambda n: constants_ref[n:n + 1, :]
    make = lambda n, first, second, by_columns, keep, give, out: Reduce(
        first, second, by_columns, keep, give, got[n], out, sems[2 * n], sems[2 * n + 1], own_sems.at[n])
    down = make(0, X, Y, False, keep_down, give_down, out_down)
    up = make(1, Y, X, False, keep_up, give_up, out_up)
    heads = make(2, X, Y, False, keep_heads, give_heads, out_heads)
    proj = make(3, Y, X, True, keep_proj, give_proj, out_proj)
    dp, tp, core = down.dp, down.tp, down.bits[0]
    n_dp = lax.axis_size("dp")
    levels = [bit for bit in (1, 2, 4, 8, 16, 32, 64, 128) if bit < n_dp]

    def vector_copy(n):
        if n < len(levels):
            return heads_like(vectors.at[n], vector_got.at[n], n, levels[n], 0)
        k = n - len(levels) + 1
        return heads_like(vectors.at[len(levels)], vector_tp.at[k - 1], n, 0, k)

    def heads_like(source, target, n, bits, k):
        return pltpu.make_async_remote_copy(
            src_ref=source, dst_ref=target, send_sem=vector_sends.at[n], recv_sem=vector_recvs.at[n],
            device_id=(flip(dp, bits), flip(tp, k)), device_id_type=pl.DeviceIdType.MESH,
        )

    def vector_step(n):
        vector_copy(n).wait_recv()
        vectors[n + 1] = vectors[n] + vector_got[n]
        if n + 1 < len(levels):
            vector_copy(n + 1).start()
        else:
            for k in (1, 2, 3):
                vector_copy(len(levels) + k - 1).start()

    def action_of(entry):
        item, k, part = entry
        if item == VECTOR:
            return functools.partial(vector_step, k)
        item = {HEADS: heads, UP: up, PROJ: proj, DOWN: down}[item]
        if part > 3:
            return (item.step4, item.step5)[part - 4]
        return functools.partial((item.step1, item.step2, item.step3)[part - 1], k)

    table = {key: [action_of(entry) for entry in entries] for key, entries in BACK_PLAN.items()}
    tail = [action_of(entry) for entry in BACK_TAIL]
    tail += [functools.partial(vector_step, n) for n in range(3, len(levels))]

    def pump(steps, unit):
        for at in steps:
            if (at, unit) in table:

                @pl.when(step == at)
                def _():
                    for action in table[(at, unit)]:
                        action()

    def each_send(item, place, steps):
        for k, at in steps:

            @pl.when(step == at)
            def _():
                item.step0(k)

    halves_of = (pl.ds(pl.multiple_of(core * (width // 2), 128), width // 2),
                 pl.ds(pl.multiple_of((1 - core) * (width // 2), 128), width // 2))

    @pl.when(step == 0)
    def _():
        vectors[0] = jnp.zeros_like(vectors[0])
        vectors[0, 7:8, :] = sums_ref[1:2, :]
        vectors[0, 8:9, :] = sums_ref[0:1, :]
        peers = [(dp, flip(tp, k)) for k in (1, 2, 3)]
        peers += [(flip(dp, bits), tp) for bits in (X, Y, X | Y, CORE)]
        peers += [(flip(dp, bit), tp) for bit in levels if bit >= 8]
        meet(peers)

    @pl.when(step < 4)
    def _():
        keep_down[step] = dot(hidden_ref[0, :, halves_of[0]], grad_low_ref[...], TN).astype(bf16)
        give_down[step] = dot(hidden_ref[0, :, halves_of[1]], grad_low_ref[...], TN).astype(bf16)
        each_send(down, 0, [(k, k) for k in range(4)])
        pump(range(4), 0)

    @pl.when(step == 4)
    def _():
        total[...] = jnp.zeros_like(total)
        flipped[...] = normed2_ref[...].T

    @pl.when(jnp.logical_and(step >= 4, step < 8))
    def _():
        unit_sum = jnp.zeros((1, slope_ref.shape[2]), f32)
        for n, (low, high) in enumerate(rows_of(slots, 208)):
            unit = dot(grad_low_ref[low:high, :], down_ref[0], NT) * slope_ref[0, low:high, :].astype(f32)
            unit = unit.astype(bf16)
            grad_unit[low:high, :] = unit
            unit_sum += jnp.sum(unit.astype(f32), axis=0, keepdims=True)
            total[low:high, :] += dot(unit, up_ref[0], NT)
            pump(range(4, 8), n)
        k = step - 4
        for at in range(4):

            @pl.when(k == at)
            def _():
                vectors[0, UNIT_ROW + at:UNIT_ROW + at + 1, :] = unit_sum
        keep_up[k] = dot(flipped[halves_of[0], :], grad_unit[...]).astype(bf16)
        for at in range(4):

            @pl.when(k == at)
            def _():
                down.given(at)
        give_up[k] = dot(flipped[halves_of[1], :], grad_unit[...]).astype(bf16)
        each_send(up, 0, [(k, 4 + k) for k in range(4)])
        pump(range(4, 8), 4)

    @pl.when(step == 7)
    def _():
        gain, attn_scale = constant(GAIN2), constant(ATTN_SCALE)

        def body(i, sums):
            here = pl.ds(pl.multiple_of(i * 64, 64), 64)
            valid, _, start = start_of(inputs_ref, column_ref, flag_ref, constant(TOKEN), here)
            grad_final = valid * grad_out_ref[here, :].astype(f32)
            grad_normed = total[here, :]
            _, scaled, inverse = layer_norm(middle_ref[here, :], gain, gain)
            grad_middle = grad_final + norm_back(grad_normed, scaled, inverse, gain)
            grad_branch1 = attn_scale * grad_middle
            grad_inputs_ref[here, :] = grad_middle
            grad_unit[here, :] = grad_branch1.astype(bf16)
            new = (grad_branch1, (middle_ref[here, :] - start) / attn_scale * grad_middle, grad_normed * scaled, grad_normed)
            return tuple(a + jnp.sum(b, axis=0, keepdims=True) for a, b in zip(sums, new))

        zero = jnp.zeros((1, width), f32)
        sums = lax.fori_loop(0, slots // 64, body, (zero,) * 4)
        for n in range(4):
            vectors[0, 3 + n:4 + n, :] = sums[n]
        total[...] = jnp.zeros_like(total)
        flipped[...] = normed1_ref[...].T

    attending = range(8, 12)
    shard_of = {8: 1, 9: 2, 10: 3, 11: 0}

    @pl.when(jnp.logical_and(step >= 8, step < 12))
    def _():
        k = lax.rem(step - 7, 4)
        grad_low1 = grad_unit
        for low in range(0, slots, 208):
            grad_mixed[low:low + 208, :] = dot(grad_low1[low:low + 208, :], proj_ref[0], NT).astype(bf16)
        value = dot(mixed_ref[0], grad_low1[...], TN).astype(bf16)
        rows = value.shape[0] // 2
        for own in (0, 1):

            @pl.when(core == own)
            def _():
                keep_proj[k] = value[own * rows:(own + 1) * rows]
                give_proj[k] = value[(1 - own) * rows:(2 - own) * rows]
        each_send(proj, 0, [(shard_of[at], at) for at in attending])
        tiles = windows(slots)
        bases = [head * triple for head in range(3)]
        owns = [slice(head * size, (head + 1) * size) for head in range(3)]
        for low, high, _, _ in tiles:
            for head, own in enumerate(owns):
                product = grad_mixed[low:high, own].astype(f32) * mixed_ref[0, low:high, own].astype(f32)
                delta[head:head + 1, low:high] = as_row(jnp.sum(product, axis=1, keepdims=True))
        grad_query[...] = jnp.zeros_like(grad_query)
        for unit, (low, high, begin, end) in enumerate(tiles):
            same = column_ref[low:high, :] == row_ref[:, begin:end]
            keys = [packed_ref[0, low:high, base + size:base + 2 * size] for base in bases]
            queries = [packed_ref[0, begin:end, base:base + size] * jnp.bfloat16(scale) for base in bases]
            grads = [grad_mixed[begin:end, own] for own in owns]
            scores = [dot(key, query, NT) for key, query in zip(keys, queries)]
            grad_shares = [
                dot(packed_ref[0, low:high, base + 2 * size:base + 3 * size], grad, NT)
                for base, grad in zip(bases, grads)
            ]
            shares = [
                jnp.exp(jnp.where(same, item - lse_ref[0, head:head + 1, begin:end], FLOOR_SCORE))
                for head, item in enumerate(scores)
            ]
            grad_scores = [
                (share * (item - delta[head:head + 1, begin:end])).astype(bf16)
                for head, (share, item) in enumerate(zip(shares, grad_shares))
            ]
            for head, base in enumerate(bases):
                grad_packed[low:high, base + size:base + 3 * size] = jnp.concatenate([
                    dot(grad_scores[head], queries[head]).astype(bf16),
                    dot(shares[head].astype(bf16), grads[head]).astype(bf16),
                ], axis=1)
                grad_query[head, begin:end, :] += dot(grad_scores[head], keys[head], TN)
            pump(attending, unit)
        for head, base in enumerate(bases):
            grad_packed[:, base:base + size] = (grad_query[head] * scale).astype(bf16)
        keep_heads[k] = dot(flipped[halves_of[0], :], grad_packed[...]).astype(bf16)
        give_heads[k] = dot(flipped[halves_of[1], :], grad_packed[...]).astype(bf16)
        each_send(heads, 0, [(shard_of[at], at) for at in attending])
        sums = jnp.sum(grad_packed[...].astype(f32), axis=0, keepdims=True)
        for at in range(4):

            @pl.when(k == at)
            def _():
                vectors[0, HEAD_ROW + at:HEAD_ROW + at + 1, :sums.shape[1]] = sums
        for low in range(0, slots, 208):
            total[low:low + 208, :] += dot(grad_packed[low:low + 208, :], heads_ref[0], NT)
        pump(attending, 7)

    @pl.when(step == 12)
    def _():
        gain = constant(GAIN1)

        def body(i, sums):
            here = pl.ds(pl.multiple_of(i * 64, 64), 64)
            valid, flagged, start = start_of(inputs_ref, column_ref, flag_ref, constant(TOKEN), here)
            _, scaled, inverse = layer_norm(start, gain, gain)
            grad_normed = total[here, :]
            grad_start = grad_inputs_ref[here, :] + norm_back(grad_normed, scaled, inverse, gain)
            grad_inputs_ref[here, :] = valid * (1.0 - flagged) * grad_start
            new = (valid * flagged * grad_start, grad_normed * scaled, grad_normed)
            return tuple(a + jnp.sum(b, axis=0, keepdims=True) for a, b in zip(sums, new))

        zero = jnp.zeros((1, width), f32)
        sums = (zero,) * 3
        for n, (low, high) in enumerate(((0, 4), (4, 8), (8, slots // 64))):
            sums = lax.fori_loop(low, high, body, sums)
            pump((12,), n)
        for n in range(3):
            vectors[0, n:n + 1, :] = sums[n]
        vector_copy(0).start()
        pump((12,), 3)
        for action in tail:
            action()
        last_level = len(levels)
        for k in (1, 2, 3):
            vector_copy(last_level + k - 1).wait_recv()
        mine = vectors[last_level]
        vector_ref[...] = mine + vector_tp[0] + vector_tp[1] + vector_tp[2]
        for row_at in (UNIT_ROW, HEAD_ROW):
            value = mine[row_at:row_at + 1]
            for k in (1, 2, 3):
                value += vector_tp[k - 1, row_at + k:row_at + k + 1, :]
            vector_ref[row_at:row_at + 1, :] = value
        for n in range(last_level + 3):
            vector_copy(n).wait_send()
        down.step6(1)
        for item in (up, heads, proj):
            item.step6()


def back(grad_low, hidden, slope, down, up, normed2, middle, grad_out, inputs, normed1, packed, mixed, lse,
         heads, proj, column, row, flag, constants, sums):
    slots, width = normed2.shape
    units, columns, part = hidden.shape[2], heads.shape[2], mixed.shape[2]
    levels = lax.axis_size("dp").bit_length() - 1
    clip = lambda low, high: lambda at: jnp.minimum(jnp.maximum(at, low), high)
    in_down, in_up = clip(0, 3), lambda at: clip(4, 7)(at) - 4
    in_heads = lambda at: lax.rem(clip(8, 11)(at) - 7, 4)
    tokens, anywhere = once(slots, width), pl.BlockSpec(memory_space=pl.ANY)
    shapes = [(units, width), (width, units), (width, columns), (part, width)]
    got = []
    for n, (rows, cols) in enumerate(shapes):
        eighth = (rows // 4, cols // 2) if n == 3 else (rows // 8, cols)
        got += [pltpu.VMEM((4, rows // 2, cols), bf16), pltpu.VMEM((4, rows // 4, cols), bf16),
                pltpu.VMEM((4,) + eighth, bf16), pltpu.VMEM((3,) + eighth, bf16), pltpu.VMEM(eighth, bf16)]
    half = [pltpu.VMEM((4, rows // 2, cols), bf16) for rows, cols in shapes]
    return pl.pallas_call(
        back_kernel,
        grid=(13,),
        in_specs=[
            tokens, each(slots, units, at=in_down), each(slots, units, at=in_up), each(units, width, at=in_up),
            each(width, units, at=in_up), tokens, tokens, tokens, tokens, tokens,
            each(slots, columns, at=in_heads), each(slots, part, at=in_heads), each(8, slots, at=in_heads),
            each(width, columns, at=in_heads), each(part, width, at=in_heads), once(slots, 1), once(1, slots),
            once(slots, 1), once(*constants.shape), once(8, width),
        ],
        out_specs=[once(slots, width), once(VECTORS, width), anywhere, anywhere, anywhere, anywhere],
        out_shape=[jax.ShapeDtypeStruct((slots, width), f32), jax.ShapeDtypeStruct((VECTORS, width), f32)]
        + [jax.ShapeDtypeStruct(shape, bf16) for shape in shapes],
        scratch_shapes=[
            pltpu.VMEM((slots, units), bf16), pltpu.VMEM((slots, width), f32), pltpu.VMEM((width, slots), bf16),
            pltpu.VMEM((slots, part), bf16), pltpu.VMEM((slots, columns), bf16), pltpu.VMEM((8, slots), f32),
            pltpu.VMEM((3, slots, columns // 9), f32),
        ] + half + [half[0]] + half[2:] + [
            pltpu.VMEM((levels + 1, VECTORS, width), f32), pltpu.VMEM((levels, VECTORS, width), f32),
            pltpu.VMEM((3, VECTORS, width), f32), pltpu.SemaphoreType.DMA((levels + 3,)),
            pltpu.SemaphoreType.DMA((levels + 3,)), pltpu.SemaphoreType.DMA((4,)),
        ] + got + [pltpu.SemaphoreType.DMA((Reduce.COPIES,))] * 8,
        compiler_params=pltpu.CompilerParams(vmem_limit_bytes=65400 << 10, collective_id=1, has_side_effects=True),
        cost_estimate=cost(36e9, 60e6, 12 * 480000),
        name="back",
    )(grad_low, hidden, slope, down, up, normed2, middle, grad_out, inputs, normed1, packed, mixed, lse,
      heads, proj, column, row, flag, constants, sums)


def local(
    inputs,
    segment_ids,
    mask_flags,
    mask_token,
    norm_gain,
    norm_shift,
    heads_weight,
    heads_bias,
    proj_weight,
    proj_bias,
    attn_scale,
    mlp_gain,
    mlp_shift,
    up_weight,
    up_bias,
    down_weight,
    down_bias,
    mlp_scale,
    grad_out,
):
    width = inputs.shape[1]
    triple = heads_weight.shape[2]
    head_size = triple // 3
    heads_here = heads_weight.shape[1]
    own_heads = heads_weight.reshape(width, -1)
    heads_cols = own_heads.shape[1]
    constants = jnp.concatenate([
        mask_token, norm_gain, norm_shift, proj_bias, attn_scale, mlp_gain, mlp_shift, down_bias, mlp_scale,
        jnp.zeros((7 * width,), bf16)]).astype(f32).reshape(16, width)
    (normed1, column, flag, row, packed, mixed, lse, middle, normed2, hidden, slope, output, grad_low2, sums_a,
     heads_all, up_all, proj_all, down_all) = forward(
        inputs, segment_ids, mask_flags, constants, heads_bias, up_bias.reshape(1, -1), grad_out, own_heads, up_weight,
        proj_weight, down_weight,
    )
    grad_inputs, small, sum_down, sum_up, sum_heads, sum_proj = back(
        grad_low2, hidden, slope, down_all, up_all, normed2, middle, grad_out, inputs, normed1, packed, mixed,
        lse, heads_all, proj_all, column, row, flag, constants, sums_a,
    )
    sum_down, sum_up, sum_proj = (item.astype(f32) for item in (sum_down, sum_up, sum_proj))
    sum_heads = sum_heads.astype(f32).reshape(heads_weight.shape)
    bias_sums = small[HEAD_ROW, :heads_cols].reshape(heads_here, triple)
    sum_heads_bias = jnp.concatenate([bias_sums[:, :head_size], bias_sums[:, 2 * head_size:]], axis=1)
    sum_up_bias = small[UNIT_ROW, :up_bias.shape[0]]
    (sum_token, sum_gain1, sum_shift1, sum_proj_bias, sum_scale1, sum_gain2, sum_shift2,
     sum_down_bias, sum_scale2) = [small[i] for i in range(9)]
    return (
        output,
        grad_inputs,
        sum_token,
        sum_gain1,
        sum_shift1,
        sum_heads,
        sum_heads_bias,
        sum_proj,
        sum_proj_bias,
        sum_scale1,
        sum_gain2,
        sum_shift2,
        sum_up,
        sum_up_bias,
        sum_down,
        sum_down_bias,
        sum_scale2,
    )


def solution(mesh):
    placed = (
        P(("dp", "tp"), None),
        P("dp", None),
        P(("dp", "tp"), None),
        P(),
        P(),
        P(),
        P(None, "tp", None),
        P("tp", None),
        P("tp", None),
        P(),
        P(),
        P(),
        P(),
        P(None, "tp"),
        P("tp"),
        P("tp", None),
        P(),
        P(),
        P(("dp", "tp"), None),
    )
    return jax.shard_map(
        local,
        mesh=mesh,
        in_specs=placed,
        out_specs=(
            P(("dp", "tp"), None),
            P(("dp", "tp"), None),
            P(),
            P(),
            P(),
            P(None, "tp", None),
            P("tp", None),
            P("tp", None),
            P(),
            P(),
            P(),
            P(),
            P(None, "tp"),
            P("tp"),
            P("tp", None),
            P(),
            P(),
        ),
        check_vma=False,
    )
```

```python
import functools

import jax
import jax.numpy as jnp
from jax import lax
from jax.experimental import pallas as pl
from jax.experimental.pallas import tpu as pltpu
from jax.sharding import PartitionSpec as P

EPSILON = 1e-06
FLOOR_SCORE = -1e30
SQRT_HALF = 0.7071067811865476
INV_ROOT_TWO_PI = 0.3989422804014327
LONGEST = 14 * 14 + 1
FIFTH_FROM = 4 * (11 * 11 + 1)
TILE = 128
CORE, X, Y = 1, 2, 4

f32, bf16 = jnp.float32, jnp.bfloat16
NN = (((1,), (0,)), ((), ()))
NT = (((1,), (1,)), ((), ()))
TN = (((0,), (0,)), ((), ()))


def dot(a, b, dims=NN):
    return lax.dot_general(a, b, dims, preferred_element_type=f32)


def layer_norm(values, gain, shift):
    centre = values - jnp.mean(values, axis=-1, keepdims=True)
    inverse = lax.rsqrt(jnp.mean(centre * centre, axis=-1, keepdims=True) + EPSILON)
    scaled = centre * inverse
    return (scaled * gain + shift, scaled, inverse)


def norm_back(grad_normed, scaled, inverse, gain):
    grad_scaled = grad_normed * gain
    first = jnp.mean(grad_scaled, axis=-1, keepdims=True)
    second = jnp.mean(grad_scaled * scaled, axis=-1, keepdims=True)
    return inverse * (grad_scaled - first - scaled * second)


def gelu_parts(inner):
    normal_cdf = 0.5 * (1.0 + lax.erf(inner * SQRT_HALF))
    density = jnp.exp(-0.5 * inner * inner) * INV_ROOT_TWO_PI
    return (inner * normal_cdf, normal_cdf + inner * density)


def windows(slots):
    out = []
    for low in range(0, slots, TILE):
        high = min(low + TILE, slots)
        begin = low - LONGEST + 1
        if low >= FIFTH_FROM:
            begin = min(begin, FIFTH_FROM)
        end = high + LONGEST - 1
        if high > FIFTH_FROM:
            end = slots
        begin = max(begin, 0) // 128 * 128
        end = min((end + 127) // 128 * 128, slots)
        out.append((low, high, begin, end))
    return out


def as_row(column):
    rows = column.shape[0]
    shape = (rows, rows)
    here = lax.broadcasted_iota(jnp.int32, shape, 0) == lax.broadcasted_iota(jnp.int32, shape, 1)
    return jnp.sum(jnp.where(here, column, 0.0), axis=0, keepdims=True)


def whole(*shape):
    return pl.BlockSpec(shape, lambda k: (0,) * len(shape))


def each(*shape, at=lambda k: k):
    return pl.BlockSpec((1,) + shape, lambda k: (at(k),) + (0,) * len(shape))


def params(megabytes):
    return pltpu.CompilerParams(vmem_limit_bytes=megabytes << 20)


def cost(flops, moved, exps=0):
    return pl.CostEstimate(flops=int(flops), transcendentals=int(exps), bytes_accessed=int(moved))


def start_of(inputs_ref, column_ref, flag_ref, token, here):
    valid = (column_ref[here, :] >= 0).astype(f32)
    flagged = (flag_ref[here, :] == 1).astype(f32)
    start = valid * (flagged * token + (1.0 - flagged) * inputs_ref[here, :].astype(f32))
    return valid, flagged, start


def blocks(columns, step=256):
    return [slice(low, min(low + step, columns)) for low in range(0, columns, step)]


def rows_of(slots, step=104):
    return [(low, min(low + step, slots)) for low in range(0, slots, step)]


def flip(index, bits):
    bit = 1
    while bit <= bits:
        if bits & bit:
            index = index + bit * (1 - 2 * lax.rem(lax.div(index, bit), 2))
        bit *= 2
    return index


class Gather:
    ROUTES = ("z", "x", "y", "fx", "fy", "c0", "c2", "c4", "c6")
    COPIES = 3 * len(ROUTES)

    def __init__(self, full_ref, by_columns, send_sems, recv_sems):
        self.dp, self.tp = lax.axis_index("dp"), lax.axis_index("tp")
        self.own = lax.rem(self.dp, 8)
        self.full, self.by_columns = full_ref, by_columns
        self.sends, self.recvs = send_sems, recv_sems
        _, rows, columns = full_ref.shape
        self.rows, self.columns = (rows // 4, columns // 2) if by_columns else (rows // 8, columns)
        self.half = self.rows // 32 * 16

    def piece(self, k, bits, half=None):
        place, columns = flip(self.own, bits), slice(None)
        if self.by_columns:
            columns = pl.ds(pl.multiple_of(lax.rem(place, 2) * self.columns, 128), self.columns)
            place = lax.div(place, 2)
        begin, height = place * self.rows, self.rows
        if half == 0:
            height = self.half
        elif half == 1:
            begin, height = begin + self.half, self.rows - self.half
        return self.full.at[k, pl.ds(pl.multiple_of(begin, 16), height), columns]

    def copy(self, k, route):
        if route == "z":
            source, target, to = self.piece(0, 0), self.piece(k, 0), (self.dp, flip(self.tp, k))
        else:
            bits, half, link = {
                "x": (0, None, X), "y": (0, None, Y), "fx": (Y, 1, X), "fy": (X, 0, Y),
                "c0": (0, None, CORE), "c2": (X, None, CORE), "c4": (Y, None, CORE), "c6": (X | Y, None, CORE),
            }[route]
            source = target = self.piece(k, bits, half)
            to = (flip(self.dp, link), self.tp)
        n = (k - 1) * len(self.ROUTES) + self.ROUTES.index(route)
        return pltpu.make_async_remote_copy(
            src_ref=source, dst_ref=target, send_sem=self.sends.at[n], recv_sem=self.recvs.at[n],
            device_id=to, device_id_type=pl.DeviceIdType.MESH,
        )

    def start(self, k, *routes):
        for route in routes:
            self.copy(k, route).start()

    def arrived(self, k, *routes):
        for route in routes:
            self.copy(k, route).wait_recv()

    def begin(self, k):
        self.start(k, "z")

    def step1(self, k):
        self.arrived(k, "z")
        self.start(k, "x", "y", "c0")

    def step2(self, k):
        self.arrived(k, "x")
        self.start(k, "fy", "c2")
        self.arrived(k, "y")
        self.start(k, "fx", "c4")

    def step3(self, k):
        self.arrived(k, "fx", "fy")
        self.start(k, "c6")

    def step4(self, k):
        self.arrived(k, "c0", "c2", "c4", "c6")

    def sent(self):
        for k in (1, 2, 3):
            for route in self.ROUTES:
                self.copy(k, route).wait_send()


def meet(peers):
    barrier = pltpu.get_barrier_semaphore()
    for peer in peers:
        pl.semaphore_signal(barrier, inc=1, device_id=peer, device_id_type=pl.DeviceIdType.MESH)
    pl.semaphore_wait(barrier, len(peers))


def as_column(row):
    size = row.shape[1]
    shape = (size, size)
    here = lax.broadcasted_iota(jnp.int32, shape, 0) == lax.broadcasted_iota(jnp.int32, shape, 1)
    return jnp.sum(jnp.where(here, row, 0), axis=1, keepdims=True)


def dispatch(table, step, steps, unit):
    for at in steps:
        if table.get((at, unit)):

            @pl.when(step == at)
            def _():
                for action in table[(at, unit)]:
                    action()


TOKEN, GAIN1, SHIFT1, PROJ_BIAS, ATTN_SCALE, GAIN2, SHIFT2, DOWN_BIAS, MLP_SCALE = range(9)

HEADS, UP, PROJ, DOWN = range(4)
FORWARD_PLAN = {
    (0, 1): ((HEADS, (1, 2), 1),),
    (0, 6): ((HEADS, (3,), 1), (HEADS, (1,), 2),),
    (1, -1): ((PROJ, (1, 2, 3), 0), (UP, (1, 2, 3), 0), (HEADS, (2, 3), 2), (PROJ, (1,), 1), (HEADS, (1, 2), 3), (PROJ, (2, 3), 1), (HEADS, (3,), 3), (HEADS, (1,), 4),),
    (1, 1): ((HEADS, (2,), 4), (PROJ, (1, 2), 2), (UP, (1,), 1),),
    (1, 3): ((HEADS, (3,), 4), (PROJ, (3,), 2),),
    (1, 6): ((DOWN, (1, 2, 3), 0), (UP, (2,), 1), (PROJ, (1, 2), 3),),
    (2, 1): ((UP, (1,), 2), (PROJ, (3,), 3), (UP, (3,), 1), (PROJ, (1, 2), 4),),
    (2, 3): ((DOWN, (1,), 1),),
    (2, 6): ((UP, (2,), 2), (PROJ, (3,), 4), (UP, (1,), 3),),
    (3, 1): ((DOWN, (2,), 1), (UP, (3,), 2),),
    (3, 3): ((UP, (1,), 4),),
    (3, 6): ((DOWN, (1,), 2), (DOWN, (3,), 1), (UP, (2,), 3),),
    (4, 1): ((UP, (2,), 4), (UP, (3,), 3), (DOWN, (2,), 2),),
    (4, 3): ((DOWN, (1,), 3),),
    (5, -1): ((DOWN, (3,), 2), (UP, (3,), 4), (DOWN, (2,), 3), (DOWN, (1,), 4),),
    (5, 3): ((DOWN, (3,), 3), (DOWN, (2,), 4),),
    (6, 3): ((DOWN, (3,), 4),),
}


def forward_kernel(
    inputs_ref, segment_ref, mask_ref, heads_bias_ref, unit_bias_ref, grad_out_ref,
    heads_ref, up_ref, proj_ref, down_ref, *rest,
):
    vector_refs, rest = rest[:9], rest[9:]
    (normed1_ref, column_ref, flag_ref, row_ref, packed_ref, mixed_ref, lse_ref, middle_ref, normed2_ref, hidden_ref,
     slope_ref, output_ref, grad_low_ref, sums_ref, vectors_ref, heads_all, up_all, proj_all, down_all,
     heads_now, up_now, proj_now, down_now, head_bias, unit_bias, mixed_all, total,
     own_sems, store_sems, bias_sends, bias_recvs, *sems) = rest
    slots = inputs_ref.shape[0]
    triple = heads_now.shape[2] // 3
    size = triple // 3
    scale = size ** (-0.5)
    part = mixed_ref.shape[2]
    step = pl.program_id(0)
    vector = lambda n: vectors_ref[n:n + 1, :]
    shards, fulls = (heads_ref, up_ref, proj_ref, down_ref), (heads_all, up_all, proj_all, down_all)
    nows = (heads_now, up_now, proj_now, down_now)
    gathers = [Gather(nows[n], n == PROJ, sems[2 * n], sems[2 * n + 1]) for n in range(4)]
    dp, tp = gathers[0].dp, gathers[0].tp
    loads = [pltpu.make_async_copy(shards[n], nows[n].at[0], own_sems.at[n]) for n in range(4)]
    store = lambda n, k: pltpu.make_async_copy(nows[n].at[k], fulls[n].at[k], store_sems.at[n, k])

    def bias_copy(n, k):
        item = (head_bias, unit_bias)[n]
        return pltpu.make_async_remote_copy(
            src_ref=item.at[0], dst_ref=item.at[k], send_sem=bias_sends.at[n, k], recv_sem=bias_recvs.at[n, k],
            device_id=(dp, flip(tp, k)), device_id_type=pl.DeviceIdType.MESH,
        )

    table = {}
    for key, entries in FORWARD_PLAN.items():
        table[key] = []
        for n, ks, action in entries:
            item = gathers[n]
            for k in ks:
                table[key].append(functools.partial(
                    (item.begin, item.step1, item.step2, item.step3, item.step4)[action], k))
                if action == 4:
                    table[key].append(store(n, k).start)

    @pl.when(step == 0)
    def _():
        for load in loads:
            load.start()
        meet([(dp, flip(tp, k)) for k in (1, 2, 3)] + [(flip(dp, bit), tp) for bit in (X, Y, CORE)])
        loads[HEADS].wait()
        for k in (1, 2, 3):
            gathers[HEADS].begin(k)
        vectors_ref[...] = jnp.zeros_like(vectors_ref)
        for n, ref in enumerate(vector_refs):
            vectors_ref[n:n + 1, :] = ref[...].astype(f32).reshape(1, -1)
        blank = jnp.zeros((1, size), f32)
        pieces = []
        for head in range(3):
            here = heads_bias_ref[head:head + 1, :].astype(f32)
            pieces += [here[:, :size], blank, here[:, size:]]
        head_bias[0] = jnp.broadcast_to(jnp.concatenate(pieces, axis=1), head_bias.shape[1:])
        unit_bias[0] = jnp.broadcast_to(unit_bias_ref[...].astype(f32).reshape(1, -1), unit_bias.shape[1:])
        for n in range(2):
            for k in (1, 2, 3):
                bias_copy(n, k).start()
        row_ref[...] = segment_ref[pl.ds(tp, 1), :]
        for low in range(0, slots, 128):
            high = min(low + 128, slots)
            column_ref[low:high, :] = as_column(row_ref[:, low:high])
            flag_ref[low:high, :] = as_column(mask_ref[:, low:high])

        def body(i, carry):
            here = pl.ds(pl.multiple_of(i * 64, 64), 64)
            _, _, start = start_of(inputs_ref, column_ref, flag_ref, vector(TOKEN), here)
            normed1_ref[here, :] = layer_norm(start, vector(GAIN1), vector(SHIFT1))[0].astype(bf16)
            return carry

        lax.fori_loop(0, slots // 64, body, 0)
        for load in loads[1:]:
            load.wait()
        for n in range(4):
            store(n, 0).start()

    @pl.when(step == 1)
    def _():
        for k in (1, 2, 3):
            bias_copy(0, k).wait_recv()

    dispatch(table, step, range(1, 8), -1)

    @pl.when(step < 4)
    def _():
        for low in range(0, slots, 208):
            product = dot(normed1_ref[low:low + 208, :], heads_now[step])
            packed_ref[0, low:low + 208, :] = (product + head_bias[step, 0:1, :]).astype(bf16)
        lse_ref[...] = jnp.zeros_like(lse_ref)
        bases = [head * triple for head in range(3)]
        for unit, (low, high, begin, end) in enumerate(windows(slots)):
            same = column_ref[low:high, :] == row_ref[:, begin:end]
            scores = [
                dot(packed_ref[0, low:high, base:base + size] * jnp.bfloat16(scale),
                    packed_ref[0, begin:end, base + size:base + 2 * size], NT)
                for base in bases
            ]
            scores = [jnp.where(same, item, FLOOR_SCORE) for item in scores]
            largest = [jnp.max(item, axis=1, keepdims=True) for item in scores]
            raised = [jnp.exp(item - top) for item, top in zip(scores, largest)]
            totals = [jnp.sum(item, axis=1, keepdims=True) for item in raised]
            mixed = [
                dot(item.astype(bf16), packed_ref[0, begin:end, base + 2 * size:base + 3 * size])
                for item, base in zip(raised, bases)
            ]
            mixed = [(item * (1.0 / total)).astype(bf16) for item, total in zip(mixed, totals)]
            mixed_ref[0, low:high, :] = jnp.concatenate(mixed, axis=1)
            for head in range(3):
                lse_ref[0, head:head + 1, low:high] = as_row(largest[head] + jnp.log(totals[head]))
            dispatch(table, step, range(4), unit)

    for k in range(4):

        @pl.when(step == k)
        def _():
            mixed_all[:, k * part:(k + 1) * part] = mixed_ref[0]

    @pl.when(step == 4)
    def _():
        for k in (1, 2, 3):
            bias_copy(1, k).wait_recv()
        total[...] = jnp.zeros_like(total)
        proj = proj_now[...].reshape(-1, proj_now.shape[2])
        for low, high in rows_of(slots, 208):
            middle_ref[low:high, :] = dot(mixed_all[low:high, :], proj) + vector(PROJ_BIAS)

        def body(i, carry):
            here = pl.ds(pl.multiple_of(i * 64, 64), 64)
            _, _, start = start_of(inputs_ref, column_ref, flag_ref, vector(TOKEN), here)
            middle = start + vector(ATTN_SCALE) * middle_ref[here, :]
            middle_ref[here, :] = middle
            normed2_ref[here, :] = layer_norm(middle, vector(GAIN2), vector(SHIFT2))[0].astype(bf16)
            return carry

        lax.fori_loop(0, slots // 64, body, 0)

    @pl.when(step >= 4)
    def _():
        k = step - 4
        for unit, (low, high) in enumerate(rows_of(slots, 208)):
            for columns in blocks(hidden_ref.shape[2]):
                inner = dot(normed2_ref[low:high, :], up_now[k, :, columns]) + unit_bias[k, 0:1, columns]
                value, slope = gelu_parts(inner)
                hidden_ref[0, low:high, columns] = value.astype(bf16)
                slope_ref[0, low:high, columns] = slope.astype(bf16)
            total[low:high, :] += dot(hidden_ref[0, low:high, :], down_now[k])
            dispatch(table, step, range(4, 8), unit)

    @pl.when(step == 7)
    def _():
        def body(i, sums):
            here = pl.ds(pl.multiple_of(i * 64, 64), 64)
            valid = (column_ref[here, :] >= 0).astype(f32)
            branch2 = total[here, :] + vector(DOWN_BIAS)
            output_ref[here, :] = (valid * (middle_ref[here, :] + vector(MLP_SCALE) * branch2)).astype(bf16)
            grad_final = valid * grad_out_ref[here, :].astype(f32)
            grad_branch2 = vector(MLP_SCALE) * grad_final
            grad_low_ref[here, :] = grad_branch2.astype(bf16)
            return tuple(a + jnp.sum(b, axis=0, keepdims=True) for a, b in zip(sums, (branch2 * grad_final, grad_branch2)))

        zero = jnp.zeros((1, inputs_ref.shape[1]), f32)
        sums = lax.fori_loop(0, slots // 64, body, (zero, zero))
        sums_ref[...] = jnp.zeros_like(sums_ref)
        sums_ref[0:1, :], sums_ref[1:2, :] = sums
        for n, item in enumerate(gathers):
            item.sent()
            for k in range(4):
                store(n, k).wait()
        for n in range(2):
            for k in (1, 2, 3):
                bias_copy(n, k).wait_send()


def once(*shape):
    return pl.BlockSpec(shape, lambda at: (0,) * len(shape), pipeline_mode=pl.Buffered(1))


def forward(inputs, segments, mask, vectors, heads_bias, unit_bias, grad_out, heads, up, proj, down):
    slots, width = inputs.shape
    columns, units = heads.shape[1], up.shape[1]
    part = columns // 3
    anywhere = pl.BlockSpec(memory_space=pl.ANY)
    early = lambda at: jnp.minimum(at, 3)
    late = lambda at: jnp.maximum(at - 4, 0)
    tokens = once(slots, width)
    shape = jax.ShapeDtypeStruct
    return pl.pallas_call(
        forward_kernel,
        grid=(8,),
        in_specs=[
            tokens, once(*segments.shape), once(1, slots), once(*heads_bias.shape),
            once(*unit_bias.shape), tokens, anywhere, anywhere, anywhere, anywhere,
        ] + [once(width)] * len(vectors),
        out_specs=[
            tokens, once(slots, 1), once(slots, 1), once(1, slots), each(slots, columns, at=early),
            each(slots, part, at=early), each(8, slots, at=early), tokens, tokens, each(slots, units, at=late),
            each(slots, units, at=late), tokens, tokens, once(8, width), once(16, width), anywhere, anywhere, anywhere, anywhere,
        ],
        out_shape=[
            shape((slots, width), bf16), shape((slots, 1), jnp.int32), shape((slots, 1), jnp.int32),
            shape((1, slots), jnp.int32), shape((4, slots, columns), bf16), shape((4, slots, part), bf16),
            shape((4, 8, slots), f32), shape((slots, width), f32), shape((slots, width), bf16),
            shape((4, slots, units), bf16), shape((4, slots, units), bf16), shape((slots, width), bf16),
            shape((slots, width), bf16), shape((8, width), f32), shape((16, width), f32),
        ] + [shape((4,) + item.shape, bf16) for item in (heads, up, proj, down)],
        scratch_shapes=[
            pltpu.VMEM((4,) + heads.shape, bf16), pltpu.VMEM((4,) + up.shape, bf16), pltpu.VMEM((4,) + proj.shape, bf16),
            pltpu.VMEM((4,) + down.shape, bf16), pltpu.VMEM((4, 8, columns), f32), pltpu.VMEM((4, 8, units), f32),
            pltpu.VMEM((slots, width), bf16), pltpu.VMEM((slots, width), f32),
            pltpu.SemaphoreType.DMA((4,)), pltpu.SemaphoreType.DMA((4, 4)), pltpu.SemaphoreType.DMA((2, 4)), pltpu.SemaphoreType.DMA((2, 4)),
        ] + [pltpu.SemaphoreType.DMA((Gather.COPIES,))] * 8,
        compiler_params=pltpu.CompilerParams(vmem_limit_bytes=60 << 20, collective_id=0, has_side_effects=True),
        cost_estimate=cost(26e9, 60e6, 6e6),
        name="forward",
    )(inputs, segments, mask, heads_bias, unit_bias, grad_out, heads, up, proj, down, *vectors)


class Reduce:
    COPIES = 4 * 4 + 7

    def __init__(self, first, second, by_columns, keep, give, got, out, send_sems, recv_sems, own_sem):
        self.dp, self.tp = lax.axis_index("dp"), lax.axis_index("tp")
        self.first, self.second, self.by_columns = first, second, by_columns
        self.keep, self.give, self.out = keep, give, out
        self.got0, self.got1, self.got2, self.got_tp, self.total = got
        self.sends, self.recvs, self.own_sem = send_sems, recv_sems, own_sem
        self.rows, self.columns = keep.shape[1] * 2, keep.shape[2]
        self.bits = tuple(lax.rem(lax.div(self.dp, bit), 2) for bit in (CORE, first, second))

    def quarter(self, first):
        rows = self.rows // 4
        return pl.multiple_of(first * rows, 16), rows

    def eighth(self, first, second):
        begin, rows = self.quarter(first)
        if self.by_columns:
            width = self.columns // 2
            return begin, rows, pl.ds(pl.multiple_of(second * width, 128), width)
        return pl.multiple_of(begin + second * (rows // 2), 16), rows // 2, slice(None)

    def part(self, ref, spot):
        begin, rows, columns = spot
        return ref.at[pl.ds(begin, rows), columns]

    def place(self, flips):
        core, first, second = (1 - bit if turned else bit for bit, turned in zip(self.bits, flips))
        begin, rows, columns = self.eighth(first, second)
        return self.out.at[pl.ds(pl.multiple_of(core * (self.rows // 2) + begin, 16), rows), columns]

    def remote(self, n, source, target, bits=0, k=0):
        return pltpu.make_async_remote_copy(
            src_ref=source, dst_ref=target, send_sem=self.sends.at[n], recv_sem=self.recvs.at[n],
            device_id=(flip(self.dp, bits), flip(self.tp, k)), device_id_type=pl.DeviceIdType.MESH,
        )

    def copy(self, k, level):
        core, first, second = self.bits
        n = 4 * k + level
        if level == 0:
            return self.remote(n, self.give.at[k], self.got0.at[k], CORE)
        if level == 1:
            begin, rows = self.quarter(1 - first)
            return self.remote(n, self.keep.at[k, pl.ds(begin, rows), :], self.got1.at[k], self.first)
        if level == 2:
            return self.remote(n, self.part(self.keep.at[k], self.eighth(first, 1 - second)), self.got2.at[k], self.second)
        return self.remote(n, self.part(self.keep.at[k], self.eighth(first, second)), self.got_tp.at[k - 1], 0, k)

    def share(self, n):
        first, second = self.first, self.second
        bits, source = (
            (first, (0, 0, 0)), (second, (0, 0, 0)), (first | second, (0, 0, 0)), (CORE, (0, 0, 0)),
            (CORE, (0, 1, 0)), (CORE, (0, 0, 1)), (CORE, (0, 1, 1)),
        )[n]
        place = self.place(source)
        return self.remote(16 + n, self.total if n < 4 else place, place, bits)

    def add(self, target, begin, rows, columns, *items):
        step = 48

        def body(i, carry):
            here = pl.ds(pl.multiple_of(begin + i * step, 16), step)
            there = pl.ds(pl.multiple_of(i * step, 16), step)
            if len(items) == 1:
                target[here, columns] = target[here, columns] + items[0][there, :]
            else:
                total = target[here, columns].astype(f32)
                for item in items:
                    total += item[there, :].astype(f32)
                target[here, columns] = total.astype(bf16)
            return carry

        lax.fori_loop(0, rows // step, body, 0)

    def step0(self, k):
        self.copy(k, 0).start()

    def given(self, k):
        self.copy(k, 0).wait_send()

    def step1(self, k):
        self.copy(k, 0).wait_recv()
        self.add(self.keep.at[k], 0, self.rows // 2, slice(None), self.got0.at[k])
        self.copy(k, 1).start()

    def step2(self, k):
        self.copy(k, 1).wait_recv()
        begin, rows = self.quarter(self.bits[1])
        self.add(self.keep.at[k], begin, rows, slice(None), self.got1.at[k])
        self.copy(k, 2).start()

    def step3(self, k):
        self.copy(k, 2).wait_recv()
        self.add(self.keep.at[k], *self.eighth(*self.bits[1:]), self.got2.at[k])
        if k:
            self.copy(k, 3).start()

    def step4(self):
        for k in (1, 2, 3):
            self.copy(k, 3).wait_recv()
        begin, rows, columns = self.eighth(*self.bits[1:])
        self.add(self.keep.at[0], begin, rows, columns, *[self.got_tp.at[k] for k in range(3)])
        self.total[...] = self.keep[0, pl.ds(begin, rows), columns]
        for n in range(4):
            self.share(n).start()
        self.own_copy().start()

    def own_copy(self):
        return pltpu.make_async_copy(self.total, self.place((0, 0, 0)), self.own_sem)

    def step5(self):
        for n in range(3):
            self.share(n).wait_recv()
            self.share(4 + n).start()

    def step6(self, lowest=0):
        for n in range(3, 7):
            self.share(n).wait_recv()
        for n in range(7):
            self.share(n).wait_send()
        for k in range(4):
            for level in range(lowest, 4 if k else 3):
                self.copy(k, level).wait_send()
        self.own_copy().wait()


VECTORS = 24
UNIT_ROW, HEAD_ROW = 9, 13


VECTOR = 4
BACK_PLAN = {
    (3, 0): ((DOWN, 0, 1),),
    (4, 1): ((DOWN, 1, 1), (DOWN, 2, 1),),
    (4, 3): ((DOWN, 3, 1),),
    (5, 3): ((DOWN, 0, 2), (UP, 0, 1),),
    (6, 1): ((DOWN, 1, 2),),
    (6, 3): ((UP, 1, 1), (DOWN, 0, 3),),
    (7, 1): ((DOWN, 2, 2),),
    (7, 3): ((UP, 2, 1), (UP, 0, 2),),
    (8, 1): ((DOWN, 1, 3), (DOWN, 3, 2), (UP, 3, 1), (UP, 0, 3), (UP, 1, 2),),
    (8, 3): ((DOWN, 2, 3), (PROJ, 1, 1),),
    (8, 7): ((UP, 2, 2), (UP, 1, 3),),
    (9, 1): ((DOWN, 3, 3), (HEADS, 1, 1),),
    (9, 3): ((PROJ, 2, 1), (UP, 2, 3),),
    (9, 6): ((UP, 3, 2), (PROJ, 1, 2),),
    (9, 7): ((PROJ, 2, 2),),
    (10, 1): ((HEADS, 1, 2), (DOWN, 0, 4), (HEADS, 2, 1), (UP, 3, 3),),
    (10, 3): ((PROJ, 1, 3), (PROJ, 3, 1), (PROJ, 2, 3),),
    (10, 6): ((HEADS, 1, 3),),
    (11, 1): ((UP, 0, 4), (HEADS, 3, 1), (DOWN, 0, 5),),
    (11, 3): ((PROJ, 3, 2), (PROJ, 0, 1), (HEADS, 2, 2),),
    (12, 1): ((UP, 0, 5), (PROJ, 0, 2),),
    (12, 2): ((HEADS, 0, 1),),
}
BACK_TAIL = (
    (HEADS, 2, 3),
    (HEADS, 3, 2),
    (PROJ, 3, 3),
    (PROJ, 0, 3),
    (VECTOR, 0, 0),
    (HEADS, 3, 3),
    (HEADS, 0, 2),
    (VECTOR, 1, 0),
    (PROJ, 0, 4),
    (HEADS, 0, 3),
    (HEADS, 0, 4),
    (VECTOR, 2, 0),
    (PROJ, 0, 5),
    (HEADS, 0, 5),
)


def back_kernel(
    grad_low_ref, hidden_ref, slope_ref, down_ref, up_ref, normed2_ref, middle_ref, grad_out_ref,
    inputs_ref, normed1_ref, packed_ref, mixed_ref, lse_ref, heads_ref, proj_ref, column_ref, row_ref, flag_ref,
    constants_ref, sums_ref,
    grad_inputs_ref, vector_ref, out_down, out_up, out_heads, out_proj,
    grad_unit, total, flipped, grad_mixed, grad_packed, delta, grad_query,
    keep_down, keep_up, keep_heads, keep_proj, give_down, give_heads, give_proj,
    vectors, vector_got, vector_tp, vector_sends, vector_recvs, own_sems,
    *rest,
):
    slots, width = normed2_ref.shape
    triple = heads_ref.shape[2] // 3
    size = triple // 3
    scale = size ** (-0.5)
    step = pl.program_id(0)
    got, sems = [rest[5 * n:5 * n + 5] for n in range(4)], rest[20:]
    give_up = give_down
    constant = lambda n: constants_ref[n:n + 1, :]
    make = lambda n, first, second, by_columns, keep, give, out: Reduce(
        first, second, by_columns, keep, give, got[n], out, sems[2 * n], sems[2 * n + 1], own_sems.at[n])
    down = make(0, X, Y, False, keep_down, give_down, out_down)
    up = make(1, Y, X, False, keep_up, give_up, out_up)
    heads = make(2, X, Y, False, keep_heads, give_heads, out_heads)
    proj = make(3, Y, X, True, keep_proj, give_proj, out_proj)
    dp, tp, core = down.dp, down.tp, down.bits[0]
    n_dp = lax.axis_size("dp")
    levels = [bit for bit in (1, 2, 4, 8, 16, 32, 64, 128) if bit < n_dp]

    def vector_copy(n):
        if n < len(levels):
            return heads_like(vectors.at[n], vector_got.at[n], n, levels[n], 0)
        k = n - len(levels) + 1
        return heads_like(vectors.at[len(levels)], vector_tp.at[k - 1], n, 0, k)

    def heads_like(source, target, n, bits, k):
        return pltpu.make_async_remote_copy(
            src_ref=source, dst_ref=target, send_sem=vector_sends.at[n], recv_sem=vector_recvs.at[n],
            device_id=(flip(dp, bits), flip(tp, k)), device_id_type=pl.DeviceIdType.MESH,
        )

    def vector_step(n):
        vector_copy(n).wait_recv()
        vectors[n + 1] = vectors[n] + vector_got[n]
        if n + 1 < len(levels):
            vector_copy(n + 1).start()
        else:
            for k in (1, 2, 3):
                vector_copy(len(levels) + k - 1).start()

    def action_of(entry):
        item, k, part = entry
        if item == VECTOR:
            return functools.partial(vector_step, k)
        item = {HEADS: heads, UP: up, PROJ: proj, DOWN: down}[item]
        if part > 3:
            return (item.step4, item.step5)[part - 4]
        return functools.partial((item.step1, item.step2, item.step3)[part - 1], k)

    table = {key: [action_of(entry) for entry in entries] for key, entries in BACK_PLAN.items()}
    tail = [action_of(entry) for entry in BACK_TAIL]
    tail += [functools.partial(vector_step, n) for n in range(3, len(levels))]

    def pump(steps, unit):
        for at in steps:
            if (at, unit) in table:

                @pl.when(step == at)
                def _():
                    for action in table[(at, unit)]:
                        action()

    def each_send(item, place, steps):
        for k, at in steps:

            @pl.when(step == at)
            def _():
                item.step0(k)

    halves_of = (pl.ds(pl.multiple_of(core * (width // 2), 128), width // 2),
                 pl.ds(pl.multiple_of((1 - core) * (width // 2), 128), width // 2))

    @pl.when(step == 0)
    def _():
        vectors[0] = jnp.zeros_like(vectors[0])
        vectors[0, 7:8, :] = sums_ref[1:2, :]
        vectors[0, 8:9, :] = sums_ref[0:1, :]
        peers = [(dp, flip(tp, k)) for k in (1, 2, 3)]
        peers += [(flip(dp, bits), tp) for bits in (X, Y, X | Y, CORE)]
        peers += [(flip(dp, bit), tp) for bit in levels if bit >= 8]
        meet(peers)

    @pl.when(step < 4)
    def _():
        keep_down[step] = dot(hidden_ref[0, :, halves_of[0]], grad_low_ref[...], TN).astype(bf16)
        give_down[step] = dot(hidden_ref[0, :, halves_of[1]], grad_low_ref[...], TN).astype(bf16)
        each_send(down, 0, [(k, k) for k in range(4)])
        pump(range(4), 0)

    @pl.when(step == 4)
    def _():
        total[...] = jnp.zeros_like(total)
        flipped[...] = normed2_ref[...].T

    @pl.when(jnp.logical_and(step >= 4, step < 8))
    def _():
        unit_sum = jnp.zeros((1, slope_ref.shape[2]), f32)
        for n, (low, high) in enumerate(rows_of(slots, 208)):
            unit = dot(grad_low_ref[low:high, :], down_ref[0], NT) * slope_ref[0, low:high, :].astype(f32)
            unit = unit.astype(bf16)
            grad_unit[low:high, :] = unit
            unit_sum += jnp.sum(unit.astype(f32), axis=0, keepdims=True)
            total[low:high, :] += dot(unit, up_ref[0], NT)
            pump(range(4, 8), n)
        k = step - 4
        for at in range(4):

            @pl.when(k == at)
            def _():
                vectors[0, UNIT_ROW + at:UNIT_ROW + at + 1, :] = unit_sum
        keep_up[k] = dot(flipped[halves_of[0], :], grad_unit[...]).astype(bf16)
        for at in range(4):

            @pl.when(k == at)
            def _():
                down.given(at)
        give_up[k] = dot(flipped[halves_of[1], :], grad_unit[...]).astype(bf16)
        each_send(up, 0, [(k, 4 + k) for k in range(4)])
        pump(range(4, 8), 4)

    @pl.when(step == 7)
    def _():
        gain, attn_scale = constant(GAIN2), constant(ATTN_SCALE)

        def body(i, sums):
            here = pl.ds(pl.multiple_of(i * 64, 64), 64)
            valid, _, start = start_of(inputs_ref, column_ref, flag_ref, constant(TOKEN), here)
            grad_final = valid * grad_out_ref[here, :].astype(f32)
            grad_normed = total[here, :]
            _, scaled, inverse = layer_norm(middle_ref[here, :], gain, gain)
            grad_middle = grad_final + norm_back(grad_normed, scaled, inverse, gain)
            grad_branch1 = attn_scale * grad_middle
            grad_inputs_ref[here, :] = grad_middle
            grad_unit[here, :] = grad_branch1.astype(bf16)
            new = (grad_branch1, (middle_ref[here, :] - start) / attn_scale * grad_middle, grad_normed * scaled, grad_normed)
            return tuple(a + jnp.sum(b, axis=0, keepdims=True) for a, b in zip(sums, new))

        zero = jnp.zeros((1, width), f32)
        sums = lax.fori_loop(0, slots // 64, body, (zero,) * 4)
        for n in range(4):
            vectors[0, 3 + n:4 + n, :] = sums[n]
        total[...] = jnp.zeros_like(total)
        flipped[...] = normed1_ref[...].T

    attending = range(8, 12)
    shard_of = {8: 1, 9: 2, 10: 3, 11: 0}

    @pl.when(jnp.logical_and(step >= 8, step < 12))
    def _():
        k = lax.rem(step - 7, 4)
        grad_low1 = grad_unit
        for low in range(0, slots, 208):
            grad_mixed[low:low + 208, :] = dot(grad_low1[low:low + 208, :], proj_ref[0], NT).astype(bf16)
        value = dot(mixed_ref[0], grad_low1[...], TN).astype(bf16)
        rows = value.shape[0] // 2
        for own in (0, 1):

            @pl.when(core == own)
            def _():
                keep_proj[k] = value[own * rows:(own + 1) * rows]
                give_proj[k] = value[(1 - own) * rows:(2 - own) * rows]
        each_send(proj, 0, [(shard_of[at], at) for at in attending])
        tiles = windows(slots)
        bases = [head * triple for head in range(3)]
        owns = [slice(head * size, (head + 1) * size) for head in range(3)]
        for low, high, _, _ in tiles:
            for head, own in enumerate(owns):
                product = grad_mixed[low:high, own].astype(f32) * mixed_ref[0, low:high, own].astype(f32)
                delta[head:head + 1, low:high] = as_row(jnp.sum(product, axis=1, keepdims=True))
        grad_query[...] = jnp.zeros_like(grad_query)
        for unit, (low, high, begin, end) in enumerate(tiles):
            same = column_ref[low:high, :] == row_ref[:, begin:end]
            keys = [packed_ref[0, low:high, base + size:base + 2 * size] for base in bases]
            queries = [packed_ref[0, begin:end, base:base + size] * jnp.bfloat16(scale) for base in bases]
            grads = [grad_mixed[begin:end, own] for own in owns]
            scores = [dot(key, query, NT) for key, query in zip(keys, queries)]
            grad_shares = [
                dot(packed_ref[0, low:high, base + 2 * size:base + 3 * size], grad, NT)
                for base, grad in zip(bases, grads)
            ]
            shares = [
                jnp.exp(jnp.where(same, item - lse_ref[0, head:head + 1, begin:end], FLOOR_SCORE))
                for head, item in enumerate(scores)
            ]
            grad_scores = [
                (share * (item - delta[head:head + 1, begin:end])).astype(bf16)
                for head, (share, item) in enumerate(zip(shares, grad_shares))
            ]
            for head, base in enumerate(bases):
                grad_packed[low:high, base + size:base + 3 * size] = jnp.concatenate([
                    dot(grad_scores[head], queries[head]).astype(bf16),
                    dot(shares[head].astype(bf16), grads[head]).astype(bf16),
                ], axis=1)
                grad_query[head, begin:end, :] += dot(grad_scores[head], keys[head], TN)
            pump(attending, unit)
        for head, base in enumerate(bases):
            grad_packed[:, base:base + size] = (grad_query[head] * scale).astype(bf16)
        keep_heads[k] = dot(flipped[halves_of[0], :], grad_packed[...]).astype(bf16)
        give_heads[k] = dot(flipped[halves_of[1], :], grad_packed[...]).astype(bf16)
        each_send(heads, 0, [(shard_of[at], at) for at in attending])
        sums = jnp.sum(grad_packed[...].astype(f32), axis=0, keepdims=True)
        for at in range(4):

            @pl.when(k == at)
            def _():
                vectors[0, HEAD_ROW + at:HEAD_ROW + at + 1, :sums.shape[1]] = sums
        for low in range(0, slots, 208):
            total[low:low + 208, :] += dot(grad_packed[low:low + 208, :], heads_ref[0], NT)
        pump(attending, 7)

    @pl.when(step == 12)
    def _():
        gain = constant(GAIN1)

        def body(i, sums):
            here = pl.ds(pl.multiple_of(i * 64, 64), 64)
            valid, flagged, start = start_of(inputs_ref, column_ref, flag_ref, constant(TOKEN), here)
            _, scaled, inverse = layer_norm(start, gain, gain)
            grad_normed = total[here, :]
            grad_start = grad_inputs_ref[here, :] + norm_back(grad_normed, scaled, inverse, gain)
            grad_inputs_ref[here, :] = valid * (1.0 - flagged) * grad_start
            new = (valid * flagged * grad_start, grad_normed * scaled, grad_normed)
            return tuple(a + jnp.sum(b, axis=0, keepdims=True) for a, b in zip(sums, new))

        zero = jnp.zeros((1, width), f32)
        sums = (zero,) * 3
        for n, (low, high) in enumerate(((0, 4), (4, 8), (8, slots // 64))):
            sums = lax.fori_loop(low, high, body, sums)
            pump((12,), n)
        for n in range(3):
            vectors[0, n:n + 1, :] = sums[n]
        vector_copy(0).start()
        pump((12,), 3)
        for action in tail:
            action()
        last_level = len(levels)
        for k in (1, 2, 3):
            vector_copy(last_level + k - 1).wait_recv()
        mine = vectors[last_level]
        vector_ref[...] = mine + vector_tp[0] + vector_tp[1] + vector_tp[2]
        for row_at in (UNIT_ROW, HEAD_ROW):
            value = mine[row_at:row_at + 1]
            for k in (1, 2, 3):
                value += vector_tp[k - 1, row_at + k:row_at + k + 1, :]
            vector_ref[row_at:row_at + 1, :] = value
        for n in range(last_level + 3):
            vector_copy(n).wait_send()
        down.step6(1)
        for item in (up, heads, proj):
            item.step6()


def back(grad_low, hidden, slope, down, up, normed2, middle, grad_out, inputs, normed1, packed, mixed, lse,
         heads, proj, column, row, flag, constants, sums):
    slots, width = normed2.shape
    units, columns, part = hidden.shape[2], heads.shape[2], mixed.shape[2]
    levels = lax.axis_size("dp").bit_length() - 1
    clip = lambda low, high: lambda at: jnp.minimum(jnp.maximum(at, low), high)
    in_down, in_up = clip(0, 3), lambda at: clip(4, 7)(at) - 4
    in_heads = lambda at: lax.rem(clip(8, 11)(at) - 7, 4)
    tokens, anywhere = once(slots, width), pl.BlockSpec(memory_space=pl.ANY)
    shapes = [(units, width), (width, units), (width, columns), (part, width)]
    got = []
    for n, (rows, cols) in enumerate(shapes):
        eighth = (rows // 4, cols // 2) if n == 3 else (rows // 8, cols)
        got += [pltpu.VMEM((4, rows // 2, cols), bf16), pltpu.VMEM((4, rows // 4, cols), bf16),
                pltpu.VMEM((4,) + eighth, bf16), pltpu.VMEM((3,) + eighth, bf16), pltpu.VMEM(eighth, bf16)]
    half = [pltpu.VMEM((4, rows // 2, cols), bf16) for rows, cols in shapes]
    return pl.pallas_call(
        back_kernel,
        grid=(13,),
        in_specs=[
            tokens, each(slots, units, at=in_down), each(slots, units, at=in_up), each(units, width, at=in_up),
            each(width, units, at=in_up), tokens, tokens, tokens, tokens, tokens,
            each(slots, columns, at=in_heads), each(slots, part, at=in_heads), each(8, slots, at=in_heads),
            each(width, columns, at=in_heads), each(part, width, at=in_heads), once(slots, 1), once(1, slots),
            once(slots, 1), once(*constants.shape), once(8, width),
        ],
        out_specs=[once(slots, width), once(VECTORS, width), anywhere, anywhere, anywhere, anywhere],
        out_shape=[jax.ShapeDtypeStruct((slots, width), f32), jax.ShapeDtypeStruct((VECTORS, width), f32)]
        + [jax.ShapeDtypeStruct(shape, bf16) for shape in shapes],
        scratch_shapes=[
            pltpu.VMEM((slots, units), bf16), pltpu.VMEM((slots, width), f32), pltpu.VMEM((width, slots), bf16),
            pltpu.VMEM((slots, part), bf16), pltpu.VMEM((slots, columns), bf16), pltpu.VMEM((8, slots), f32),
            pltpu.VMEM((3, slots, columns // 9), f32),
        ] + half + [half[0]] + half[2:] + [
            pltpu.VMEM((levels + 1, VECTORS, width), f32), pltpu.VMEM((levels, VECTORS, width), f32),
            pltpu.VMEM((3, VECTORS, width), f32), pltpu.SemaphoreType.DMA((levels + 3,)),
            pltpu.SemaphoreType.DMA((levels + 3,)), pltpu.SemaphoreType.DMA((4,)),
        ] + got + [pltpu.SemaphoreType.DMA((Reduce.COPIES,))] * 8,
        compiler_params=pltpu.CompilerParams(vmem_limit_bytes=65400 << 10, collective_id=1, has_side_effects=True),
        cost_estimate=cost(36e9, 60e6, 12 * 480000),
        name="back",
    )(grad_low, hidden, slope, down, up, normed2, middle, grad_out, inputs, normed1, packed, mixed, lse,
      heads, proj, column, row, flag, constants, sums)


def local(
    inputs,
    segment_ids,
    mask_flags,
    mask_token,
    norm_gain,
    norm_shift,
    heads_weight,
    heads_bias,
    proj_weight,
    proj_bias,
    attn_scale,
    mlp_gain,
    mlp_shift,
    up_weight,
    up_bias,
    down_weight,
    down_bias,
    mlp_scale,
    grad_out,
):
    width = inputs.shape[1]
    triple = heads_weight.shape[2]
    head_size = triple // 3
    heads_here = heads_weight.shape[1]
    own_heads = heads_weight.reshape(width, -1)
    heads_cols = own_heads.shape[1]
    vectors = (mask_token, norm_gain, norm_shift, proj_bias, attn_scale, mlp_gain, mlp_shift, down_bias, mlp_scale)
    (normed1, column, flag, row, packed, mixed, lse, middle, normed2, hidden, slope, output, grad_low2, sums_a,
     constants, heads_all, up_all, proj_all, down_all) = forward(
        inputs, segment_ids, mask_flags, vectors, heads_bias, up_bias, grad_out, own_heads, up_weight,
        proj_weight, down_weight,
    )
    grad_inputs, small, sum_down, sum_up, sum_heads, sum_proj = back(
        grad_low2, hidden, slope, down_all, up_all, normed2, middle, grad_out, inputs, normed1, packed, mixed,
        lse, heads_all, proj_all, column, row, flag, constants, sums_a,
    )
    sum_down, sum_up, sum_proj = (item.astype(f32) for item in (sum_down, sum_up, sum_proj))
    sum_heads = sum_heads.astype(f32).reshape(heads_weight.shape)
    bias_sums = small[HEAD_ROW, :heads_cols].reshape(heads_here, triple)
    sum_heads_bias = jnp.concatenate([bias_sums[:, :head_size], bias_sums[:, 2 * head_size:]], axis=1)
    sum_up_bias = small[UNIT_ROW, :up_bias.shape[0]]
    (sum_token, sum_gain1, sum_shift1, sum_proj_bias, sum_scale1, sum_gain2, sum_shift2,
     sum_down_bias, sum_scale2) = [small[i] for i in range(9)]
    return (
        output,
        grad_inputs,
        sum_token,
        sum_gain1,
        sum_shift1,
        sum_heads,
        sum_heads_bias,
        sum_proj,
        sum_proj_bias,
        sum_scale1,
        sum_gain2,
        sum_shift2,
        sum_up,
        sum_up_bias,
        sum_down,
        sum_down_bias,
        sum_scale2,
    )


def solution(mesh):
    placed = (
        P(("dp", "tp"), None),
        P("dp", None),
        P(("dp", "tp"), None),
        P(),
        P(),
        P(),
        P(None, "tp", None),
        P("tp", None),
        P("tp", None),
        P(),
        P(),
        P(),
        P(),
        P(None, "tp"),
        P("tp"),
        P("tp", None),
        P(),
        P(),
        P(("dp", "tp"), None),
    )
    return jax.shard_map(
        local,
        mesh=mesh,
        in_specs=placed,
        out_specs=(
            P(("dp", "tp"), None),
            P(("dp", "tp"), None),
            P(),
            P(),
            P(),
            P(None, "tp", None),
            P("tp", None),
            P("tp", None),
            P(),
            P(),
            P(),
            P(),
            P(None, "tp"),
            P("tp"),
            P("tp", None),
            P(),
            P(),
        ),
        check_vma=False,
    )
```

```python
import functools

import jax
import jax.numpy as jnp
from jax import lax
from jax.experimental import pallas as pl
from jax.experimental.pallas import tpu as pltpu
from jax.sharding import PartitionSpec as P

EPSILON = 1e-06
FLOOR_SCORE = -1e30
SQRT_HALF = 0.7071067811865476
INV_ROOT_TWO_PI = 0.3989422804014327
LONGEST = 14 * 14 + 1
FIFTH_FROM = 4 * (11 * 11 + 1)
TILE = 128
CORE, X, Y = 1, 2, 4

f32, bf16 = jnp.float32, jnp.bfloat16
NN = (((1,), (0,)), ((), ()))
NT = (((1,), (1,)), ((), ()))
TN = (((0,), (0,)), ((), ()))


def dot(a, b, dims=NN):
    return lax.dot_general(a, b, dims, preferred_element_type=f32)


def layer_norm(values, gain, shift):
    centre = values - jnp.mean(values, axis=-1, keepdims=True)
    inverse = lax.rsqrt(jnp.mean(centre * centre, axis=-1, keepdims=True) + EPSILON)
    scaled = centre * inverse
    return (scaled * gain + shift, scaled, inverse)


def norm_back(grad_normed, scaled, inverse, gain):
    grad_scaled = grad_normed * gain
    first = jnp.mean(grad_scaled, axis=-1, keepdims=True)
    second = jnp.mean(grad_scaled * scaled, axis=-1, keepdims=True)
    return inverse * (grad_scaled - first - scaled * second)


def gelu_parts(inner):
    normal_cdf = 0.5 * (1.0 + lax.erf(inner * SQRT_HALF))
    density = jnp.exp(-0.5 * inner * inner) * INV_ROOT_TWO_PI
    return (inner * normal_cdf, normal_cdf + inner * density)


def windows(slots):
    out = []
    for low in range(0, slots, TILE):
        high = min(low + TILE, slots)
        begin = low - LONGEST + 1
        if low >= FIFTH_FROM:
            begin = min(begin, FIFTH_FROM)
        end = high + LONGEST - 1
        if high > FIFTH_FROM:
            end = slots
        begin = max(begin, 0) // 128 * 128
        end = min((end + 127) // 128 * 128, slots)
        out.append((low, high, begin, end))
    return out


def as_row(column):
    rows = column.shape[0]
    shape = (rows, rows)
    here = lax.broadcasted_iota(jnp.int32, shape, 0) == lax.broadcasted_iota(jnp.int32, shape, 1)
    return jnp.sum(jnp.where(here, column, 0.0), axis=0, keepdims=True)


def whole(*shape):
    return pl.BlockSpec(shape, lambda k: (0,) * len(shape))


def each(*shape, at=lambda k: k):
    return pl.BlockSpec((1,) + shape, lambda k: (at(k),) + (0,) * len(shape))


def params(megabytes):
    return pltpu.CompilerParams(vmem_limit_bytes=megabytes << 20)


def cost(flops, moved, exps=0):
    return pl.CostEstimate(flops=int(flops), transcendentals=int(exps), bytes_accessed=int(moved))


def start_of(inputs_ref, column_ref, flag_ref, token, here):
    valid = (column_ref[here, :] >= 0).astype(f32)
    flagged = (flag_ref[here, :] == 1).astype(f32)
    start = valid * (flagged * token + (1.0 - flagged) * inputs_ref[here, :].astype(f32))
    return valid, flagged, start


def blocks(columns, step=256):
    return [slice(low, min(low + step, columns)) for low in range(0, columns, step)]


def rows_of(slots, step=104):
    return [(low, min(low + step, slots)) for low in range(0, slots, step)]


def flip(index, bits):
    bit = 1
    while bit <= bits:
        if bits & bit:
            index = index + bit * (1 - 2 * lax.rem(lax.div(index, bit), 2))
        bit *= 2
    return index


class Gather:
    ROUTES = ("z", "x", "y", "fx", "fy", "c0", "c2", "c4", "c6")
    COPIES = 3 * len(ROUTES)

    def __init__(self, full_ref, by_columns, send_sems, recv_sems):
        self.dp, self.tp = lax.axis_index("dp"), lax.axis_index("tp")
        self.own = lax.rem(self.dp, 8)
        self.full, self.by_columns = full_ref, by_columns
        self.sends, self.recvs = send_sems, recv_sems
        _, rows, columns = full_ref.shape
        self.rows, self.columns = (rows // 4, columns // 2) if by_columns else (rows // 8, columns)
        self.half = self.rows // 32 * 16

    def piece(self, k, bits, half=None):
        place, columns = flip(self.own, bits), slice(None)
        if self.by_columns:
            columns = pl.ds(pl.multiple_of(lax.rem(place, 2) * self.columns, 128), self.columns)
            place = lax.div(place, 2)
        begin, height = place * self.rows, self.rows
        if half == 0:
            height = self.half
        elif half == 1:
            begin, height = begin + self.half, self.rows - self.half
        return self.full.at[k, pl.ds(pl.multiple_of(begin, 16), height), columns]

    def copy(self, k, route):
        if route == "z":
            source, target, to = self.piece(0, 0), self.piece(k, 0), (self.dp, flip(self.tp, k))
        else:
            bits, half, link = {
                "x": (0, None, X), "y": (0, None, Y), "fx": (Y, 1, X), "fy": (X, 0, Y),
                "c0": (0, None, CORE), "c2": (X, None, CORE), "c4": (Y, None, CORE), "c6": (X | Y, None, CORE),
            }[route]
            source = target = self.piece(k, bits, half)
            to = (flip(self.dp, link), self.tp)
        n = (k - 1) * len(self.ROUTES) + self.ROUTES.index(route)
        return pltpu.make_async_remote_copy(
            src_ref=source, dst_ref=target, send_sem=self.sends.at[n], recv_sem=self.recvs.at[n],
            device_id=to, device_id_type=pl.DeviceIdType.MESH,
        )

    def start(self, k, *routes):
        for route in routes:
            self.copy(k, route).start()

    def arrived(self, k, *routes):
        for route in routes:
            self.copy(k, route).wait_recv()

    def begin(self, k):
        self.start(k, "z")

    def step1(self, k):
        self.arrived(k, "z")
        self.start(k, "x", "y", "c0")

    def step2(self, k):
        self.arrived(k, "x")
        self.start(k, "fy", "c2")
        self.arrived(k, "y")
        self.start(k, "fx", "c4")

    def step3(self, k):
        self.arrived(k, "fx", "fy")
        self.start(k, "c6")

    def step4(self, k):
        self.arrived(k, "c0", "c2", "c4", "c6")

    def sent(self):
        for k in (1, 2, 3):
            for route in self.ROUTES:
                self.copy(k, route).wait_send()


def meet(peers):
    barrier = pltpu.get_barrier_semaphore()
    for peer in peers:
        pl.semaphore_signal(barrier, inc=1, device_id=peer, device_id_type=pl.DeviceIdType.MESH)
    pl.semaphore_wait(barrier, len(peers))


def as_column(row):
    size = row.shape[1]
    shape = (size, size)
    here = lax.broadcasted_iota(jnp.int32, shape, 0) == lax.broadcasted_iota(jnp.int32, shape, 1)
    return jnp.sum(jnp.where(here, row, 0), axis=1, keepdims=True)


def dispatch(table, step, steps, unit):
    for at in steps:
        if table.get((at, unit)):

            @pl.when(step == at)
            def _():
                for action in table[(at, unit)]:
                    action()


TOKEN, GAIN1, SHIFT1, PROJ_BIAS, ATTN_SCALE, GAIN2, SHIFT2, DOWN_BIAS, MLP_SCALE = range(9)

HEADS, UP, PROJ, DOWN = range(4)
FORWARD_PLAN = {
    (0, 1): ((HEADS, (1, 2), 1),),
    (0, 6): ((HEADS, (3,), 1), (HEADS, (1,), 2),),
    (1, -1): ((PROJ, (1, 2, 3), 0), (UP, (1, 2, 3), 0), (HEADS, (2, 3), 2), (PROJ, (1,), 1), (HEADS, (1, 2), 3), (PROJ, (2, 3), 1), (HEADS, (3,), 3), (HEADS, (1,), 4),),
    (1, 1): ((HEADS, (2,), 4), (PROJ, (1, 2), 2), (UP, (1,), 1),),
    (1, 3): ((HEADS, (3,), 4), (PROJ, (3,), 2),),
    (1, 6): ((DOWN, (1, 2, 3), 0), (UP, (2,), 1), (PROJ, (1, 2), 3),),
    (2, 1): ((UP, (1,), 2), (PROJ, (3,), 3), (UP, (3,), 1), (PROJ, (1, 2), 4),),
    (2, 3): ((DOWN, (1,), 1),),
    (2, 6): ((UP, (2,), 2), (PROJ, (3,), 4), (UP, (1,), 3),),
    (3, 1): ((DOWN, (2,), 1), (UP, (3,), 2),),
    (3, 3): ((UP, (1,), 4),),
    (3, 6): ((DOWN, (1,), 2), (DOWN, (3,), 1), (UP, (2,), 3),),
    (4, 1): ((UP, (2,), 4), (UP, (3,), 3), (DOWN, (2,), 2),),
    (4, 3): ((DOWN, (1,), 3),),
    (5, -1): ((DOWN, (3,), 2), (UP, (3,), 4), (DOWN, (2,), 3), (DOWN, (1,), 4),),
    (5, 3): ((DOWN, (3,), 3), (DOWN, (2,), 4),),
    (6, 3): ((DOWN, (3,), 4),),
}


def forward_kernel(
    inputs_ref, segment_ref, mask_ref, heads_bias_ref, unit_bias_ref, grad_out_ref,
    heads_ref, up_ref, proj_ref, down_ref, *rest,
):
    vector_refs, rest = rest[:9], rest[9:]
    (normed1_ref, column_ref, flag_ref, row_ref, packed_ref, mixed_ref, lse_ref, middle_ref, normed2_ref, hidden_ref,
     slope_ref, output_ref, grad_low_ref, sums_ref, vectors_ref, heads_all, up_all, proj_all, down_all,
     heads_now, up_now, proj_now, down_now, head_bias, unit_bias, mixed_all, total,
     own_sems, store_sems, bias_sends, bias_recvs, *sems) = rest
    slots = inputs_ref.shape[0]
    triple = heads_now.shape[2] // 3
    size = triple // 3
    scale = size ** (-0.5)
    part = mixed_ref.shape[2]
    step = pl.program_id(0)
    vector = lambda n: vectors_ref[n:n + 1, :]
    shards, fulls = (heads_ref, up_ref, proj_ref, down_ref), (heads_all, up_all, proj_all, down_all)
    nows = (heads_now, up_now, proj_now, down_now)
    gathers = [Gather(nows[n], n == PROJ, sems[2 * n], sems[2 * n + 1]) for n in range(4)]
    dp, tp = gathers[0].dp, gathers[0].tp
    loads = [pltpu.make_async_copy(shards[n], nows[n].at[0], own_sems.at[n]) for n in range(4)]
    store = lambda n, k: pltpu.make_async_copy(nows[n].at[k], fulls[n].at[k], store_sems.at[n, k])

    def bias_copy(n, k):
        item = (head_bias, unit_bias)[n]
        return pltpu.make_async_remote_copy(
            src_ref=item.at[0], dst_ref=item.at[k], send_sem=bias_sends.at[n, k], recv_sem=bias_recvs.at[n, k],
            device_id=(dp, flip(tp, k)), device_id_type=pl.DeviceIdType.MESH,
        )

    table = {}
    for key, entries in FORWARD_PLAN.items():
        table[key] = []
        for n, ks, action in entries:
            item = gathers[n]
            for k in ks:
                table[key].append(functools.partial(
                    (item.begin, item.step1, item.step2, item.step3, item.step4)[action], k))
                if action == 4:
                    table[key].append(store(n, k).start)

    @pl.when(step == 0)
    def _():
        for load in loads:
            load.start()
        meet([(dp, flip(tp, k)) for k in (1, 2, 3)] + [(flip(dp, bit), tp) for bit in (X, Y, CORE)])
        loads[HEADS].wait()
        for k in (1, 2, 3):
            gathers[HEADS].begin(k)
        vectors_ref[...] = jnp.zeros_like(vectors_ref)
        for n, ref in enumerate(vector_refs):
            vectors_ref[n:n + 1, :] = ref[...].astype(f32).reshape(1, -1)
        blank = jnp.zeros((1, size), f32)
        pieces = []
        for head in range(3):
            here = heads_bias_ref[head:head + 1, :].astype(f32)
            pieces += [here[:, :size], blank, here[:, size:]]
        head_bias[0] = jnp.broadcast_to(jnp.concatenate(pieces, axis=1), head_bias.shape[1:])
        unit_bias[0] = jnp.broadcast_to(unit_bias_ref[...].astype(f32).reshape(1, -1), unit_bias.shape[1:])
        for n in range(2):
            for k in (1, 2, 3):
                bias_copy(n, k).start()
        row_ref[...] = segment_ref[pl.ds(tp, 1), :]
        for low in range(0, slots, 128):
            high = min(low + 128, slots)
            column_ref[low:high, :] = as_column(row_ref[:, low:high])
            flag_ref[low:high, :] = as_column(mask_ref[:, low:high])

        def body(i, carry):
            here = pl.ds(pl.multiple_of(i * 208, 16), 208)
            _, _, start = start_of(inputs_ref, column_ref, flag_ref, vector(TOKEN), here)
            normed1_ref[here, :] = layer_norm(start, vector(GAIN1), vector(SHIFT1))[0].astype(bf16)
            return carry

        lax.fori_loop(0, slots // 208, body, 0)
        for load in loads[1:]:
            load.wait()
        for n in range(4):
            store(n, 0).start()

    @pl.when(step == 1)
    def _():
        for k in (1, 2, 3):
            bias_copy(0, k).wait_recv()

    dispatch(table, step, range(1, 8), -1)

    @pl.when(step < 4)
    def _():
        for low in range(0, slots, 208):
            product = dot(normed1_ref[low:low + 208, :], heads_now[step])
            packed_ref[0, low:low + 208, :] = (product + head_bias[step, 0:1, :]).astype(bf16)
        lse_ref[...] = jnp.zeros_like(lse_ref)
        bases = [head * triple for head in range(3)]
        for unit, (low, high, begin, end) in enumerate(windows(slots)):
            same = column_ref[low:high, :] == row_ref[:, begin:end]
            scores = [
                dot(packed_ref[0, low:high, base:base + size] * jnp.bfloat16(scale),
                    packed_ref[0, begin:end, base + size:base + 2 * size], NT)
                for base in bases
            ]
            scores = [jnp.where(same, item, FLOOR_SCORE) for item in scores]
            largest = [jnp.max(item, axis=1, keepdims=True) for item in scores]
            raised = [jnp.exp(item - top) for item, top in zip(scores, largest)]
            totals = [jnp.sum(item, axis=1, keepdims=True) for item in raised]
            mixed = [
                dot(item.astype(bf16), packed_ref[0, begin:end, base + 2 * size:base + 3 * size])
                for item, base in zip(raised, bases)
            ]
            mixed = [(item * (1.0 / total)).astype(bf16) for item, total in zip(mixed, totals)]
            mixed_ref[0, low:high, :] = jnp.concatenate(mixed, axis=1)
            for head in range(3):
                lse_ref[0, head:head + 1, low:high] = as_row(largest[head] + jnp.log(totals[head]))
            dispatch(table, step, range(4), unit)

    for k in range(4):

        @pl.when(step == k)
        def _():
            mixed_all[:, k * part:(k + 1) * part] = mixed_ref[0]

    @pl.when(step == 4)
    def _():
        for k in (1, 2, 3):
            bias_copy(1, k).wait_recv()
        total[...] = jnp.zeros_like(total)
        proj = proj_now[...].reshape(-1, proj_now.shape[2])
        for low, high in rows_of(slots, 208):
            middle_ref[low:high, :] = dot(mixed_all[low:high, :], proj) + vector(PROJ_BIAS)

        def body(i, carry):
            here = pl.ds(pl.multiple_of(i * 208, 16), 208)
            _, _, start = start_of(inputs_ref, column_ref, flag_ref, vector(TOKEN), here)
            middle = start + vector(ATTN_SCALE) * middle_ref[here, :]
            middle_ref[here, :] = middle
            normed2_ref[here, :] = layer_norm(middle, vector(GAIN2), vector(SHIFT2))[0].astype(bf16)
            return carry

        lax.fori_loop(0, slots // 208, body, 0)

    @pl.when(step >= 4)
    def _():
        k = step - 4
        for unit, (low, high) in enumerate(rows_of(slots, 208)):
            for columns in blocks(hidden_ref.shape[2]):
                inner = dot(normed2_ref[low:high, :], up_now[k, :, columns]) + unit_bias[k, 0:1, columns]
                value, slope = gelu_parts(inner)
                hidden_ref[0, low:high, columns] = value.astype(bf16)
                slope_ref[0, low:high, columns] = slope.astype(bf16)
            total[low:high, :] += dot(hidden_ref[0, low:high, :], down_now[k])
            dispatch(table, step, range(4, 8), unit)

    @pl.when(step == 7)
    def _():
        def body(i, sums):
            here = pl.ds(pl.multiple_of(i * 208, 16), 208)
            valid = (column_ref[here, :] >= 0).astype(f32)
            branch2 = total[here, :] + vector(DOWN_BIAS)
            output_ref[here, :] = (valid * (middle_ref[here, :] + vector(MLP_SCALE) * branch2)).astype(bf16)
            grad_final = valid * grad_out_ref[here, :].astype(f32)
            grad_branch2 = vector(MLP_SCALE) * grad_final
            grad_low_ref[here, :] = grad_branch2.astype(bf16)
            return tuple(a + jnp.sum(b, axis=0, keepdims=True) for a, b in zip(sums, (branch2 * grad_final, grad_branch2)))

        zero = jnp.zeros((1, inputs_ref.shape[1]), f32)
        sums = lax.fori_loop(0, slots // 208, body, (zero, zero))
        sums_ref[...] = jnp.zeros_like(sums_ref)
        sums_ref[0:1, :], sums_ref[1:2, :] = sums
        for n, item in enumerate(gathers):
            item.sent()
            for k in range(4):
                store(n, k).wait()
        for n in range(2):
            for k in (1, 2, 3):
                bias_copy(n, k).wait_send()


def once(*shape):
    return pl.BlockSpec(shape, lambda at: (0,) * len(shape), pipeline_mode=pl.Buffered(1))


def forward(inputs, segments, mask, vectors, heads_bias, unit_bias, grad_out, heads, up, proj, down):
    slots, width = inputs.shape
    columns, units = heads.shape[1], up.shape[1]
    part = columns // 3
    anywhere = pl.BlockSpec(memory_space=pl.ANY)
    early = lambda at: jnp.minimum(at, 3)
    late = lambda at: jnp.maximum(at - 4, 0)
    tokens = once(slots, width)
    shape = jax.ShapeDtypeStruct
    return pl.pallas_call(
        forward_kernel,
        grid=(8,),
        in_specs=[
            tokens, once(*segments.shape), once(1, slots), once(*heads_bias.shape),
            once(*unit_bias.shape), tokens, anywhere, anywhere, anywhere, anywhere,
        ] + [once(width)] * len(vectors),
        out_specs=[
            tokens, once(slots, 1), once(slots, 1), once(1, slots), each(slots, columns, at=early),
            each(slots, part, at=early), each(8, slots, at=early), tokens, tokens, each(slots, units, at=late),
            each(slots, units, at=late), tokens, tokens, once(8, width), once(16, width), anywhere, anywhere, anywhere, anywhere,
        ],
        out_shape=[
            shape((slots, width), bf16), shape((slots, 1), jnp.int32), shape((slots, 1), jnp.int32),
            shape((1, slots), jnp.int32), shape((4, slots, columns), bf16), shape((4, slots, part), bf16),
            shape((4, 8, slots), f32), shape((slots, width), f32), shape((slots, width), bf16),
            shape((4, slots, units), bf16), shape((4, slots, units), bf16), shape((slots, width), bf16),
            shape((slots, width), bf16), shape((8, width), f32), shape((16, width), f32),
        ] + [shape((4,) + item.shape, bf16) for item in (heads, up, proj, down)],
        scratch_shapes=[
            pltpu.VMEM((4,) + heads.shape, bf16), pltpu.VMEM((4,) + up.shape, bf16), pltpu.VMEM((4,) + proj.shape, bf16),
            pltpu.VMEM((4,) + down.shape, bf16), pltpu.VMEM((4, 8, columns), f32), pltpu.VMEM((4, 8, units), f32),
            pltpu.VMEM((slots, width), bf16), pltpu.VMEM((slots, width), f32),
            pltpu.SemaphoreType.DMA((4,)), pltpu.SemaphoreType.DMA((4, 4)), pltpu.SemaphoreType.DMA((2, 4)), pltpu.SemaphoreType.DMA((2, 4)),
        ] + [pltpu.SemaphoreType.DMA((Gather.COPIES,))] * 8,
        compiler_params=pltpu.CompilerParams(vmem_limit_bytes=60 << 20, collective_id=0, has_side_effects=True),
        cost_estimate=cost(26e9, 60e6, 6e6),
        name="forward",
    )(inputs, segments, mask, heads_bias, unit_bias, grad_out, heads, up, proj, down, *vectors)


class Reduce:
    COPIES = 4 * 4 + 7

    def __init__(self, first, second, by_columns, keep, give, got, out, send_sems, recv_sems, own_sem):
        self.dp, self.tp = lax.axis_index("dp"), lax.axis_index("tp")
        self.first, self.second, self.by_columns = first, second, by_columns
        self.keep, self.give, self.out = keep, give, out
        self.got0, self.got1, self.got2, self.got_tp, self.total = got
        self.sends, self.recvs, self.own_sem = send_sems, recv_sems, own_sem
        self.rows, self.columns = keep.shape[1] * 2, keep.shape[2]
        self.bits = tuple(lax.rem(lax.div(self.dp, bit), 2) for bit in (CORE, first, second))

    def quarter(self, first):
        rows = self.rows // 4
        return pl.multiple_of(first * rows, 16), rows

    def eighth(self, first, second):
        begin, rows = self.quarter(first)
        if self.by_columns:
            width = self.columns // 2
            return begin, rows, pl.ds(pl.multiple_of(second * width, 128), width)
        return pl.multiple_of(begin + second * (rows // 2), 16), rows // 2, slice(None)

    def part(self, ref, spot):
        begin, rows, columns = spot
        return ref.at[pl.ds(begin, rows), columns]

    def place(self, flips):
        core, first, second = (1 - bit if turned else bit for bit, turned in zip(self.bits, flips))
        begin, rows, columns = self.eighth(first, second)
        return self.out.at[pl.ds(pl.multiple_of(core * (self.rows // 2) + begin, 16), rows), columns]

    def remote(self, n, source, target, bits=0, k=0):
        return pltpu.make_async_remote_copy(
            src_ref=source, dst_ref=target, send_sem=self.sends.at[n], recv_sem=self.recvs.at[n],
            device_id=(flip(self.dp, bits), flip(self.tp, k)), device_id_type=pl.DeviceIdType.MESH,
        )

    def copy(self, k, level):
        core, first, second = self.bits
        n = 4 * k + level
        if level == 0:
            return self.remote(n, self.give.at[k], self.got0.at[k], CORE)
        if level == 1:
            begin, rows = self.quarter(1 - first)
            return self.remote(n, self.keep.at[k, pl.ds(begin, rows), :], self.got1.at[k], self.first)
        if level == 2:
            return self.remote(n, self.part(self.keep.at[k], self.eighth(first, 1 - second)), self.got2.at[k], self.second)
        return self.remote(n, self.part(self.keep.at[k], self.eighth(first, second)), self.got_tp.at[k - 1], 0, k)

    def share(self, n):
        first, second = self.first, self.second
        bits, source = (
            (first, (0, 0, 0)), (second, (0, 0, 0)), (first | second, (0, 0, 0)), (CORE, (0, 0, 0)),
            (CORE, (0, 1, 0)), (CORE, (0, 0, 1)), (CORE, (0, 1, 1)),
        )[n]
        place = self.place(source)
        return self.remote(16 + n, self.total if n < 4 else place, place, bits)

    def add(self, target, begin, rows, columns, *items):
        step = 48

        def body(i, carry):
            here = pl.ds(pl.multiple_of(begin + i * step, 16), step)
            there = pl.ds(pl.multiple_of(i * step, 16), step)
            if len(items) == 1:
                target[here, columns] = target[here, columns] + items[0][there, :]
            else:
                total = target[here, columns].astype(f32)
                for item in items:
                    total += item[there, :].astype(f32)
                target[here, columns] = total.astype(bf16)
            return carry

        lax.fori_loop(0, rows // step, body, 0)

    def step0(self, k):
        self.copy(k, 0).start()

    def given(self, k):
        self.copy(k, 0).wait_send()

    def step1(self, k):
        self.copy(k, 0).wait_recv()
        self.add(self.keep.at[k], 0, self.rows // 2, slice(None), self.got0.at[k])
        self.copy(k, 1).start()

    def step2(self, k):
        self.copy(k, 1).wait_recv()
        begin, rows = self.quarter(self.bits[1])
        self.add(self.keep.at[k], begin, rows, slice(None), self.got1.at[k])
        self.copy(k, 2).start()

    def step3(self, k):
        self.copy(k, 2).wait_recv()
        self.add(self.keep.at[k], *self.eighth(*self.bits[1:]), self.got2.at[k])
        if k:
            self.copy(k, 3).start()

    def step4(self):
        for k in (1, 2, 3):
            self.copy(k, 3).wait_recv()
        begin, rows, columns = self.eighth(*self.bits[1:])
        self.add(self.keep.at[0], begin, rows, columns, *[self.got_tp.at[k] for k in range(3)])
        self.total[...] = self.keep[0, pl.ds(begin, rows), columns]
        for n in range(4):
            self.share(n).start()
        self.own_copy().start()

    def own_copy(self):
        return pltpu.make_async_copy(self.total, self.place((0, 0, 0)), self.own_sem)

    def step5(self):
        for n in range(3):
            self.share(n).wait_recv()
            self.share(4 + n).start()

    def step6(self, lowest=0):
        for n in range(3, 7):
            self.share(n).wait_recv()
        for n in range(7):
            self.share(n).wait_send()
        for k in range(4):
            for level in range(lowest, 4 if k else 3):
                self.copy(k, level).wait_send()
        self.own_copy().wait()


VECTORS = 24
UNIT_ROW, HEAD_ROW = 9, 13


VECTOR = 4
BACK_PLAN = {
    (3, 0): ((DOWN, 0, 1),),
    (4, 1): ((DOWN, 1, 1), (DOWN, 2, 1),),
    (4, 3): ((DOWN, 3, 1),),
    (5, 3): ((DOWN, 0, 2), (UP, 0, 1),),
    (6, 1): ((DOWN, 1, 2),),
    (6, 3): ((UP, 1, 1), (DOWN, 0, 3),),
    (7, 1): ((DOWN, 2, 2),),
    (7, 3): ((UP, 2, 1), (UP, 0, 2),),
    (8, 1): ((DOWN, 1, 3), (DOWN, 3, 2), (UP, 3, 1), (UP, 0, 3), (UP, 1, 2),),
    (8, 3): ((DOWN, 2, 3), (PROJ, 1, 1),),
    (8, 7): ((UP, 2, 2), (UP, 1, 3),),
    (9, 1): ((DOWN, 3, 3), (HEADS, 1, 1),),
    (9, 3): ((PROJ, 2, 1), (UP, 2, 3),),
    (9, 6): ((UP, 3, 2), (PROJ, 1, 2),),
    (9, 7): ((PROJ, 2, 2),),
    (10, 1): ((HEADS, 1, 2), (DOWN, 0, 4), (HEADS, 2, 1), (UP, 3, 3),),
    (10, 3): ((PROJ, 1, 3), (PROJ, 3, 1), (PROJ, 2, 3),),
    (10, 6): ((HEADS, 1, 3),),
    (11, 1): ((UP, 0, 4), (HEADS, 3, 1), (DOWN, 0, 5),),
    (11, 3): ((PROJ, 3, 2), (PROJ, 0, 1), (HEADS, 2, 2),),
    (12, 1): ((UP, 0, 5), (PROJ, 0, 2),),
    (12, 2): ((HEADS, 0, 1),),
}
BACK_TAIL = (
    (HEADS, 2, 3),
    (HEADS, 3, 2),
    (PROJ, 3, 3),
    (PROJ, 0, 3),
    (VECTOR, 0, 0),
    (HEADS, 3, 3),
    (HEADS, 0, 2),
    (VECTOR, 1, 0),
    (PROJ, 0, 4),
    (HEADS, 0, 3),
    (HEADS, 0, 4),
    (VECTOR, 2, 0),
    (PROJ, 0, 5),
    (HEADS, 0, 5),
)


def back_kernel(
    grad_low_ref, hidden_ref, slope_ref, down_ref, up_ref, normed2_ref, middle_ref, grad_out_ref,
    inputs_ref, normed1_ref, packed_ref, mixed_ref, lse_ref, heads_ref, proj_ref, column_ref, row_ref, flag_ref,
    constants_ref, sums_ref,
    grad_inputs_ref, vector_ref, out_down, out_up, out_heads, out_proj,
    grad_unit, total, flipped, grad_mixed, grad_packed, delta, grad_query,
    keep_down, keep_up, keep_heads, keep_proj, give_down, give_heads, give_proj,
    vectors, vector_got, vector_tp, vector_sends, vector_recvs, own_sems,
    *rest,
):
    slots, width = normed2_ref.shape
    triple = heads_ref.shape[2] // 3
    size = triple // 3
    scale = size ** (-0.5)
    step = pl.program_id(0)
    got, sems = [rest[5 * n:5 * n + 5] for n in range(4)], rest[20:]
    give_up = give_down
    constant = lambda n: constants_ref[n:n + 1, :]
    make = lambda n, first, second, by_columns, keep, give, out: Reduce(
        first, second, by_columns, keep, give, got[n], out, sems[2 * n], sems[2 * n + 1], own_sems.at[n])
    down = make(0, X, Y, False, keep_down, give_down, out_down)
    up = make(1, Y, X, False, keep_up, give_up, out_up)
    heads = make(2, X, Y, False, keep_heads, give_heads, out_heads)
    proj = make(3, Y, X, True, keep_proj, give_proj, out_proj)
    dp, tp, core = down.dp, down.tp, down.bits[0]
    n_dp = lax.axis_size("dp")
    levels = [bit for bit in (1, 2, 4, 8, 16, 32, 64, 128) if bit < n_dp]

    def vector_copy(n):
        if n < len(levels):
            return heads_like(vectors.at[n], vector_got.at[n], n, levels[n], 0)
        k = n - len(levels) + 1
        return heads_like(vectors.at[len(levels)], vector_tp.at[k - 1], n, 0, k)

    def heads_like(source, target, n, bits, k):
        return pltpu.make_async_remote_copy(
            src_ref=source, dst_ref=target, send_sem=vector_sends.at[n], recv_sem=vector_recvs.at[n],
            device_id=(flip(dp, bits), flip(tp, k)), device_id_type=pl.DeviceIdType.MESH,
        )

    def vector_step(n):
        vector_copy(n).wait_recv()
        vectors[n + 1] = vectors[n] + vector_got[n]
        if n + 1 < len(levels):
            vector_copy(n + 1).start()
        else:
            for k in (1, 2, 3):
                vector_copy(len(levels) + k - 1).start()

    def action_of(entry):
        item, k, part = entry
        if item == VECTOR:
            return functools.partial(vector_step, k)
        item = {HEADS: heads, UP: up, PROJ: proj, DOWN: down}[item]
        if part > 3:
            return (item.step4, item.step5)[part - 4]
        return functools.partial((item.step1, item.step2, item.step3)[part - 1], k)

    table = {key: [action_of(entry) for entry in entries] for key, entries in BACK_PLAN.items()}
    tail = [action_of(entry) for entry in BACK_TAIL]
    tail += [functools.partial(vector_step, n) for n in range(3, len(levels))]

    def pump(steps, unit):
        for at in steps:
            if (at, unit) in table:

                @pl.when(step == at)
                def _():
                    for action in table[(at, unit)]:
                        action()

    def each_send(item, place, steps):
        for k, at in steps:

            @pl.when(step == at)
            def _():
                item.step0(k)

    halves_of = (pl.ds(pl.multiple_of(core * (width // 2), 128), width // 2),
                 pl.ds(pl.multiple_of((1 - core) * (width // 2), 128), width // 2))

    @pl.when(step == 0)
    def _():
        vectors[0] = jnp.zeros_like(vectors[0])
        vectors[0, 7:8, :] = sums_ref[1:2, :]
        vectors[0, 8:9, :] = sums_ref[0:1, :]
        peers = [(dp, flip(tp, k)) for k in (1, 2, 3)]
        peers += [(flip(dp, bits), tp) for bits in (X, Y, X | Y, CORE)]
        peers += [(flip(dp, bit), tp) for bit in levels if bit >= 8]
        meet(peers)

    @pl.when(step < 4)
    def _():
        keep_down[step] = dot(hidden_ref[0, :, halves_of[0]], grad_low_ref[...], TN).astype(bf16)
        give_down[step] = dot(hidden_ref[0, :, halves_of[1]], grad_low_ref[...], TN).astype(bf16)
        each_send(down, 0, [(k, k) for k in range(4)])
        pump(range(4), 0)

    @pl.when(step == 4)
    def _():
        total[...] = jnp.zeros_like(total)
        flipped[...] = normed2_ref[...].T

    @pl.when(jnp.logical_and(step >= 4, step < 8))
    def _():
        unit_sum = jnp.zeros((1, slope_ref.shape[2]), f32)
        for n, (low, high) in enumerate(rows_of(slots, 208)):
            unit = dot(grad_low_ref[low:high, :], down_ref[0], NT) * slope_ref[0, low:high, :].astype(f32)
            unit = unit.astype(bf16)
            grad_unit[low:high, :] = unit
            unit_sum += jnp.sum(unit.astype(f32), axis=0, keepdims=True)
            total[low:high, :] += dot(unit, up_ref[0], NT)
            pump(range(4, 8), n)
        k = step - 4
        for at in range(4):

            @pl.when(k == at)
            def _():
                vectors[0, UNIT_ROW + at:UNIT_ROW + at + 1, :] = unit_sum
        keep_up[k] = dot(flipped[halves_of[0], :], grad_unit[...]).astype(bf16)
        for at in range(4):

            @pl.when(k == at)
            def _():
                down.given(at)
        give_up[k] = dot(flipped[halves_of[1], :], grad_unit[...]).astype(bf16)
        each_send(up, 0, [(k, 4 + k) for k in range(4)])
        pump(range(4, 8), 4)

    @pl.when(step == 7)
    def _():
        gain, attn_scale = constant(GAIN2), constant(ATTN_SCALE)

        def body(i, sums):
            here = pl.ds(pl.multiple_of(i * 64, 64), 64)
            valid, _, start = start_of(inputs_ref, column_ref, flag_ref, constant(TOKEN), here)
            grad_final = valid * grad_out_ref[here, :].astype(f32)
            grad_normed = total[here, :]
            _, scaled, inverse = layer_norm(middle_ref[here, :], gain, gain)
            grad_middle = grad_final + norm_back(grad_normed, scaled, inverse, gain)
            grad_branch1 = attn_scale * grad_middle
            grad_inputs_ref[here, :] = grad_middle
            grad_unit[here, :] = grad_branch1.astype(bf16)
            new = (grad_branch1, (middle_ref[here, :] - start) / attn_scale * grad_middle, grad_normed * scaled, grad_normed)
            return tuple(a + jnp.sum(b, axis=0, keepdims=True) for a, b in zip(sums, new))

        zero = jnp.zeros((1, width), f32)
        sums = lax.fori_loop(0, slots // 64, body, (zero,) * 4)
        for n in range(4):
            vectors[0, 3 + n:4 + n, :] = sums[n]
        total[...] = jnp.zeros_like(total)
        flipped[...] = normed1_ref[...].T

    attending = range(8, 12)
    shard_of = {8: 1, 9: 2, 10: 3, 11: 0}

    @pl.when(jnp.logical_and(step >= 8, step < 12))
    def _():
        k = lax.rem(step - 7, 4)
        grad_low1 = grad_unit
        for low in range(0, slots, 208):
            grad_mixed[low:low + 208, :] = dot(grad_low1[low:low + 208, :], proj_ref[0], NT).astype(bf16)
        value = dot(mixed_ref[0], grad_low1[...], TN).astype(bf16)
        rows = value.shape[0] // 2
        for own in (0, 1):

            @pl.when(core == own)
            def _():
                keep_proj[k] = value[own * rows:(own + 1) * rows]
                give_proj[k] = value[(1 - own) * rows:(2 - own) * rows]
        each_send(proj, 0, [(shard_of[at], at) for at in attending])
        tiles = windows(slots)
        bases = [head * triple for head in range(3)]
        owns = [slice(head * size, (head + 1) * size) for head in range(3)]
        for low, high, _, _ in tiles:
            for head, own in enumerate(owns):
                product = grad_mixed[low:high, own].astype(f32) * mixed_ref[0, low:high, own].astype(f32)
                delta[head:head + 1, low:high] = as_row(jnp.sum(product, axis=1, keepdims=True))
        grad_query[...] = jnp.zeros_like(grad_query)
        for unit, (low, high, begin, end) in enumerate(tiles):
            same = column_ref[low:high, :] == row_ref[:, begin:end]
            keys = [packed_ref[0, low:high, base + size:base + 2 * size] for base in bases]
            queries = [packed_ref[0, begin:end, base:base + size] * jnp.bfloat16(scale) for base in bases]
            grads = [grad_mixed[begin:end, own] for own in owns]
            scores = [dot(key, query, NT) for key, query in zip(keys, queries)]
            grad_shares = [
                dot(packed_ref[0, low:high, base + 2 * size:base + 3 * size], grad, NT)
                for base, grad in zip(bases, grads)
            ]
            shares = [
                jnp.exp(jnp.where(same, item - lse_ref[0, head:head + 1, begin:end], FLOOR_SCORE))
                for head, item in enumerate(scores)
            ]
            grad_scores = [
                (share * (item - delta[head:head + 1, begin:end])).astype(bf16)
                for head, (share, item) in enumerate(zip(shares, grad_shares))
            ]
            for head, base in enumerate(bases):
                grad_packed[low:high, base + size:base + 3 * size] = jnp.concatenate([
                    dot(grad_scores[head], queries[head]).astype(bf16),
                    dot(shares[head].astype(bf16), grads[head]).astype(bf16),
                ], axis=1)
                grad_query[head, begin:end, :] += dot(grad_scores[head], keys[head], TN)
            pump(attending, unit)
        for head, base in enumerate(bases):
            grad_packed[:, base:base + size] = (grad_query[head] * scale).astype(bf16)
        keep_heads[k] = dot(flipped[halves_of[0], :], grad_packed[...]).astype(bf16)
        give_heads[k] = dot(flipped[halves_of[1], :], grad_packed[...]).astype(bf16)
        each_send(heads, 0, [(shard_of[at], at) for at in attending])
        sums = jnp.sum(grad_packed[...].astype(f32), axis=0, keepdims=True)
        for at in range(4):

            @pl.when(k == at)
            def _():
                vectors[0, HEAD_ROW + at:HEAD_ROW + at + 1, :sums.shape[1]] = sums
        for low in range(0, slots, 208):
            total[low:low + 208, :] += dot(grad_packed[low:low + 208, :], heads_ref[0], NT)
        pump(attending, 7)

    @pl.when(step == 12)
    def _():
        gain = constant(GAIN1)

        def body(i, sums):
            here = pl.ds(pl.multiple_of(i * 64, 64), 64)
            valid, flagged, start = start_of(inputs_ref, column_ref, flag_ref, constant(TOKEN), here)
            _, scaled, inverse = layer_norm(start, gain, gain)
            grad_normed = total[here, :]
            grad_start = grad_inputs_ref[here, :] + norm_back(grad_normed, scaled, inverse, gain)
            grad_inputs_ref[here, :] = valid * (1.0 - flagged) * grad_start
            new = (valid * flagged * grad_start, grad_normed * scaled, grad_normed)
            return tuple(a + jnp.sum(b, axis=0, keepdims=True) for a, b in zip(sums, new))

        zero = jnp.zeros((1, width), f32)
        sums = (zero,) * 3
        for n, (low, high) in enumerate(((0, 4), (4, 8), (8, slots // 64))):
            sums = lax.fori_loop(low, high, body, sums)
            pump((12,), n)
        for n in range(3):
            vectors[0, n:n + 1, :] = sums[n]
        vector_copy(0).start()
        pump((12,), 3)
        for action in tail:
            action()
        last_level = len(levels)
        for k in (1, 2, 3):
            vector_copy(last_level + k - 1).wait_recv()
        mine = vectors[last_level]
        vector_ref[...] = mine + vector_tp[0] + vector_tp[1] + vector_tp[2]
        for row_at in (UNIT_ROW, HEAD_ROW):
            value = mine[row_at:row_at + 1]
            for k in (1, 2, 3):
                value += vector_tp[k - 1, row_at + k:row_at + k + 1, :]
            vector_ref[row_at:row_at + 1, :] = value
        for n in range(last_level + 3):
            vector_copy(n).wait_send()
        down.step6(1)
        for item in (up, heads, proj):
            item.step6()


def back(grad_low, hidden, slope, down, up, normed2, middle, grad_out, inputs, normed1, packed, mixed, lse,
         heads, proj, column, row, flag, constants, sums):
    slots, width = normed2.shape
    units, columns, part = hidden.shape[2], heads.shape[2], mixed.shape[2]
    levels = lax.axis_size("dp").bit_length() - 1
    clip = lambda low, high: lambda at: jnp.minimum(jnp.maximum(at, low), high)
    in_down, in_up = clip(0, 3), lambda at: clip(4, 7)(at) - 4
    in_heads = lambda at: lax.rem(clip(8, 11)(at) - 7, 4)
    tokens, anywhere = once(slots, width), pl.BlockSpec(memory_space=pl.ANY)
    shapes = [(units, width), (width, units), (width, columns), (part, width)]
    got = []
    for n, (rows, cols) in enumerate(shapes):
        eighth = (rows // 4, cols // 2) if n == 3 else (rows // 8, cols)
        got += [pltpu.VMEM((4, rows // 2, cols), bf16), pltpu.VMEM((4, rows // 4, cols), bf16),
                pltpu.VMEM((4,) + eighth, bf16), pltpu.VMEM((3,) + eighth, bf16), pltpu.VMEM(eighth, bf16)]
    half = [pltpu.VMEM((4, rows // 2, cols), bf16) for rows, cols in shapes]
    return pl.pallas_call(
        back_kernel,
        grid=(13,),
        in_specs=[
            tokens, each(slots, units, at=in_down), each(slots, units, at=in_up), each(units, width, at=in_up),
            each(width, units, at=in_up), tokens, tokens, tokens, tokens, tokens,
            each(slots, columns, at=in_heads), each(slots, part, at=in_heads), each(8, slots, at=in_heads),
            each(width, columns, at=in_heads), each(part, width, at=in_heads), once(slots, 1), once(1, slots),
            once(slots, 1), once(*constants.shape), once(8, width),
        ],
        out_specs=[once(slots, width), once(VECTORS, width), anywhere, anywhere, anywhere, anywhere],
        out_shape=[jax.ShapeDtypeStruct((slots, width), f32), jax.ShapeDtypeStruct((VECTORS, width), f32)]
        + [jax.ShapeDtypeStruct(shape, bf16) for shape in shapes],
        scratch_shapes=[
            pltpu.VMEM((slots, units), bf16), pltpu.VMEM((slots, width), f32), pltpu.VMEM((width, slots), bf16),
            pltpu.VMEM((slots, part), bf16), pltpu.VMEM((slots, columns), bf16), pltpu.VMEM((8, slots), f32),
            pltpu.VMEM((3, slots, columns // 9), f32),
        ] + half + [half[0]] + half[2:] + [
            pltpu.VMEM((levels + 1, VECTORS, width), f32), pltpu.VMEM((levels, VECTORS, width), f32),
            pltpu.VMEM((3, VECTORS, width), f32), pltpu.SemaphoreType.DMA((levels + 3,)),
            pltpu.SemaphoreType.DMA((levels + 3,)), pltpu.SemaphoreType.DMA((4,)),
        ] + got + [pltpu.SemaphoreType.DMA((Reduce.COPIES,))] * 8,
        compiler_params=pltpu.CompilerParams(vmem_limit_bytes=65400 << 10, collective_id=1, has_side_effects=True),
        cost_estimate=cost(36e9, 60e6, 12 * 480000),
        name="back",
    )(grad_low, hidden, slope, down, up, normed2, middle, grad_out, inputs, normed1, packed, mixed, lse,
      heads, proj, column, row, flag, constants, sums)


def local(
    inputs,
    segment_ids,
    mask_flags,
    mask_token,
    norm_gain,
    norm_shift,
    heads_weight,
    heads_bias,
    proj_weight,
    proj_bias,
    attn_scale,
    mlp_gain,
    mlp_shift,
    up_weight,
    up_bias,
    down_weight,
    down_bias,
    mlp_scale,
    grad_out,
):
    width = inputs.shape[1]
    triple = heads_weight.shape[2]
    head_size = triple // 3
    heads_here = heads_weight.shape[1]
    own_heads = heads_weight.reshape(width, -1)
    heads_cols = own_heads.shape[1]
    vectors = (mask_token, norm_gain, norm_shift, proj_bias, attn_scale, mlp_gain, mlp_shift, down_bias, mlp_scale)
    (normed1, column, flag, row, packed, mixed, lse, middle, normed2, hidden, slope, output, grad_low2, sums_a,
     constants, heads_all, up_all, proj_all, down_all) = forward(
        inputs, segment_ids, mask_flags, vectors, heads_bias, up_bias, grad_out, own_heads, up_weight,
        proj_weight, down_weight,
    )
    grad_inputs, small, sum_down, sum_up, sum_heads, sum_proj = back(
        grad_low2, hidden, slope, down_all, up_all, normed2, middle, grad_out, inputs, normed1, packed, mixed,
        lse, heads_all, proj_all, column, row, flag, constants, sums_a,
    )
    sum_down, sum_up, sum_proj = (item.astype(f32) for item in (sum_down, sum_up, sum_proj))
    sum_heads = sum_heads.astype(f32).reshape(heads_weight.shape)
    bias_sums = small[HEAD_ROW, :heads_cols].reshape(heads_here, triple)
    sum_heads_bias = jnp.concatenate([bias_sums[:, :head_size], bias_sums[:, 2 * head_size:]], axis=1)
    sum_up_bias = small[UNIT_ROW, :up_bias.shape[0]]
    (sum_token, sum_gain1, sum_shift1, sum_proj_bias, sum_scale1, sum_gain2, sum_shift2,
     sum_down_bias, sum_scale2) = [small[i] for i in range(9)]
    return (
        output,
        grad_inputs,
        sum_token,
        sum_gain1,
        sum_shift1,
        sum_heads,
        sum_heads_bias,
        sum_proj,
        sum_proj_bias,
        sum_scale1,
        sum_gain2,
        sum_shift2,
        sum_up,
        sum_up_bias,
        sum_down,
        sum_down_bias,
        sum_scale2,
    )


def solution(mesh):
    placed = (
        P(("dp", "tp"), None),
        P("dp", None),
        P(("dp", "tp"), None),
        P(),
        P(),
        P(),
        P(None, "tp", None),
        P("tp", None),
        P("tp", None),
        P(),
        P(),
        P(),
        P(),
        P(None, "tp"),
        P("tp"),
        P("tp", None),
        P(),
        P(),
        P(("dp", "tp"), None),
    )
    return jax.shard_map(
        local,
        mesh=mesh,
        in_specs=placed,
        out_specs=(
            P(("dp", "tp"), None),
            P(("dp", "tp"), None),
            P(),
            P(),
            P(),
            P(None, "tp", None),
            P("tp", None),
            P("tp", None),
            P(),
            P(),
            P(),
            P(),
            P(None, "tp"),
            P("tp"),
            P("tp", None),
            P(),
            P(),
        ),
        check_vma=False,
    )
```
